32 devices in a mesh: segment: 2 (over x), skyx: 4 (over z), skyy: 4 (over y, core).
Axes of the slice: x: 2, y: 2, z: 4, core: 2. Of those that a mesh axis runs over, the one named last changes fastest.
Arguments:
- frames: float32 [2, 2048, 2048], P('segment', 'skyx', 'skyy'), may hold values from -6 to 6
- row_shift: int32 [16], P('skyx'), may hold values from -126 to 125, as said below
- row_frac: float32 [2048], P('skyx'), may hold values from 0 to 1
- col_shift: int32 [16], P('skyy'), may hold values from -126 to 125, as said below
- col_frac: float32 [2048], P('skyy'), may hold values from 0 to 1
- profile_cols: bfloat16 [4, 31], replicated, may hold values from -1 to 1
- profile_rows: bfloat16 [8, 31], replicated, may hold values from -1 to 1
- coef_table: float32 [16, 32], replicated, may hold values from -1 to 1
- weight_ids: int32 [16, 16], P('skyx', 'skyy'), may hold values from 0 to 15
Outputs:
- images: float32 [2, 2048, 2048], P('segment', 'skyx', 'skyy')
The draws below stay inside these ranges and needn't reach their ends.
Inputs may be any that keep to these rules, and one draw needn't show every extreme that they name: `row_shift`: in the first block of every sky tile the shift is at most -64, in the last block of every sky tile at least 64. Both ends of the range occur in every draw. `col_shift`: in the first block of every sky tile the shift is at most -64, in the last block of every sky tile at least 64. Both ends of the range occur in every draw.
All inputs are finite; a program needn't handle non-finite values.
Results may differ from the reference program's by a relative error of at most 0.0033.
Values may be sent and summed in bfloat16 or wider, within the bound.
No kernel may reach another device: no remote copies, remote signals or barrier semaphores. Data moves between devices by JAX's collectives and lax.ppermute only.
A program may use at most 192 MiB of HBM per device.

```python
import jax
import jax.numpy as jnp
from jax import lax

TS = 512
BLK = 128
MARGIN = 128
KW = 31
NU = 4
NV = 8
NSET = 16
HALF = 15
NBASIS = 32
NX = 2048
NY = 2048


def shift_draw(key, blocks):
    lowest = 2 - MARGIN
    highest = MARGIN - 3
    per_tile = TS // BLK
    tiles = blocks // per_tile
    values = jax.random.randint(jax.random.fold_in(key, 11), (blocks,), lowest, highest + 1)
    first_vals = jax.random.randint(jax.random.fold_in(key, 14), (blocks,), lowest, -(MARGIN // 2) + 1)
    last_vals = jax.random.randint(jax.random.fold_in(key, 15), (blocks,), MARGIN // 2, highest + 1)
    position = jnp.arange(blocks, dtype=jnp.int32) % per_tile
    values = jnp.where(position == 0, first_vals, values)
    values = jnp.where(position == per_tile - 1, last_vals, values)
    low_tile = jax.random.randint(jax.random.fold_in(key, 12), (), 0, tiles)
    high_tile = jax.random.randint(jax.random.fold_in(key, 13), (), 0, tiles)
    values = values.at[low_tile * per_tile].set(lowest)
    values = values.at[high_tile * per_tile + per_tile - 1].set(highest)
    return values.astype(jnp.int32)


def draw_row_shift(key, part):
    return shift_draw(jax.random.fold_in(key, 1), NX // BLK)


def draw_col_shift(key, part):
    return shift_draw(jax.random.fold_in(key, 2), NY // BLK)


def set_ends(result, key, low, high):
    place = [jax.random.randint(jax.random.fold_in(key, axis), (), 0, length) for axis, length in enumerate(result.shape)]
    longest = result.shape.index(max(result.shape))
    neighbour = place[:longest] + [(place[longest] + 1) % result.shape[longest]] + place[longest + 1:]
    return result.at[tuple(place)].set(low).at[tuple(neighbour)].set(high)


def shard_levels(key, dims, pieces, low, top_value):
    loudness, own = 1.0, jax.random.fold_in(key, 6)
    for dim, parts in pieces:
        draws = jnp.exp(jax.random.uniform(jax.random.fold_in(own, dim), (parts,), jnp.float32, low / len(pieces), top_value / len(pieces)))
        loudness = loudness * jnp.repeat(draws, dims[dim] // parts).reshape([-1 if axis == dim else 1 for axis in range(len(dims))])
    return loudness


def normal_values(key, shape, scale, reach, pieces=(), kind=jnp.bfloat16):
    level = shard_levels(key, shape, pieces, -0.22, 0.18) if pieces else 1.0
    drawn = jax.random.normal(key, shape, jnp.float32) * scale * level
    return jnp.minimum(jnp.maximum(drawn, -reach), reach).astype(kind)


def setup_inputs(seed: int = 0) -> dict:
    key_list = jax.random.split(jax.random.key(seed), 10)
    frames = normal_values(key_list[0], (2, NX, NY), 1.0, 6.0, ((0, 2), (1, 4), (2, 4)), jnp.float32)
    row_shift = draw_row_shift(jax.random.fold_in(key_list[9], 71), 0)
    row_frac = jnp.clip(1.0 * jax.random.uniform(key_list[2], (NX,), jnp.float32) ** shard_levels(key_list[2], (NX,), ((0, 4),), -0.2, 0.2), 0.0, 1.0)
    col_shift = draw_col_shift(jax.random.fold_in(key_list[9], 71), 0)
    col_frac = jnp.clip(1.0 * jax.random.uniform(key_list[4], (NY,), jnp.float32) ** shard_levels(key_list[4], (NY,), ((0, 4),), -0.2, 0.2), 0.0, 1.0)
    profile_cols = normal_values(key_list[5], (NU, KW), KW ** -0.5, 1.0)
    profile_rows = normal_values(key_list[6], (NV, KW), KW ** -0.5, 1.0)
    coef_table = normal_values(key_list[7], (NSET, NBASIS), NBASIS ** -0.5, 1.0, (), jnp.float32)
    weight_ids = set_ends(jax.random.randint(key_list[8], (NX // BLK, NY // BLK), 0, NSET), jax.random.fold_in(key_list[8], 1), 0, NSET - 1).astype(jnp.int32)
    return {"frames": frames, "row_shift": row_shift, "row_frac": row_frac, "col_shift": col_shift, "col_frac": col_frac, "profile_cols": profile_cols, "profile_rows": profile_rows, "coef_table": coef_table, "weight_ids": weight_ids}


def lanczos(values):
    return jnp.where(jnp.abs(values) < 3.0, jnp.sinc(values) * jnp.sinc(values / 3.0), 0.0)


def band_weights(shifts, fractions):
    blocks = shifts.shape[0]
    offsets = jnp.arange(BLK)[:, None]
    columns = jnp.arange(BLK + 5)[None, :]
    lag_rows = (columns - 2 - offsets).astype(fractions.dtype)
    return lanczos(lag_rows[None] - fractions.reshape(blocks, BLK)[:, :, None])


def reference(frames, row_shift, row_frac, col_shift, col_frac, profile_cols, profile_rows, coef_table, weight_ids):
    template = frames[0]
    science = frames[1]
    padded = jnp.pad(template, MARGIN)
    row_band = band_weights(row_shift, row_frac)
    row_start = (MARGIN + BLK * jnp.arange(NX // BLK) + row_shift - 2).astype(jnp.int32)

    def warp_rows(block_item):
        weights, start_row = block_item
        source_slab = lax.dynamic_slice_in_dim(padded, start_row, BLK + 5, 0)
        return jnp.dot(weights, source_slab, precision=lax.Precision.HIGHEST)

    rows_warped = lax.map(warp_rows, (row_band, row_start)).reshape(NX, NY + 2 * MARGIN)
    col_band = band_weights(col_shift, col_frac)
    col_start = (MARGIN + BLK * jnp.arange(NY // BLK) + col_shift - 2).astype(jnp.int32)

    def warp_cols(block_item):
        weights, start_col = block_item
        source_slab = lax.dynamic_slice_in_dim(rows_warped, start_col, BLK + 5, 1)
        return jnp.dot(source_slab, weights.T, precision=lax.Precision.HIGHEST)

    warped = lax.map(warp_cols, (col_band, col_start))
    warped = jnp.transpose(warped, (1, 0, 2)).reshape(NX, NY).astype(jnp.bfloat16)

    padded_grid = jnp.pad(warped.astype(jnp.float32), HALF)[None, None]
    col_kernel = profile_cols.astype(jnp.float32)[:, None, None, :]
    rowpass = lax.conv_general_dilated(padded_grid, col_kernel, (1, 1), "VALID", precision=lax.Precision.HIGHEST)[0]
    rounded = lax.optimization_barrier(rowpass.astype(jnp.bfloat16))
    rowpass = rounded.astype(jnp.float32)
    row_kernel = profile_rows.astype(jnp.float32)[:, None, :, None]
    coef_map = coef_table[weight_ids]
    total_sum = jnp.zeros((NX, NY), jnp.float32)
    for prof_col in range(NU):
        source = rowpass[prof_col][None, None]
        for prof_row in range(NV):
            basis_image = lax.conv_general_dilated(source, row_kernel[prof_row:prof_row + 1], (1, 1), "VALID", precision=lax.Precision.HIGHEST)[0, 0]
            factor_map = jnp.repeat(jnp.repeat(coef_map[:, :, prof_col * NV + prof_row], BLK, axis=0), BLK, axis=1)
            total_sum = total_sum + factor_map * basis_image
    difference = science - total_sum
    return jnp.stack([warped.astype(jnp.float32), difference])
```

```python
import functools
import math

import jax
import jax.numpy as jnp
from jax import lax
from jax.experimental import pallas as pl
from jax.experimental.pallas import tpu as pltpu
from jax.sharding import PartitionSpec as P

BLK = 128
KW = 31
HALF = 15
ROW0 = 48
F32 = jnp.float32
BF16 = jnp.bfloat16
HIGHEST = lax.Precision.HIGHEST
VM = pl.BlockSpec(memory_space=pltpu.VMEM)
HBM = pl.BlockSpec(memory_space=pl.ANY)
SM = pl.BlockSpec(memory_space=pltpu.SMEM)


def moved(block, step, sources):
    axes = ("segment", "skyx", "skyy")
    counts = [lax.axis_size(axis) for axis in axes]
    route = []
    for s in range(counts[0]):
        for i in range(counts[1]):
            for j in range(counts[2]):
                to = (s + step[0], i + step[1], j + step[2])
                if s in sources and all(0 <= to[k] < counts[k] for k in range(3)):
                    flat = [(a * counts[1] + b) * counts[2] + c for a, b, c in ((s, i, j), to)]
                    route.append(tuple(flat))
    return lax.ppermute(block, axes, route)


def sinc(values):
    angle = math.pi * values
    zero = values == 0.0
    return jnp.where(zero, 1.0, jnp.sin(angle) / jnp.where(zero, 1.0, angle))


def taps(frac):
    lag = lax.broadcasted_iota(jnp.int32, (8, BLK), 0) - 2
    values = lag.astype(F32) - frac
    weight = jnp.where(jnp.abs(values) < 3.0, sinc(values) * sinc(values / 3.0), 0.0)
    return jnp.where(lag <= 3, weight, 0.0)


def split(values):
    high = values.astype(BF16)
    return high, (values - high.astype(F32)).astype(BF16)


def banded(weight, shift, depth, offset):
    lag = (
        lax.broadcasted_iota(jnp.int32, (depth, BLK), 0)
        - lax.broadcasted_iota(jnp.int32, (depth, BLK), 1)
        + offset
        - shift.astype(jnp.int32)
    )
    total = jnp.zeros((depth, BLK), F32)
    for tap in range(6):
        total = jnp.where(lag == tap - 2, weight[tap : tap + 1], total)
    return total


def dot3(left, right, dims):
    lh, ll = left
    rh, rl = right
    dot = functools.partial(
        lax.dot_general, dimension_numbers=(dims, ((), ())), preferred_element_type=F32
    )
    return dot(lh, rh) + dot(lh, rl) + dot(ll, rh)


def prepare_kernel(
    nb, nu, nv, nx, ny,
    frame, left, right, meta, meta_up, meta_down, prof_cols, prof_rows, table, ids,
    own, across, to_up, to_down, side_up, side_down, kernels_out, band_out,
    src_hi, src_lo, row_hi, row_lo, kernels, band, coefs, sem,
):
    side = nb * BLK
    warper = lax.axis_index("segment") == 0
    i = lax.axis_index("skyx")
    j = lax.axis_index("skyy")

    @pl.when(warper)
    def _():
        for part, lane in ((left, 0), (frame, BLK), (right, BLK + side)):
            width = part.shape[1]
            hi, lo = split(part[0:side, :])
            src_hi[:, lane : lane + width] = hi
            src_lo[:, lane : lane + width] = lo
        lanes = lax.broadcasted_iota(jnp.int32, (1, BLK), 1)
        for b in range(nb):
            first = 0 if b == 0 else b
            count = 2 if b in (0, nb - 1) else 3
            if b == nb - 1:
                first = nb
            depth = count * BLK
            weight = taps(meta[2 * nb + b : 2 * nb + b + 1, :])
            shift = meta[3 * nb + b : 3 * nb + b + 1, :]
            mat = split(banded(weight, shift, depth, (first - 1 - b) * BLK))
            cols = slice(first * BLK, first * BLK + depth)
            hi, lo = split(dot3((src_hi[:, cols], src_lo[:, cols]), mat, ((1,), (0,))))
            row_hi[:, b * BLK : (b + 1) * BLK] = hi
            row_lo[:, b * BLK : (b + 1) * BLK] = lo
        low_ok = jnp.logical_and(lanes >= BLK - HALF, j > 0)
        high_ok = jnp.logical_and(lanes < HALF, j < ny - 1)
        low = split(jnp.where(low_ok, banded(taps(left[side : side + 1, :]), left[side + 1 : side + 2, :], BLK, BLK), 0.0))
        high = split(jnp.where(high_ok, banded(taps(right[side : side + 1, :]), right[side + 1 : side + 2, :], BLK, -BLK), 0.0))
        hi, lo = split(
            dot3((src_hi[:, BLK : 2 * BLK], src_lo[:, BLK : 2 * BLK]), low, ((1,), (0,)))
            + dot3((src_hi[:, side : side + BLK], src_lo[:, side : side + BLK]), high, ((1,), (0,)))
        )
        row_hi[:, side : side + BLK] = hi
        row_lo[:, side : side + BLK] = lo
        for b in range(-1, nb + 1):
            if b == -1:
                first, count = 0, 1
                weight = jnp.where(i > 0, taps(meta_up[0:1, :]), 0.0)
                shift = meta_up[1:2, :]
            elif b == nb:
                first, count = nb - 1, 1
                weight = jnp.where(i < nx - 1, taps(meta_down[0:1, :]), 0.0)
                shift = meta_down[1:2, :]
            else:
                first, count = (b, 1) if b in (0, nb - 1) else (b - 1, 3)
                weight = taps(meta[b : b + 1, :])
                shift = meta[nb + b : nb + b + 1, :]
            depth = count * BLK
            mat = split(banded(weight, shift, depth, (first - b) * BLK))
            rows = slice(first * BLK, first * BLK + depth)
            got = dot3(mat, (row_hi[rows, :], row_lo[rows, :]), ((0,), (0,))).astype(BF16)
            kept = side - 2 * ROW0
            if b == -1:
                to_up[...] = got[:, :side]
                side_up[...] = got
                across[kept + 16 : kept + 32, :] = got[BLK - 16 :, :]
            elif b == nb:
                to_down[...] = got[:, :side]
                side_down[...] = got
                across[kept : kept + 16, :] = got[:16, :]
            else:
                own[b * BLK : (b + 1) * BLK, :] = got[:, :side]
                low_row = max(b * BLK, ROW0)
                high_row = min((b + 1) * BLK, side - ROW0)
                across[low_row - ROW0 : high_row - ROW0, :] = got[low_row - b * BLK : high_row - b * BLK, :]

    @pl.when(jnp.logical_not(warper))
    def _():
        for bi in range(nb):
            for bj in range(nb):
                cell = bi * nb + bj
                coefs[cell : cell + 1, :] = table[pl.ds(ids[bi, bj], 1), :]
        width = nu * 160
        padded = prof_rows[...]
        spread = jnp.concatenate(
            [pltpu.roll(padded, p * 160 + 1, 1) for p in range(nu)], axis=0
        )
        base = jnp.dot(coefs[...], spread, precision=HIGHEST, preferred_element_type=F32)
        for cell in range(nb * nb):
            row = jnp.broadcast_to(base[cell : cell + 1, :], (BLK, width))
            kernels[cell] = pltpu.roll(row, 0, 1, stride=1, stride_axis=0).astype(BF16)
        for p in range(nu):
            row = jnp.broadcast_to(prof_cols[p : p + 1, :], (BLK, 3 * BLK))
            band[p * BLK : (p + 1) * BLK, :] = pltpu.roll(
                row, BLK - HALF, 1, stride=1, stride_axis=0
            ).astype(BF16)
        first = pltpu.make_async_copy(kernels, kernels_out, sem.at[0])
        second = pltpu.make_async_copy(band, band_out, sem.at[1])
        first.start()
        second.start()
        first.wait()
        second.wait()


def finish_kernel(
    nb, nu,
    frame, own, got_up, got_down, across, side_up, side_down, kernels_in, band_in,
    out, full, passed, kernels, band, sem,
):
    side = nb * BLK
    warper = lax.axis_index("segment") == 0
    last = side - BLK

    @pl.when(warper)
    def _():
        out[...] = own[...].astype(F32)
        for start, got in ((0, got_up), (last, got_down)):
            total = own[start : start + BLK, :].astype(F32) + got[...].astype(F32)
            out[start : start + BLK, :] = total.astype(BF16).astype(F32)

    @pl.when(jnp.logical_not(warper))
    def _():
        first = pltpu.make_async_copy(band_in, band, sem.at[0])
        second = pltpu.make_async_copy(kernels_in, kernels, sem.at[1])
        first.start()
        second.start()
        kept = side - 2 * ROW0

        def put(start, rows):
            stop = start + rows.shape[0]
            full[start:stop, BLK : BLK + side] = rows[:, :side]
            full[start:stop, :BLK] = rows[:, side:]
            full[start:stop, BLK + side :] = rows[:, side:]

        def added(one, two):
            return (one.astype(F32) + two.astype(F32)).astype(BF16)

        put(0, across[kept + 16 : kept + 32, :])
        put(16 + side, across[kept : kept + 16, :])
        put(16, side_up[:ROW0, :])
        both = BLK - ROW0
        put(16 + ROW0, added(across[:both, :], side_up[ROW0:, :]))
        put(16 + BLK, across[both : kept - both, :])
        put(16 + last, added(across[kept - both : kept, :], side_down[:both, :]))
        put(16 + side - ROW0, side_down[both:, :])
        first.wait()
        for bj in range(nb):
            got = lax.dot_general(
                full[:, bj * BLK : (bj + 3) * BLK], band[...], (((1,), (1,)), ((), ())),
                preferred_element_type=F32,
            ).astype(BF16)
            for p in range(nu):
                passed[p, :, bj * BLK : (bj + 1) * BLK] = got[:, p * BLK : (p + 1) * BLK]
        second.wait()
        for bi in range(nb):
            for bj in range(nb):
                cols = slice(bj * BLK, (bj + 1) * BLK)
                window = jnp.concatenate(
                    [passed[p, bi * BLK : bi * BLK + 160, cols] for p in range(nu)], axis=0
                )
                total = jnp.dot(kernels[bi * nb + bj], window, preferred_element_type=F32)
                rows = slice(bi * BLK, (bi + 1) * BLK)
                out[rows, cols] = frame[rows, cols] - total


def local(
    frames, row_shift, row_frac, col_shift, col_frac,
    profile_cols, profile_rows, coef_table, weight_ids,
):
    frame = frames[0]
    side = frame.shape[0]
    nb = side // BLK
    nu, nv = profile_cols.shape[0], profile_rows.shape[0]
    nx, ny = lax.axis_size("skyx"), lax.axis_size("skyy")
    spread_shift = lambda shift: jnp.broadcast_to(shift[:, None].astype(F32), (nb, BLK))
    row_meta = jnp.concatenate([row_frac.reshape(nb, BLK), spread_shift(row_shift)])
    col_meta = jnp.concatenate([col_frac.reshape(nb, BLK), spread_shift(col_shift)])
    meta = jnp.concatenate([row_meta, col_meta])
    fill = jnp.zeros((6, BLK), F32)

    def edge(array, b):
        return jnp.concatenate([array, col_meta[b : b + 1], col_meta[nb + b : nb + b + 1], fill])

    def row_edge(b):
        return jnp.concatenate([row_meta[b : b + 1], row_meta[nb + b : nb + b + 1], fill])

    left = moved(edge(frame[:, side - BLK :], nb - 1), (0, 0, 1), (0,))
    right = moved(edge(frame[:, :BLK], 0), (0, 0, -1), (0,))
    meta_up = moved(row_edge(nb - 1), (0, 1, 0), (0,))
    meta_down = moved(row_edge(0), (0, -1, 0), (0,))
    width = nu * 160
    prof_rows = jnp.pad(profile_rows.astype(F32), ((0, 0), (0, width - KW)))
    prof_cols = jnp.pad(profile_cols.astype(F32), ((0, 0), (0, 3 * BLK - KW)))
    wide = side + BLK
    kept = side - 2 * ROW0 + 32
    cells = nb * nb
    shape = jax.ShapeDtypeStruct
    own, across, to_up, to_down, side_up, side_down, kernels, band = pl.pallas_call(
        functools.partial(prepare_kernel, nb, nu, nv, nx, ny),
        out_shape=(
            shape((side, side), BF16), shape((kept, wide), BF16),
            shape((BLK, side), BF16), shape((BLK, side), BF16),
            shape((BLK, wide), BF16), shape((BLK, wide), BF16),
            shape((cells, BLK, width), BF16), shape((nu * BLK, 3 * BLK), BF16),
        ),
        in_specs=[VM] * 9 + [SM],
        out_specs=(VM,) * 6 + (HBM,) * 2,
        scratch_shapes=[
            pltpu.VMEM((side, side + 2 * BLK), BF16), pltpu.VMEM((side, side + 2 * BLK), BF16),
            pltpu.VMEM((side, wide), BF16), pltpu.VMEM((side, wide), BF16),
            pltpu.VMEM((cells, BLK, width), BF16), pltpu.VMEM((nu * BLK, 3 * BLK), BF16),
            pltpu.VMEM((cells, nu * nv), F32), pltpu.SemaphoreType.DMA((2,)),
        ],
        compiler_params=pltpu.CompilerParams(vmem_limit_bytes=48 << 20),
        name="prepare",
    )(frame, left, right, meta, meta_up, meta_down, prof_cols, prof_rows, coef_table, weight_ids)
    across = moved(across, (1, 0, 0), (0,))
    side_down_got = moved(side_up, (1, -1, 0), (0,))
    side_up_got = moved(side_down, (1, 1, 0), (0,))
    got_down = moved(to_up, (0, -1, 0), (0,))
    got_up = moved(to_down, (0, 1, 0), (0,))
    result = pl.pallas_call(
        functools.partial(finish_kernel, nb, nu),
        out_shape=shape((side, side), F32),
        in_specs=[VM] * 7 + [HBM] * 2,
        out_specs=VM,
        scratch_shapes=[
            pltpu.VMEM((side + 32, side + 2 * BLK), BF16), pltpu.VMEM((nu, side + 32, side), BF16),
            pltpu.VMEM((cells, BLK, width), BF16), pltpu.VMEM((nu * BLK, 3 * BLK), BF16),
            pltpu.SemaphoreType.DMA((2,)),
        ],
        compiler_params=pltpu.CompilerParams(vmem_limit_bytes=48 << 20),
        name="finish",
    )(frame, own, got_up, got_down, across, side_up_got, side_down_got, kernels, band)
    return result[None]


def solution(mesh):
    placed = (
        P("segment", "skyx", "skyy"), P("skyx"), P("skyx"), P("skyy"), P("skyy"),
        P(), P(), P(), P("skyx", "skyy"),
    )
    return jax.shard_map(
        local, mesh=mesh, in_specs=placed, out_specs=P("segment", "skyx", "skyy"), check_vma=False
    )
```

```python
import functools
import math

import jax
import jax.numpy as jnp
from jax import lax
from jax.experimental import pallas as pl
from jax.experimental.pallas import tpu as pltpu
from jax.sharding import PartitionSpec as P

BLK = 128
KW = 31
HALF = 15
ROW0 = 48
F32 = jnp.float32
BF16 = jnp.bfloat16
HIGHEST = lax.Precision.HIGHEST
VM = pl.BlockSpec(memory_space=pltpu.VMEM)
SM = pl.BlockSpec(memory_space=pltpu.SMEM)


def moved(block, step, sources):
    axes = ("segment", "skyx", "skyy")
    counts = [lax.axis_size(axis) for axis in axes]
    route = []
    for s in range(counts[0]):
        for i in range(counts[1]):
            for j in range(counts[2]):
                to = (s + step[0], i + step[1], j + step[2])
                if s in sources and all(0 <= to[k] < counts[k] for k in range(3)):
                    flat = [(a * counts[1] + b) * counts[2] + c for a, b, c in ((s, i, j), to)]
                    route.append(tuple(flat))
    return lax.ppermute(block, axes, route)


def sinc(values):
    angle = math.pi * values
    zero = values == 0.0
    return jnp.where(zero, 1.0, jnp.sin(angle) / jnp.where(zero, 1.0, angle))


def taps(fracs):
    count = len(fracs)
    spread = jnp.concatenate([jnp.broadcast_to(frac, (8, BLK)) for frac in fracs], axis=0)
    lag = (lax.broadcasted_iota(jnp.int32, (8 * count, BLK), 0) & 7) - 2
    values = lag.astype(F32) - spread
    weight = jnp.where(jnp.abs(values) < 3.0, sinc(values) * sinc(values / 3.0), 0.0)
    return [weight[8 * n : 8 * n + 8] for n in range(count)]


def split(values):
    high = values.astype(BF16)
    return high, (values - high.astype(F32)).astype(BF16)


def banded(weight, shift, depth, offset):
    lag = (
        lax.broadcasted_iota(jnp.int32, (depth, BLK), 0)
        - lax.broadcasted_iota(jnp.int32, (depth, BLK), 1)
        + (offset - shift)
    )
    total = jnp.zeros((depth, BLK), F32)
    for tap in range(6):
        total = jnp.where(lag == tap - 2, weight[tap : tap + 1], total)
    return total


def dot3(left, right, dims):
    lh, ll = left
    rh, rl = right
    dot = functools.partial(
        lax.dot_general, dimension_numbers=(dims, ((), ())), preferred_element_type=F32
    )
    return dot(lh, rh) + dot(lh, rl) + dot(ll, rh)


MATMUL = ((1,), (0,))
LEFT_T = ((0,), (0,))


def row_depth(b, nb):
    return BLK if b in (0, nb - 1) else 3 * BLK


def row_start(b, nb):
    return sum(row_depth(a, nb) for a in range(b))


def row_source(b, nb):
    first = b if b in (0, nb - 1) else b - 1
    return slice(first * BLK, first * BLK + row_depth(b, nb))


def pack_kernel(nb, frame, row_frac, col_frac, row_shift, col_shift, to_right, to_left, to_up, to_down):
    side = nb * BLK

    @pl.when(lax.axis_index("segment") == 0)
    def _():
        for out, lane, b in ((to_right, side - BLK, nb - 1), (to_left, 0, 0)):
            out[:side, :] = frame[:, lane : lane + BLK]
            out[side : side + 1, :] = col_frac[b : b + 1, :]
            out[side + 1 : side + 2, :] = jnp.full((1, BLK), col_shift[b].astype(F32))
        for out, b in ((to_up, 0), (to_down, nb - 1)):
            out[0:1, :] = row_frac[b : b + 1, :]
            out[1:2, :] = jnp.full((1, BLK), row_shift[b].astype(F32))


def center_kernel(
    nb, nu, nv,
    frame, row_frac, col_frac, row_shift, col_shift, prof_cols, prof_rows, table, ids,
    own, across, src_hi, src_lo, mid_hi, mid_lo, row_hi, row_lo, edge_hi, edge_lo, kernels, band,
    coefs, padded,
):
    side = nb * BLK
    warper = lax.axis_index("segment") == 0

    @pl.when(warper)
    def _():
        weights = taps([col_frac[b : b + 1, :] for b in range(nb)] + [row_frac[b : b + 1, :] for b in range(nb)])
        hi, lo = split(frame[...])
        src_hi[...] = hi
        src_lo[...] = lo
        for b in range(1, nb - 1):
            mat = split(banded(weights[b], col_shift[b], 3 * BLK, -BLK))
            cols = slice((b - 1) * BLK, (b + 2) * BLK)
            hi, lo = split(dot3((src_hi[:, cols], src_lo[:, cols]), mat, MATMUL))
            mid_hi[:, (b - 1) * BLK : b * BLK] = hi
            mid_lo[:, (b - 1) * BLK : b * BLK] = lo
        for b in range(nb):
            offset = 0 if b in (0, nb - 1) else -BLK
            depth = row_depth(b, nb)
            hi, lo = split(banded(weights[nb + b], row_shift[b], depth, offset))
            kept = slice(row_start(b, nb), row_start(b, nb) + depth)
            row_hi[kept, :] = hi
            row_lo[kept, :] = lo
            rows = row_source(b, nb)
            got = dot3((hi, lo), (mid_hi[rows, :], mid_lo[rows, :]), LEFT_T).astype(BF16)
            own[b * BLK : (b + 1) * BLK, :] = got
            low = max(b * BLK, ROW0)
            high = min((b + 1) * BLK, side - ROW0)
            across[low - ROW0 : high - ROW0, :] = got[low - b * BLK : high - b * BLK, :]
        for n, (b, offset) in enumerate(((0, -BLK), (nb - 1, 0))):
            hi, lo = split(banded(weights[b], col_shift[b], 2 * BLK, offset))
            edge_hi[n * 2 * BLK : (n + 1) * 2 * BLK, :] = hi
            edge_lo[n * 2 * BLK : (n + 1) * 2 * BLK, :] = lo

    @pl.when(jnp.logical_not(warper))
    def _():
        for bi in range(nb):
            for bj in range(nb):
                cell = bi * nb + bj
                coefs[cell : cell + 1, :] = table[pl.ds(ids[bi, bj], 1), :]
        width = nu * 160
        padded[...] = jnp.zeros_like(padded)
        padded[0:nv, 0:KW] = prof_rows[...].astype(F32)
        profile = padded[0:nv, :]
        spread = jnp.concatenate(
            [pltpu.roll(profile, p * 160 + 1, 1) for p in range(nu)], axis=0
        )
        base = jnp.dot(coefs[...], spread, precision=HIGHEST, preferred_element_type=F32)
        for cell in range(nb * nb):
            row = jnp.broadcast_to(base[cell : cell + 1, :], (BLK, width))
            kernels[cell] = pltpu.roll(row, 0, 1, stride=1, stride_axis=0).astype(BF16)
        padded[...] = jnp.zeros_like(padded)
        padded[0:nu, 0:KW] = prof_cols[...].astype(F32)
        for p in range(nu):
            row = jnp.broadcast_to(padded[p : p + 1, : 3 * BLK], (BLK, 3 * BLK))
            band[p * BLK : (p + 1) * BLK, :] = pltpu.roll(
                row, BLK - HALF, 1, stride=1, stride_axis=0
            ).astype(BF16)


def edge_kernel(
    nb, nx, ny,
    left, right, meta_up, meta_down, src_hi, src_lo, mid_hi, mid_lo, row_hi, row_lo, edge_hi, edge_lo,
    own, across, side_up, side_down,
    end_hi, end_lo,
):
    side = nb * BLK
    kept = side - 2 * ROW0
    half = side // 2
    i = lax.axis_index("skyx")
    j = lax.axis_index("skyy")

    @pl.when(lax.axis_index("segment") == 0)
    def _():
        lanes = lax.broadcasted_iota(jnp.int32, (8, BLK), 1)
        weights = taps([left[side : side + 1, :], right[side : side + 1, :], meta_up[0:1, :], meta_down[0:1, :]])
        shifts = [
            part[row : row + 1, :].astype(jnp.int32)
            for part, row in ((left, side + 1), (right, side + 1), (meta_up, 1), (meta_down, 1))
        ]
        parts = [split(left[:side, :]), split(right[:side, :])]
        for n, col in ((0, 0), (1, side - BLK)):
            source = []
            for part, src in zip(parts[n], (src_hi, src_lo)):
                inner = src[:, col : col + BLK]
                source.append(jnp.concatenate([part, inner] if n == 0 else [inner, part], axis=1))
            mat = tuple(edge[n * 2 * BLK : (n + 1) * 2 * BLK, :] for edge in (edge_hi, edge_lo))
            hi, lo = split(dot3(source, mat, MATMUL))
            end_hi[:, n * BLK : (n + 1) * BLK] = hi
            end_lo[:, n * BLK : (n + 1) * BLK] = lo
        low_ok = jnp.logical_and(lanes >= BLK - HALF, j > 0)
        high_ok = jnp.logical_and(lanes < HALF, j < ny - 1)
        low = split(banded(jnp.where(low_ok, weights[0], 0.0), shifts[0], BLK, BLK))
        high = split(banded(jnp.where(high_ok, weights[1], 0.0), shifts[1], BLK, -BLK))
        mat = [jnp.concatenate(pair, axis=0) for pair in zip(low, high)]
        source = [
            jnp.concatenate([src[:, :BLK], src[:, side - BLK :]], axis=1) for src in (src_hi, src_lo)
        ]
        hi, lo = split(dot3(source, mat, MATMUL))
        end_hi[:, 2 * BLK :] = hi
        end_lo[:, 2 * BLK :] = lo
        outer = []
        for n, b in ((0, 0), (1, nb - 1)):
            there = (i > 0) if n == 0 else (i < nx - 1)
            mat = split(banded(jnp.where(there, weights[2 + n], 0.0), shifts[2 + n], BLK, BLK if n == 0 else -BLK))
            rows = slice(b * BLK, (b + 1) * BLK)
            end = dot3(mat, (end_hi[rows, : 2 * BLK], end_lo[rows, : 2 * BLK]), LEFT_T).astype(BF16)
            mid = dot3(mat, (mid_hi[rows, :], mid_lo[rows, :]), LEFT_T).astype(BF16)
            turned = dot3((end_hi[rows, 2 * BLK :], end_lo[rows, 2 * BLK :]), mat, LEFT_T)
            out = side_up if n == 0 else side_down
            out[:BLK, :BLK] = end[:, :BLK]
            out[:BLK, BLK : side - BLK] = mid
            out[:BLK, side - BLK :] = end[:, BLK:]
            out[BLK:, :BLK] = turned[:16].astype(BF16)
            out[BLK:, BLK : 2 * BLK] = turned[BLK - 16 :].astype(BF16)
            outer.append(turned)
        across[kept : kept + 16, :] = side_down[:16, :half]
        across[kept + 16 : kept + 32, :] = side_up[BLK - 16 : BLK, :half]
        across[kept + 32 : kept + 48, :] = side_down[:16, half:]
        across[kept + 48 : kept + 64, :] = side_up[BLK - 16 : BLK, half:]
        columns = lax.broadcasted_iota(jnp.int32, (BLK, BLK), 1)
        for b in range(nb):
            hi, lo = (mat[row_start(b, nb) : row_start(b, nb) + row_depth(b, nb), :] for mat in (row_hi, row_lo))
            rows = row_source(b, nb)
            got = dot3((hi, lo), (end_hi[rows, : 2 * BLK], end_lo[rows, : 2 * BLK]), LEFT_T).astype(BF16)
            own[b * BLK : (b + 1) * BLK, :] = got
            low = max(b * BLK, ROW0)
            high = min((b + 1) * BLK, side - ROW0)
            across[low - ROW0 : high - ROW0, :] = got[low - b * BLK : high - b * BLK, :]
            turned = dot3((end_hi[rows, 2 * BLK :], end_lo[rows, 2 * BLK :]), (hi, lo), LEFT_T)
            if b == 0:
                turned = jnp.where(columns < ROW0, pltpu.roll(outer[0], ROW0, 1), turned)
            if b == nb - 1:
                turned = jnp.where(columns >= BLK - ROW0, pltpu.roll(outer[1], BLK - ROW0, 1), turned)
            half_at, lane = divmod(b * BLK, half)
            base = kept + 64 + 32 * half_at
            across[base : base + 16, lane : lane + BLK] = turned[:16].astype(BF16)
            across[base + 16 : base + 32, lane : lane + BLK] = turned[BLK - 16 :].astype(BF16)


def finish_kernel(
    nb, nu,
    frame, own_mid, own_end, side_up, side_down, mid, end, kernels, band, got_up, got_down,
    out, full, passed,
):
    side = nb * BLK
    half = side // 2
    warper = lax.axis_index("segment") == 0
    last = side - BLK

    @pl.when(warper)
    def _():
        for b in range(nb):
            rows = slice(b * BLK, (b + 1) * BLK)
            pieces = ((0, own_end[rows, :BLK]), (BLK, own_mid[rows, :]), (last, own_end[rows, BLK:]))
            for lane, piece in pieces:
                cols = slice(lane, lane + piece.shape[1])
                total = piece.astype(F32)
                if b == 0:
                    total = (total + got_up[:BLK, cols].astype(F32)).astype(BF16).astype(F32)
                if b == nb - 1:
                    total = (total + got_down[:BLK, cols].astype(F32)).astype(BF16).astype(F32)
                out[rows, cols] = total

    @pl.when(jnp.logical_not(warper))
    def _():
        kept = side - 2 * ROW0
        both = BLK - ROW0
        stop = 16 + side

        def added(one, two):
            return (one.astype(F32) + two.astype(F32)).astype(BF16)

        def fill(at, width, own, above, below):
            cols = slice(at, at + width)
            full[16 : 16 + ROW0, cols] = above[:ROW0]
            full[16 + ROW0 : 16 + BLK, cols] = added(own[:both], above[ROW0:])
            full[16 + BLK : 16 + last, cols] = own[both : kept - both]
            full[16 + last : stop - ROW0, cols] = added(own[kept - both :], below[:both])
            full[stop - ROW0 : stop, cols] = below[both:]

        fill(2 * BLK, side - 2 * BLK, mid[:kept, :], side_up[:BLK, BLK:last], side_down[:BLK, BLK:last])
        fill(BLK, BLK, end[:kept, :BLK], side_up[:BLK, :BLK], side_down[:BLK, :BLK])
        fill(side, BLK, end[:kept, BLK:], side_up[:BLK, last:], side_down[:BLK, last:])
        full[:16, BLK : BLK + half] = end[kept + 16 : kept + 32, :]
        full[:16, BLK + half : BLK + side] = end[kept + 48 : kept + 64, :]
        full[stop:, BLK : BLK + half] = end[kept : kept + 16, :]
        full[stop:, BLK + half : BLK + side] = end[kept + 32 : kept + 48, :]
        k = lax.broadcasted_iota(jnp.int32, (32, BLK), 0)
        lanes = lax.broadcasted_iota(jnp.int32, (32, BLK), 1)
        pick = (lanes == jnp.where(k < 16, k, k + BLK - 32)).astype(BF16)

        def turned(rows):
            return lax.dot_general(
                rows, pick, (LEFT_T, ((), ())), preferred_element_type=F32
            ).astype(BF16)

        base = kept + 64
        own = jnp.concatenate([turned(end[base : base + 32, :]), turned(end[base + 32 : base + 64, :])], axis=0)
        above, below = (
            turned(jnp.concatenate([part[BLK:, :BLK], part[BLK:, BLK : 2 * BLK]], axis=0))
            for part in (side_up, side_down)
        )
        fill(0, BLK, own[ROW0 : side - ROW0], above, below)
        full[:16, :BLK] = own[ROW0 - 16 : ROW0]
        full[stop:, :BLK] = own[side - ROW0 : side - ROW0 + 16]
        full[:, BLK + side :] = full[:, :BLK]
        for bj in range(nb):
            got = lax.dot_general(
                full[:, bj * BLK : (bj + 3) * BLK], band[...], (((1,), (1,)), ((), ())),
                preferred_element_type=F32,
            ).astype(BF16)
            for p in range(nu):
                passed[p, :, bj * BLK : (bj + 1) * BLK] = got[:, p * BLK : (p + 1) * BLK]
        for bi in range(nb):
            for bj in range(nb):
                cols = slice(bj * BLK, (bj + 1) * BLK)
                window = jnp.concatenate(
                    [passed[p, bi * BLK : bi * BLK + 160, cols] for p in range(nu)], axis=0
                )
                total = jnp.dot(kernels[bi * nb + bj], window, preferred_element_type=F32)
                rows = slice(bi * BLK, (bi + 1) * BLK)
                out[rows, cols] = frame[rows, cols] - total


def call(kernel, name, out_shape, in_specs, scratch=(), flops=0):
    many = isinstance(out_shape, tuple)
    return pl.pallas_call(
        kernel,
        out_shape=out_shape,
        in_specs=in_specs,
        out_specs=(VM,) * len(out_shape) if many else VM,
        scratch_shapes=list(scratch),
        compiler_params=pltpu.CompilerParams(vmem_limit_bytes=40 << 20),
        cost_estimate=pl.CostEstimate(flops=flops, bytes_accessed=flops // 500, transcendentals=0),
        name=name,
    )


def local(
    frames, row_shift, row_frac, col_shift, col_frac,
    profile_cols, profile_rows, coef_table, weight_ids,
):
    frame = frames[0]
    side = frame.shape[0]
    nb = side // BLK
    nu, nv = profile_cols.shape[0], profile_rows.shape[0]
    nx, ny = lax.axis_size("skyx"), lax.axis_size("skyy")
    row_frac = row_frac.reshape(nb, BLK)
    col_frac = col_frac.reshape(nb, BLK)
    width = nu * 160
    kept = side - 2 * ROW0
    inner = side - 2 * BLK
    cells = nb * nb
    shape = jax.ShapeDtypeStruct
    to_right, to_left, to_up, to_down = call(
        functools.partial(pack_kernel, nb), "pack",
        (shape((side + 8, BLK), F32),) * 2 + (shape((8, BLK), F32),) * 2,
        [VM] * 3 + [SM] * 2,
    )(frame, row_frac, col_frac, row_shift, col_shift)
    left = moved(to_right, (0, 0, 1), (0,))
    right = moved(to_left, (0, 0, -1), (0,))
    meta_up = moved(to_down, (0, 1, 0), (0,))
    meta_down = moved(to_up, (0, -1, 0), (0,))
    depth = row_start(nb, nb)
    own_mid, mid, *parts, kernels, band = call(
        functools.partial(center_kernel, nb, nu, nv), "center",
        (shape((side, inner), BF16), shape((kept, inner), BF16))
        + (shape((side, side), BF16),) * 2
        + (shape((side, inner), BF16),) * 2
        + (shape((depth, BLK), BF16),) * 2
        + (shape((4 * BLK, BLK), BF16),) * 2
        + (shape((cells, BLK, width), BF16), shape((nu * BLK, 3 * BLK), BF16)),
        [VM] * 3 + [SM] * 2 + [VM] * 3 + [SM],
        [pltpu.VMEM((cells, nu * nv), F32), pltpu.VMEM((8, width), F32)],
        flops=1 << 30,
    )(frame, row_frac, col_frac, row_shift, col_shift, profile_cols, profile_rows, coef_table, weight_ids)
    mid = moved(mid, (1, 0, 0), (0,))
    own_end, end, to_up, to_down = call(
        functools.partial(edge_kernel, nb, nx, ny), "edges",
        (shape((side, 2 * BLK), BF16), shape((kept + 128, side // 2), BF16))
        + (shape((BLK + 16, side), BF16),) * 2,
        [VM] * 12,
        [pltpu.VMEM((side, 3 * BLK), BF16)] * 2,
        flops=1 << 30,
    )(left, right, meta_up, meta_down, *parts)
    end = moved(end, (1, 0, 0), (0,))
    side_down = moved(to_up, (1, -1, 0), (0,))
    side_up = moved(to_down, (1, 1, 0), (0,))
    got_down = moved(to_up, (0, -1, 0), (0,))
    got_up = moved(to_down, (0, 1, 0), (0,))
    result = call(
        functools.partial(finish_kernel, nb, nu), "finish",
        shape((side, side), F32),
        [VM] * 11,
        [pltpu.VMEM((side + 32, side + 2 * BLK), BF16), pltpu.VMEM((nu, side + 32, side), BF16)],
        flops=1 << 30,
    )(frame, own_mid, own_end, side_up, side_down, mid, end, kernels, band, got_up, got_down)
    return result[None]


def solution(mesh):
    placed = (
        P("segment", "skyx", "skyy"), P("skyx"), P("skyx"), P("skyy"), P("skyy"),
        P(), P(), P(), P("skyx", "skyy"),
    )
    return jax.shard_map(
        local, mesh=mesh, in_specs=placed, out_specs=P("segment", "skyx", "skyy"), check_vma=False
    )
```

```python
import functools
import math

import jax
import jax.numpy as jnp
from jax import lax
from jax.experimental import pallas as pl
from jax.experimental.pallas import tpu as pltpu
from jax.sharding import PartitionSpec as P

BLK = 128
KW = 31
HALF = 15
ROW0 = 48
F32 = jnp.float32
BF16 = jnp.bfloat16
HIGHEST = lax.Precision.HIGHEST
VM = pl.BlockSpec(memory_space=pltpu.VMEM)
ANY = pl.BlockSpec(memory_space=pl.ANY)
FULL = 64 << 20


def moved(block, step, sources):
    axes = ("segment", "skyx", "skyy")
    counts = [lax.axis_size(axis) for axis in axes]
    route = []
    for s in range(counts[0]):
        for i in range(counts[1]):
            for j in range(counts[2]):
                to = (s + step[0], i + step[1], j + step[2])
                if s in sources and all(0 <= to[k] < counts[k] for k in range(3)):
                    flat = [(a * counts[1] + b) * counts[2] + c for a, b, c in ((s, i, j), to)]
                    route.append(tuple(flat))
    return lax.ppermute(block, axes, route)


def sinc(values):
    angle = math.pi * values
    zero = values == 0.0
    return jnp.where(zero, 1.0, jnp.sin(angle) / jnp.where(zero, 1.0, angle))


def taps(fracs):
    count = len(fracs)
    spread = jnp.concatenate([jnp.broadcast_to(frac, (8, BLK)) for frac in fracs], axis=0)
    lag = (lax.broadcasted_iota(jnp.int32, (8 * count, BLK), 0) & 7) - 2
    values = lag.astype(F32) - spread
    weight = jnp.where(jnp.abs(values) < 3.0, sinc(values) * sinc(values / 3.0), 0.0)
    return [weight[8 * n : 8 * n + 8] for n in range(count)]


def split(values):
    high = values.astype(BF16)
    return high, (values - high.astype(F32)).astype(BF16)


def banded(weight, shift, depth, offset):
    lag = (
        lax.broadcasted_iota(jnp.int32, (depth, BLK), 0)
        - lax.broadcasted_iota(jnp.int32, (depth, BLK), 1)
        + (offset - shift)
    )
    total = jnp.zeros((depth, BLK), F32)
    for tap in range(6):
        total = jnp.where(lag == tap - 2, weight[tap : tap + 1], total)
    return total


def dot3(left, right, dims):
    lh, ll = left
    rh, rl = right
    dot = functools.partial(
        lax.dot_general, dimension_numbers=(dims, ((), ())), preferred_element_type=F32
    )
    return dot(lh, rh) + dot(lh, rl) + dot(ll, rh)


MATMUL = ((1,), (0,))
LEFT_T = ((0,), (0,))


def row_depth(b, nb):
    return BLK if b in (0, nb - 1) else 3 * BLK


def row_start(b, nb):
    return sum(row_depth(a, nb) for a in range(b))


def row_source(b, nb):
    first = b if b in (0, nb - 1) else b - 1
    return slice(first * BLK, first * BLK + row_depth(b, nb))


def gather_kernel(
    nb, frame, row_frac, col_frac, row_shift, col_shift, table, prof_rows, prof_cols, ids,
    meta, row_meta, to_right, to_left,
    table_v, rows_v, cols_v, ids_v, row_s, col_s, sems,
):
    side = nb * BLK
    pairs = (
        (row_frac, meta.at[0:nb, :]),
        (col_frac, meta.at[2 * nb : 3 * nb, :]),
        (row_shift, row_s),
        (col_shift, col_s),
        (table, table_v),
        (prof_rows, rows_v),
        (prof_cols, cols_v),
        (ids, ids_v),
        (frame.at[:, side - BLK :], to_right.at[:side, :]),
        (frame.at[:, :BLK], to_left.at[:side, :]),
    )
    copies = [pltpu.make_async_copy(src, dst, sems.at[n]) for n, (src, dst) in enumerate(pairs)]
    for copy in copies:
        copy.start()
    for copy in copies:
        copy.wait()
    for b in range(nb):
        meta[nb + b : nb + b + 1, :] = jnp.full((1, BLK), row_s[b].astype(F32))
        meta[3 * nb + b : 3 * nb + b + 1, :] = jnp.full((1, BLK), col_s[b].astype(F32))
    base = 4 * nb
    for part in (table_v, rows_v, cols_v, ids_v):
        meta[base : base + part.shape[0], : part.shape[1]] = part[...].astype(F32)
        base += part.shape[0]
    row_meta[...] = meta[: 2 * nb, :]
    for out, b in ((to_right, nb - 1), (to_left, 0)):
        out[side : side + 1, :] = meta[2 * nb + b : 2 * nb + b + 1, :]
        out[side + 1 : side + 2, :] = meta[3 * nb + b : 3 * nb + b + 1, :]


def center_kernel(
    nb, frame, meta,
    own, across, src_hi, src_lo, mid_hi, mid_lo, row_hi, row_lo, edge_hi, edge_lo,
):
    side = nb * BLK

    @pl.when(lax.axis_index("segment") == 0)
    def _():
        fracs = [meta[2 * nb + b : 2 * nb + b + 1, :] for b in range(nb)]
        weights = taps(fracs + [meta[b : b + 1, :] for b in range(nb)])
        col_shift = [meta[3 * nb + b : 3 * nb + b + 1, :].astype(jnp.int32) for b in range(nb)]
        row_shift = [meta[nb + b : nb + b + 1, :].astype(jnp.int32) for b in range(nb)]
        hi, lo = split(frame[...])
        src_hi[...] = hi
        src_lo[...] = lo
        for b in range(1, nb - 1):
            mat = split(banded(weights[b], col_shift[b], 3 * BLK, -BLK))
            cols = slice((b - 1) * BLK, (b + 2) * BLK)
            hi, lo = split(dot3((src_hi[:, cols], src_lo[:, cols]), mat, MATMUL))
            mid_hi[:, (b - 1) * BLK : b * BLK] = hi
            mid_lo[:, (b - 1) * BLK : b * BLK] = lo
        for b in range(nb):
            offset = 0 if b in (0, nb - 1) else -BLK
            depth = row_depth(b, nb)
            hi, lo = split(banded(weights[nb + b], row_shift[b], depth, offset))
            kept = slice(row_start(b, nb), row_start(b, nb) + depth)
            row_hi[kept, :] = hi
            row_lo[kept, :] = lo
            rows = row_source(b, nb)
            got = dot3((hi, lo), (mid_hi[rows, :], mid_lo[rows, :]), LEFT_T).astype(BF16)
            own[b * BLK : (b + 1) * BLK, :] = got
            low = max(b * BLK, ROW0)
            high = min((b + 1) * BLK, side - ROW0)
            across[low - ROW0 : high - ROW0, :] = got[low - b * BLK : high - b * BLK, :]
        for n, (b, offset) in enumerate(((0, -BLK), (nb - 1, 0))):
            hi, lo = split(banded(weights[b], col_shift[b], 2 * BLK, offset))
            edge_hi[n * 2 * BLK : (n + 1) * 2 * BLK, :] = hi
            edge_lo[n * 2 * BLK : (n + 1) * 2 * BLK, :] = lo


def matrices_kernel(nb, nu, nv, sets, meta, after, kernels, band, padded):
    @pl.when(lax.axis_index("segment") != 0)
    def _():
        base = 4 * nb
        table = meta[base : base + sets, : nu * nv]
        base += sets
        prof_rows = meta[base : base + nv, :KW]
        base += nv
        prof_cols = meta[base : base + nu, :KW]
        base += nu
        entry = lax.broadcasted_iota(jnp.int32, (1, sets), 1)
        cells = []
        for bi in range(nb):
            for bj in range(nb):
                chosen = jnp.broadcast_to(meta[base + bi : base + bi + 1, bj : bj + 1], (1, sets))
                cells.append((chosen.astype(jnp.int32) == entry).astype(F32))
        coefs = jnp.dot(
            jnp.concatenate(cells, axis=0), table, precision=HIGHEST, preferred_element_type=F32
        )
        width = nu * 160
        padded[...] = jnp.zeros_like(padded)
        padded[0:nv, 0:KW] = prof_rows
        profile = padded[0:nv, :]
        spread = jnp.concatenate(
            [pltpu.roll(profile, p * 160 + 1, 1) for p in range(nu)], axis=0
        )
        base = jnp.dot(coefs, spread, precision=HIGHEST, preferred_element_type=F32)
        for cell in range(nb * nb):
            row = jnp.broadcast_to(base[cell : cell + 1, :], (BLK, width))
            kernels[cell] = pltpu.roll(row, 0, 1, stride=1, stride_axis=0).astype(BF16)
        padded[...] = jnp.zeros_like(padded)
        padded[0:nu, 0:KW] = prof_cols
        for p in range(nu):
            row = jnp.broadcast_to(padded[p : p + 1, : 3 * BLK], (BLK, 3 * BLK))
            band[p * BLK : (p + 1) * BLK, :] = pltpu.roll(
                row, BLK - HALF, 1, stride=1, stride_axis=0
            ).astype(BF16)


def edge_kernel(
    nb, nx, ny,
    left, right, meta_up, meta_down, src_hi, src_lo, mid_hi, mid_lo, row_hi, row_lo, edge_hi, edge_lo,
    own, across, side_up, side_down,
    end_hi, end_lo,
):
    side = nb * BLK
    kept = side - 2 * ROW0
    half = side // 2
    i = lax.axis_index("skyx")
    j = lax.axis_index("skyy")

    @pl.when(lax.axis_index("segment") == 0)
    def _():
        lanes = lax.broadcasted_iota(jnp.int32, (8, BLK), 1)
        weights = taps([left[side : side + 1, :], right[side : side + 1, :], meta_up[nb - 1 : nb, :], meta_down[0:1, :]])
        shifts = [
            part[row : row + 1, :].astype(jnp.int32)
            for part, row in ((left, side + 1), (right, side + 1), (meta_up, 2 * nb - 1), (meta_down, nb))
        ]
        parts = [split(left[:side, :]), split(right[:side, :])]
        for n, col in ((0, 0), (1, side - BLK)):
            source = []
            for part, src in zip(parts[n], (src_hi, src_lo)):
                inner = src[:, col : col + BLK]
                source.append(jnp.concatenate([part, inner] if n == 0 else [inner, part], axis=1))
            mat = tuple(edge[n * 2 * BLK : (n + 1) * 2 * BLK, :] for edge in (edge_hi, edge_lo))
            hi, lo = split(dot3(source, mat, MATMUL))
            end_hi[:, n * BLK : (n + 1) * BLK] = hi
            end_lo[:, n * BLK : (n + 1) * BLK] = lo
        low_ok = jnp.logical_and(lanes >= BLK - HALF, j > 0)
        high_ok = jnp.logical_and(lanes < HALF, j < ny - 1)
        low = split(banded(jnp.where(low_ok, weights[0], 0.0), shifts[0], BLK, BLK))
        high = split(banded(jnp.where(high_ok, weights[1], 0.0), shifts[1], BLK, -BLK))
        mat = [jnp.concatenate(pair, axis=0) for pair in zip(low, high)]
        source = [
            jnp.concatenate([src[:, :BLK], src[:, side - BLK :]], axis=1) for src in (src_hi, src_lo)
        ]
        hi, lo = split(dot3(source, mat, MATMUL))
        end_hi[:, 2 * BLK :] = hi
        end_lo[:, 2 * BLK :] = lo
        outer = []
        for n, b in ((0, 0), (1, nb - 1)):
            there = (i > 0) if n == 0 else (i < nx - 1)
            mat = split(banded(jnp.where(there, weights[2 + n], 0.0), shifts[2 + n], BLK, BLK if n == 0 else -BLK))
            rows = slice(b * BLK, (b + 1) * BLK)
            end = dot3(mat, (end_hi[rows, : 2 * BLK], end_lo[rows, : 2 * BLK]), LEFT_T).astype(BF16)
            mid = dot3(mat, (mid_hi[rows, :], mid_lo[rows, :]), LEFT_T).astype(BF16)
            turned = dot3((end_hi[rows, 2 * BLK :], end_lo[rows, 2 * BLK :]), mat, LEFT_T)
            out = side_up if n == 0 else side_down
            out[:BLK, :BLK] = end[:, :BLK]
            out[:BLK, BLK : side - BLK] = mid
            out[:BLK, side - BLK :] = end[:, BLK:]
            out[BLK:, :BLK] = turned[:16].astype(BF16)
            out[BLK:, BLK : 2 * BLK] = turned[BLK - 16 :].astype(BF16)
            outer.append(turned)
        across[kept : kept + 16, :] = side_down[:16, :half]
        across[kept + 16 : kept + 32, :] = side_up[BLK - 16 : BLK, :half]
        across[kept + 32 : kept + 48, :] = side_down[:16, half:]
        across[kept + 48 : kept + 64, :] = side_up[BLK - 16 : BLK, half:]
        columns = lax.broadcasted_iota(jnp.int32, (BLK, BLK), 1)
        for b in range(nb):
            hi, lo = (mat[row_start(b, nb) : row_start(b, nb) + row_depth(b, nb), :] for mat in (row_hi, row_lo))
            rows = row_source(b, nb)
            got = dot3((hi, lo), (end_hi[rows, : 2 * BLK], end_lo[rows, : 2 * BLK]), LEFT_T).astype(BF16)
            own[b * BLK : (b + 1) * BLK, :] = got
            low = max(b * BLK, ROW0)
            high = min((b + 1) * BLK, side - ROW0)
            across[low - ROW0 : high - ROW0, :] = got[low - b * BLK : high - b * BLK, :]
            turned = dot3((end_hi[rows, 2 * BLK :], end_lo[rows, 2 * BLK :]), (hi, lo), LEFT_T)
            if b == 0:
                turned = jnp.where(columns < ROW0, pltpu.roll(outer[0], ROW0, 1), turned)
            if b == nb - 1:
                turned = jnp.where(columns >= BLK - ROW0, pltpu.roll(outer[1], BLK - ROW0, 1), turned)
            half_at, lane = divmod(b * BLK, half)
            base = kept + 64 + 32 * half_at
            across[base : base + 16, lane : lane + BLK] = turned[:16].astype(BF16)
            across[base + 16 : base + 32, lane : lane + BLK] = turned[BLK - 16 :].astype(BF16)


def relay_kernel(up_in, down_in, end_in, up, down):
    @pl.when(lax.axis_index("segment") == 0)
    def _():
        up[...] = up_in[:BLK, :]
        down[...] = down_in[:BLK, :]


def finish_kernel(
    nb, nu,
    frame, own_mid, own_end, side_up, side_down, mid, end, kernels, band, got_up, got_down,
    out, full, passed,
):
    side = nb * BLK
    half = side // 2
    warper = lax.axis_index("segment") == 0
    last = side - BLK

    @pl.when(warper)
    def _():
        for b in range(nb):
            rows = slice(b * BLK, (b + 1) * BLK)
            pieces = ((0, own_end[rows, :BLK]), (BLK, own_mid[rows, :]), (last, own_end[rows, BLK:]))
            for lane, piece in pieces:
                cols = slice(lane, lane + piece.shape[1])
                total = piece.astype(F32)
                if b == 0:
                    total = (total + got_up[:BLK, cols].astype(F32)).astype(BF16).astype(F32)
                if b == nb - 1:
                    total = (total + got_down[:BLK, cols].astype(F32)).astype(BF16).astype(F32)
                out[rows, cols] = total

    @pl.when(jnp.logical_not(warper))
    def _():
        kept = side - 2 * ROW0
        both = BLK - ROW0
        stop = 16 + side

        def added(one, two):
            return (one.astype(F32) + two.astype(F32)).astype(BF16)

        def fill(at, width, own, above, below):
            cols = slice(at, at + width)
            full[16 : 16 + ROW0, cols] = above[:ROW0]
            full[16 + ROW0 : 16 + BLK, cols] = added(own[:both], above[ROW0:])
            full[16 + BLK : 16 + last, cols] = own[both : kept - both]
            full[16 + last : stop - ROW0, cols] = added(own[kept - both :], below[:both])
            full[stop - ROW0 : stop, cols] = below[both:]

        fill(2 * BLK, side - 2 * BLK, mid[:kept, :], side_up[:BLK, BLK:last], side_down[:BLK, BLK:last])
        fill(BLK, BLK, end[:kept, :BLK], side_up[:BLK, :BLK], side_down[:BLK, :BLK])
        fill(side, BLK, end[:kept, BLK:], side_up[:BLK, last:], side_down[:BLK, last:])
        full[:16, BLK : BLK + half] = end[kept + 16 : kept + 32, :]
        full[:16, BLK + half : BLK + side] = end[kept + 48 : kept + 64, :]
        full[stop:, BLK : BLK + half] = end[kept : kept + 16, :]
        full[stop:, BLK + half : BLK + side] = end[kept + 32 : kept + 48, :]
        k = lax.broadcasted_iota(jnp.int32, (32, BLK), 0)
        lanes = lax.broadcasted_iota(jnp.int32, (32, BLK), 1)
        pick = (lanes == jnp.where(k < 16, k, k + BLK - 32)).astype(BF16)

        def turned(rows):
            return lax.dot_general(
                rows, pick, (LEFT_T, ((), ())), preferred_element_type=F32
            ).astype(BF16)

        base = kept + 64
        own = jnp.concatenate([turned(end[base : base + 32, :]), turned(end[base + 32 : base + 64, :])], axis=0)
        above, below = (
            turned(jnp.concatenate([part[BLK:, :BLK], part[BLK:, BLK : 2 * BLK]], axis=0))
            for part in (side_up, side_down)
        )
        fill(0, BLK, own[ROW0 : side - ROW0], above, below)
        full[:16, :BLK] = own[ROW0 - 16 : ROW0]
        full[stop:, :BLK] = own[side - ROW0 : side - ROW0 + 16]
        full[:, BLK + side :] = full[:, :BLK]
        for bj in range(nb):
            got = lax.dot_general(
                full[:, bj * BLK : (bj + 3) * BLK], band[...], (((1,), (1,)), ((), ())),
                preferred_element_type=F32,
            ).astype(BF16)
            for p in range(nu):
                passed[p, :, bj * BLK : (bj + 1) * BLK] = got[:, p * BLK : (p + 1) * BLK]
        for bi in range(nb):
            for bj in range(nb):
                cols = slice(bj * BLK, (bj + 1) * BLK)
                window = jnp.concatenate(
                    [passed[p, bi * BLK : bi * BLK + 160, cols] for p in range(nu)], axis=0
                )
                total = jnp.dot(kernels[bi * nb + bj], window, preferred_element_type=F32)
                rows = slice(bi * BLK, (bi + 1) * BLK)
                out[rows, cols] = frame[rows, cols] - total


def call(kernel, name, out_shape, in_specs, scratch=(), flops=0, limit=40 << 20):
    many = isinstance(out_shape, tuple)
    return pl.pallas_call(
        kernel,
        out_shape=out_shape,
        in_specs=in_specs,
        out_specs=(VM,) * len(out_shape) if many else VM,
        scratch_shapes=list(scratch),
        compiler_params=pltpu.CompilerParams(vmem_limit_bytes=limit),
        cost_estimate=pl.CostEstimate(flops=flops, bytes_accessed=flops // 500, transcendentals=0),
        name=name,
    )


def local(
    frames, row_shift, row_frac, col_shift, col_frac,
    profile_cols, profile_rows, coef_table, weight_ids,
):
    frame = frames[0]
    side = frame.shape[0]
    nb = side // BLK
    nu, nv = profile_cols.shape[0], profile_rows.shape[0]
    nx, ny = lax.axis_size("skyx"), lax.axis_size("skyy")
    sets = coef_table.shape[0]
    row_frac = row_frac.reshape(nb, BLK)
    col_frac = col_frac.reshape(nb, BLK)

    width = nu * 160
    kept = side - 2 * ROW0
    inner = side - 2 * BLK
    cells = nb * nb
    shape = jax.ShapeDtypeStruct
    slab = shape((side + 8, BLK), F32)
    total = 4 * nb + sets + nv + nu + nb
    meta, row_meta, to_right, to_left = call(
        functools.partial(gather_kernel, nb), "gather",
        (shape((total + -total % 8, BLK), F32), shape((2 * nb, BLK), F32), slab, slab),
        [ANY] * 9,
        [
            pltpu.VMEM(coef_table.shape, F32), pltpu.VMEM(profile_rows.shape, BF16),
            pltpu.VMEM(profile_cols.shape, BF16), pltpu.VMEM(weight_ids.shape, jnp.int32),
            pltpu.SMEM((nb,), jnp.int32), pltpu.SMEM((nb,), jnp.int32), pltpu.SemaphoreType.DMA((10,)),
        ],
        limit=FULL,
    )(frame, row_frac, col_frac, row_shift, col_shift, coef_table, profile_rows, profile_cols, weight_ids)
    meta_up = moved(row_meta, (-1, 1, 0), (1,))
    meta_down = moved(row_meta, (-1, -1, 0), (1,))
    left = moved(to_right, (0, 0, 1), (0,))
    right = moved(to_left, (0, 0, -1), (0,))
    depth = row_start(nb, nb)
    own_mid, mid, *parts = call(
        functools.partial(center_kernel, nb), "center",
        (shape((side, inner), BF16), shape((kept, inner), BF16))
        + (shape((side, side), BF16),) * 2
        + (shape((side, inner), BF16),) * 2
        + (shape((depth, BLK), BF16),) * 2
        + (shape((4 * BLK, BLK), BF16),) * 2,
        [VM] * 2,
        flops=1 << 30,
    )(frame, meta)
    mid = moved(mid, (1, 0, 0), (0,))
    own_end, end, to_up, to_down = call(
        functools.partial(edge_kernel, nb, nx, ny), "edges",
        (shape((side, 2 * BLK), BF16), shape((kept + 128, side // 2), BF16))
        + (shape((BLK + 16, side), BF16),) * 2,
        [VM] * 12,
        [pltpu.VMEM((side, 3 * BLK), BF16)] * 2,
        flops=1 << 30,
    )(left, right, meta_up, meta_down, *parts)
    end = moved(end, (1, 0, 0), (0,))
    side_down = moved(to_up, (1, -1, 0), (0,))
    side_up = moved(to_down, (1, 1, 0), (0,))
    to_up, to_down = call(
        relay_kernel, "relay", (shape((BLK, side), BF16),) * 2, [VM] * 3
    )(to_up, to_down, own_end)
    got_down = moved(to_up, (0, -1, 0), (0,))
    got_up = moved(to_down, (0, 1, 0), (0,))
    kernels, band = call(
        functools.partial(matrices_kernel, nb, nu, nv, sets), "matrices",
        (shape((cells, BLK, width), BF16), shape((nu * BLK, 3 * BLK), BF16)),
        [VM] * 2,
        [pltpu.VMEM((8, width), F32)],
        flops=1 << 30,
    )(meta, own_end)
    result = call(
        functools.partial(finish_kernel, nb, nu), "finish",
        shape((side, side), F32),
        [VM] * 11,
        [pltpu.VMEM((side + 32, side + 2 * BLK), BF16), pltpu.VMEM((nu, side + 32, side), BF16)],
        flops=1 << 30,
    )(frame, own_mid, own_end, side_up, side_down, mid, end, kernels, band, got_up, got_down)
    return result[None]


def solution(mesh):
    placed = (
        P("segment", "skyx", "skyy"), P("skyx"), P("skyx"), P("skyy"), P("skyy"),
        P(), P(), P(), P("skyx", "skyy"),
    )
    return jax.shard_map(
        local, mesh=mesh, in_specs=placed, out_specs=P("segment", "skyx", "skyy"), check_vma=False
    )
```

```python
import functools
import math

import jax
import jax.numpy as jnp
from jax import lax
from jax.experimental import pallas as pl
from jax.experimental.pallas import tpu as pltpu
from jax.sharding import PartitionSpec as P

BLK = 128
KW = 31
HALF = 15
ROW0 = 48
F32 = jnp.float32
BF16 = jnp.bfloat16
HIGHEST = lax.Precision.HIGHEST
VM = pl.BlockSpec(memory_space=pltpu.VMEM)
ANY = pl.BlockSpec(memory_space=pl.ANY)
FULL = 64 << 20
SPARE = 1 << 15


def moved(block, step, sources):
    axes = ("segment", "skyx", "skyy")
    counts = [lax.axis_size(axis) for axis in axes]
    route = []
    for s in range(counts[0]):
        for i in range(counts[1]):
            for j in range(counts[2]):
                to = (s + step[0], i + step[1], j + step[2])
                if s in sources and all(0 <= to[k] < counts[k] for k in range(3)):
                    flat = [(a * counts[1] + b) * counts[2] + c for a, b, c in ((s, i, j), to)]
                    route.append(tuple(flat))
    return lax.ppermute(block, axes, route)


def sinc(values):
    angle = math.pi * values
    zero = values == 0.0
    return jnp.where(zero, 1.0, jnp.sin(angle) / jnp.where(zero, 1.0, angle))


def taps(fracs):
    count = len(fracs)
    spread = jnp.concatenate([jnp.broadcast_to(frac, (8, BLK)) for frac in fracs], axis=0)
    lag = (lax.broadcasted_iota(jnp.int32, (8 * count, BLK), 0) & 7) - 2
    values = lag.astype(F32) - spread
    weight = jnp.where(jnp.abs(values) < 3.0, sinc(values) * sinc(values / 3.0), 0.0)
    return [weight[8 * n : 8 * n + 8] for n in range(count)]


def split(values):
    high = values.astype(BF16)
    return high, (values - high.astype(F32)).astype(BF16)


def banded(weight, shift, depth, offset):
    lag = (
        lax.broadcasted_iota(jnp.int32, (depth, BLK), 0)
        - lax.broadcasted_iota(jnp.int32, (depth, BLK), 1)
        + (offset - shift)
    )
    total = jnp.zeros((depth, BLK), F32)
    for tap in range(6):
        total = jnp.where(lag == tap - 2, weight[tap : tap + 1], total)
    return total


def dot3(left, right, dims):
    lh, ll = left
    rh, rl = right
    dot = functools.partial(
        lax.dot_general, dimension_numbers=(dims, ((), ())), preferred_element_type=F32
    )
    return dot(lh, rh) + dot(lh, rl) + dot(ll, rh)


MATMUL = ((1,), (0,))
LEFT_T = ((0,), (0,))


def row_depth(b, nb):
    return BLK if b in (0, nb - 1) else 3 * BLK


def row_start(b, nb):
    return sum(row_depth(a, nb) for a in range(b))


def row_source(b, nb):
    first = b if b in (0, nb - 1) else b - 1
    return slice(first * BLK, first * BLK + row_depth(b, nb))


def gather_kernel(
    nb, frame, row_frac, col_frac, row_shift, col_shift, table, prof_rows, prof_cols, ids,
    meta_out, row_meta, to_right, to_left,
    meta, marks, table_v, rows_v, cols_v, ids_v, row_s, col_s, sems, done,
):
    side = nb * BLK
    warper = lax.axis_index("segment") == 0
    copies = [
        pltpu.make_async_copy(src, dst, sems.at[n])
        for n, (src, dst) in enumerate((
            (row_frac, meta.at[0:nb, :]),
            (col_frac, meta.at[2 * nb : 3 * nb, :]),
            (row_shift, row_s),
            (col_shift, col_s),
            (table, table_v),
            (prof_rows, rows_v),
            (prof_cols, cols_v),
            (ids, ids_v),
        ))
    ]
    slabs = [
        pltpu.make_async_copy(frame.at[:, side - BLK :], marks.at[0, :side, :], done.at[0]),
        pltpu.make_async_copy(frame.at[:, :BLK], marks.at[1, :side, :], done.at[1]),
    ]
    sends = [
        pltpu.make_async_copy(marks.at[0], to_right, done.at[2]),
        pltpu.make_async_copy(marks.at[1], to_left, done.at[3]),
    ]
    summary = pltpu.make_async_copy(meta, meta_out.at[: meta.shape[0], :], done.at[4])
    rows = pltpu.make_async_copy(meta.at[: 2 * nb, :], row_meta, done.at[5])

    @pl.when(warper)
    def _():
        for copy in slabs:
            copy.start()

    for copy in copies:
        copy.start()
    for copy in copies:
        copy.wait()
    for b in range(nb):
        meta[nb + b : nb + b + 1, :] = jnp.full((1, BLK), row_s[b].astype(F32))
        meta[3 * nb + b : 3 * nb + b + 1, :] = jnp.full((1, BLK), col_s[b].astype(F32))
    base = 4 * nb
    for part in (table_v, rows_v, cols_v, ids_v):
        meta[base : base + part.shape[0], : part.shape[1]] = part[...].astype(F32)
        base += part.shape[0]
    for n, b in ((0, nb - 1), (1, 0)):
        marks[n, side : side + 1, :] = meta[2 * nb + b : 2 * nb + b + 1, :]
        marks[n, side + 1 : side + 2, :] = meta[3 * nb + b : 3 * nb + b + 1, :]
    summary.start()
    rows.start()

    @pl.when(warper)
    def _():
        for copy, send in zip(slabs, sends):
            copy.wait()
            send.start()
        for send in sends:
            send.wait()

    summary.wait()
    rows.wait()


def center_kernel(
    nb, frame, meta_in,
    own, across, tip_hi, tip_lo, mid_hi, mid_lo, row_hi, row_lo, edge_hi, edge_lo,
    meta, src_hi, src_lo, sem,
):
    side = nb * BLK

    @pl.when(lax.axis_index("segment") == 0)
    def _():
        small = pltpu.make_async_copy(meta_in.at[: meta.shape[0], :], meta, sem)
        small.start()
        for b in range(nb):
            rows = slice(b * BLK, (b + 1) * BLK)
            hi, lo = split(frame[rows, :])
            for whole, tip, part in ((src_hi, tip_hi, hi), (src_lo, tip_lo, lo)):
                whole[rows, :] = part
                tip[rows, :BLK] = part[:, :BLK]
                tip[rows, BLK:] = part[:, side - BLK :]
        small.wait()
        fracs = [meta[2 * nb + b : 2 * nb + b + 1, :] for b in range(nb)]
        weights = taps(fracs + [meta[b : b + 1, :] for b in range(nb)])
        col_shift = [meta[3 * nb + b : 3 * nb + b + 1, :].astype(jnp.int32) for b in range(nb)]
        row_shift = [meta[nb + b : nb + b + 1, :].astype(jnp.int32) for b in range(nb)]
        for b in range(1, nb - 1):
            cols = slice((b - 1) * BLK, (b + 2) * BLK)
            mat = split(banded(weights[b], col_shift[b], 3 * BLK, -BLK))
            hi, lo = split(dot3((src_hi[:, cols], src_lo[:, cols]), mat, MATMUL))
            mid_hi[:, (b - 1) * BLK : b * BLK] = hi
            mid_lo[:, (b - 1) * BLK : b * BLK] = lo
        for b in range(nb):
            offset = 0 if b in (0, nb - 1) else -BLK
            depth = row_depth(b, nb)
            hi, lo = split(banded(weights[nb + b], row_shift[b], depth, offset))
            kept = slice(row_start(b, nb), row_start(b, nb) + depth)
            row_hi[kept, :] = hi
            row_lo[kept, :] = lo
            rows = row_source(b, nb)
            got = dot3((hi, lo), (mid_hi[rows, :], mid_lo[rows, :]), LEFT_T).astype(BF16)
            own[b * BLK : (b + 1) * BLK, :] = got
            low = max(b * BLK, ROW0)
            high = min((b + 1) * BLK, side - ROW0)
            across[low - ROW0 : high - ROW0, :] = got[low - b * BLK : high - b * BLK, :]
        for n, (b, offset) in enumerate(((0, -BLK), (nb - 1, 0))):
            hi, lo = split(banded(weights[b], col_shift[b], 2 * BLK, offset))
            edge_hi[n * 2 * BLK : (n + 1) * 2 * BLK, :] = hi
            edge_lo[n * 2 * BLK : (n + 1) * 2 * BLK, :] = lo


def matrices_kernel(nb, nu, nv, sets, meta_in, after, kernels, band, padded, meta, sem):
    @pl.when(lax.axis_index("segment") != 0)
    def _():
        small = pltpu.make_async_copy(meta_in.at[: meta.shape[0], :], meta, sem)
        small.start()
        small.wait()
        base = 4 * nb
        table = meta[base : base + sets, : nu * nv]
        base += sets
        prof_rows = meta[base : base + nv, :KW]
        base += nv
        prof_cols = meta[base : base + nu, :KW]
        base += nu
        entry = lax.broadcasted_iota(jnp.int32, (1, sets), 1)
        cells = []
        for bi in range(nb):
            for bj in range(nb):
                chosen = jnp.broadcast_to(meta[base + bi : base + bi + 1, bj : bj + 1], (1, sets))
                cells.append((chosen.astype(jnp.int32) == entry).astype(F32))
        coefs = jnp.dot(
            jnp.concatenate(cells, axis=0), table, precision=HIGHEST, preferred_element_type=F32
        )
        width = nu * 160
        padded[...] = jnp.zeros_like(padded)
        padded[0:nv, 0:KW] = prof_rows
        profile = padded[0:nv, :]
        spread = jnp.concatenate(
            [pltpu.roll(profile, p * 160 + 1, 1) for p in range(nu)], axis=0
        )
        base = jnp.dot(coefs, spread, precision=HIGHEST, preferred_element_type=F32)
        for cell in range(nb * nb):
            row = jnp.broadcast_to(base[cell : cell + 1, :], (BLK, width))
            kernels[cell] = pltpu.roll(row, 0, 1, stride=1, stride_axis=0).astype(BF16)
        padded[...] = jnp.zeros_like(padded)
        padded[0:nu, 0:KW] = prof_cols
        for p in range(nu):
            row = jnp.broadcast_to(padded[p : p + 1, : 3 * BLK], (BLK, 3 * BLK))
            band[p * BLK : (p + 1) * BLK, :] = pltpu.roll(
                row, BLK - HALF, 1, stride=1, stride_axis=0
            ).astype(BF16)


def edge_kernel(
    nb, nx, ny,
    left, right, meta_up, meta_down, tip_hi, tip_lo, mid_hi, mid_lo, row_hi, row_lo, edge_hi, edge_lo,
    own, across, side_up, side_down,
    end_hi, end_lo,
):
    side = nb * BLK
    kept = side - 2 * ROW0
    half = side // 2
    i = lax.axis_index("skyx")
    j = lax.axis_index("skyy")

    @pl.when(lax.axis_index("segment") == 0)
    def _():
        lanes = lax.broadcasted_iota(jnp.int32, (8, BLK), 1)
        weights = taps([left[side : side + 1, :], right[side : side + 1, :], meta_up[nb - 1 : nb, :], meta_down[0:1, :]])
        shifts = [
            part[row : row + 1, :].astype(jnp.int32)
            for part, row in ((left, side + 1), (right, side + 1), (meta_up, 2 * nb - 1), (meta_down, nb))
        ]
        parts = [split(left[:side, :]), split(right[:side, :])]
        for n in range(2):
            source = []
            for part, tip in zip(parts[n], (tip_hi, tip_lo)):
                inner = tip[:, n * BLK : (n + 1) * BLK]
                source.append(jnp.concatenate([part, inner] if n == 0 else [inner, part], axis=1))
            mat = tuple(edge[n * 2 * BLK : (n + 1) * 2 * BLK, :] for edge in (edge_hi, edge_lo))
            hi, lo = split(dot3(source, mat, MATMUL))
            end_hi[:, n * BLK : (n + 1) * BLK] = hi
            end_lo[:, n * BLK : (n + 1) * BLK] = lo
        low_ok = jnp.logical_and(lanes >= BLK - HALF, j > 0)
        high_ok = jnp.logical_and(lanes < HALF, j < ny - 1)
        low = split(banded(jnp.where(low_ok, weights[0], 0.0), shifts[0], BLK, BLK))
        high = split(banded(jnp.where(high_ok, weights[1], 0.0), shifts[1], BLK, -BLK))
        mat = [jnp.concatenate(pair, axis=0) for pair in zip(low, high)]
        hi, lo = split(dot3((tip_hi[...], tip_lo[...]), mat, MATMUL))
        end_hi[:, 2 * BLK :] = hi
        end_lo[:, 2 * BLK :] = lo
        outer = []
        for n, b in ((0, 0), (1, nb - 1)):
            there = (i > 0) if n == 0 else (i < nx - 1)
            mat = split(banded(jnp.where(there, weights[2 + n], 0.0), shifts[2 + n], BLK, BLK if n == 0 else -BLK))
            rows = slice(b * BLK, (b + 1) * BLK)
            end = dot3(mat, (end_hi[rows, : 2 * BLK], end_lo[rows, : 2 * BLK]), LEFT_T).astype(BF16)
            mid = dot3(mat, (mid_hi[rows, :], mid_lo[rows, :]), LEFT_T).astype(BF16)
            turned = dot3((end_hi[rows, 2 * BLK :], end_lo[rows, 2 * BLK :]), mat, LEFT_T)
            out = side_up if n == 0 else side_down
            out[:BLK, :BLK] = end[:, :BLK]
            out[:BLK, BLK : side - BLK] = mid
            out[:BLK, side - BLK :] = end[:, BLK:]
            out[BLK:, :BLK] = turned[:16].astype(BF16)
            out[BLK:, BLK : 2 * BLK] = turned[BLK - 16 :].astype(BF16)
            outer.append(turned)
        across[kept : kept + 16, :] = side_down[:16, :half]
        across[kept + 16 : kept + 32, :] = side_up[BLK - 16 : BLK, :half]
        across[kept + 32 : kept + 48, :] = side_down[:16, half:]
        across[kept + 48 : kept + 64, :] = side_up[BLK - 16 : BLK, half:]
        columns = lax.broadcasted_iota(jnp.int32, (BLK, BLK), 1)
        for b in range(nb):
            hi, lo = (mat[row_start(b, nb) : row_start(b, nb) + row_depth(b, nb), :] for mat in (row_hi, row_lo))
            rows = row_source(b, nb)
            got = dot3((hi, lo), (end_hi[rows, : 2 * BLK], end_lo[rows, : 2 * BLK]), LEFT_T).astype(BF16)
            own[b * BLK : (b + 1) * BLK, :] = got
            low = max(b * BLK, ROW0)
            high = min((b + 1) * BLK, side - ROW0)
            across[low - ROW0 : high - ROW0, :] = got[low - b * BLK : high - b * BLK, :]
            turned = dot3((end_hi[rows, 2 * BLK :], end_lo[rows, 2 * BLK :]), (hi, lo), LEFT_T)
            if b == 0:
                turned = jnp.where(columns < ROW0, pltpu.roll(outer[0], ROW0, 1), turned)
            if b == nb - 1:
                turned = jnp.where(columns >= BLK - ROW0, pltpu.roll(outer[1], BLK - ROW0, 1), turned)
            half_at, lane = divmod(b * BLK, half)
            base = kept + 64 + 32 * half_at
            across[base : base + 16, lane : lane + BLK] = turned[:16].astype(BF16)
            across[base + 16 : base + 32, lane : lane + BLK] = turned[BLK - 16 :].astype(BF16)


def relay_kernel(up_in, down_in, end_in, up, down):
    @pl.when(lax.axis_index("segment") == 0)
    def _():
        up[...] = up_in[:BLK, :]
        down[...] = down_in[:BLK, :]


def finish_kernel(
    nb, nu,
    frame, own_mid, own_end, side_up, side_down, mid, end, kernels, band, got_up, got_down,
    out, full, passed,
):
    side = nb * BLK
    half = side // 2
    warper = lax.axis_index("segment") == 0
    last = side - BLK

    @pl.when(warper)
    def _():
        for b in range(nb):
            rows = slice(b * BLK, (b + 1) * BLK)
            pieces = ((0, own_end[rows, :BLK]), (BLK, own_mid[rows, :]), (last, own_end[rows, BLK:]))
            for lane, piece in pieces:
                cols = slice(lane, lane + piece.shape[1])
                total = piece.astype(F32)
                if b == 0:
                    total = (total + got_up[:BLK, cols].astype(F32)).astype(BF16).astype(F32)
                if b == nb - 1:
                    total = (total + got_down[:BLK, cols].astype(F32)).astype(BF16).astype(F32)
                out[rows, cols] = total

    @pl.when(jnp.logical_not(warper))
    def _():
        kept = side - 2 * ROW0
        both = BLK - ROW0
        stop = 16 + side

        def added(one, two):
            return (one.astype(F32) + two.astype(F32)).astype(BF16)

        def fill(at, width, own, above, below):
            cols = slice(at, at + width)
            full[16 : 16 + ROW0, cols] = above[:ROW0]
            full[16 + ROW0 : 16 + BLK, cols] = added(own[:both], above[ROW0:])
            full[16 + BLK : 16 + last, cols] = own[both : kept - both]
            full[16 + last : stop - ROW0, cols] = added(own[kept - both :], below[:both])
            full[stop - ROW0 : stop, cols] = below[both:]

        fill(2 * BLK, side - 2 * BLK, mid[:kept, :], side_up[:BLK, BLK:last], side_down[:BLK, BLK:last])
        fill(BLK, BLK, end[:kept, :BLK], side_up[:BLK, :BLK], side_down[:BLK, :BLK])
        fill(side, BLK, end[:kept, BLK:], side_up[:BLK, last:], side_down[:BLK, last:])
        full[:16, BLK : BLK + half] = end[kept + 16 : kept + 32, :]
        full[:16, BLK + half : BLK + side] = end[kept + 48 : kept + 64, :]
        full[stop:, BLK : BLK + half] = end[kept : kept + 16, :]
        full[stop:, BLK + half : BLK + side] = end[kept + 32 : kept + 48, :]
        k = lax.broadcasted_iota(jnp.int32, (32, BLK), 0)
        lanes = lax.broadcasted_iota(jnp.int32, (32, BLK), 1)
        pick = (lanes == jnp.where(k < 16, k, k + BLK - 32)).astype(BF16)

        def turned(rows):
            return lax.dot_general(
                rows, pick, (LEFT_T, ((), ())), preferred_element_type=F32
            ).astype(BF16)

        base = kept + 64
        own = jnp.concatenate([turned(end[base : base + 32, :]), turned(end[base + 32 : base + 64, :])], axis=0)
        above, below = (
            turned(jnp.concatenate([part[BLK:, :BLK], part[BLK:, BLK : 2 * BLK]], axis=0))
            for part in (side_up, side_down)
        )
        fill(0, BLK, own[ROW0 : side - ROW0], above, below)
        full[:16, :BLK] = own[ROW0 - 16 : ROW0]
        full[stop:, :BLK] = own[side - ROW0 : side - ROW0 + 16]
        full[:, BLK + side :] = full[:, :BLK]
        for bj in range(nb):
            got = lax.dot_general(
                full[:, bj * BLK : (bj + 3) * BLK], band[...], (((1,), (1,)), ((), ())),
                preferred_element_type=F32,
            ).astype(BF16)
            for p in range(nu):
                passed[p, :, bj * BLK : (bj + 1) * BLK] = got[:, p * BLK : (p + 1) * BLK]
        for bi in range(nb):
            for bj in range(nb):
                cols = slice(bj * BLK, (bj + 1) * BLK)
                window = jnp.concatenate(
                    [passed[p, bi * BLK : bi * BLK + 160, cols] for p in range(nu)], axis=0
                )
                total = jnp.dot(kernels[bi * nb + bj], window, preferred_element_type=F32)
                rows = slice(bi * BLK, (bi + 1) * BLK)
                out[rows, cols] = frame[rows, cols] - total


def call(kernel, name, out_shape, in_specs, scratch=(), flops=0, limit=40 << 20):
    many = isinstance(out_shape, tuple)
    return pl.pallas_call(
        kernel,
        out_shape=out_shape,
        in_specs=in_specs,
        out_specs=(VM,) * len(out_shape) if many else VM,
        scratch_shapes=list(scratch),
        compiler_params=pltpu.CompilerParams(vmem_limit_bytes=limit),
        cost_estimate=pl.CostEstimate(flops=flops, bytes_accessed=flops // 500, transcendentals=0),
        name=name,
    )


def local(
    frames, row_shift, row_frac, col_shift, col_frac,
    profile_cols, profile_rows, coef_table, weight_ids,
):
    frame = frames[0]
    side = frame.shape[0]
    nb = side // BLK
    nu, nv = profile_cols.shape[0], profile_rows.shape[0]
    nx, ny = lax.axis_size("skyx"), lax.axis_size("skyy")
    sets = coef_table.shape[0]
    row_frac = row_frac.reshape(nb, BLK)
    col_frac = col_frac.reshape(nb, BLK)

    width = nu * 160
    kept = side - 2 * ROW0
    inner = side - 2 * BLK
    cells = nb * nb
    shape = jax.ShapeDtypeStruct
    slab = shape((side + 8, BLK), F32)
    total = 4 * nb + sets + nv + nu + nb
    total += -total % 8
    meta_shape = pltpu.VMEM((total, BLK), F32)
    meta, row_meta, to_right, to_left = pl.pallas_call(
        functools.partial(gather_kernel, nb),
        out_shape=(shape((SPARE, BLK), F32), shape((2 * nb, BLK), F32), slab, slab),
        in_specs=[ANY] * 9,
        out_specs=(ANY,) * 4,
        scratch_shapes=[
            meta_shape, pltpu.VMEM((2, side + 8, BLK), F32),
            pltpu.VMEM(coef_table.shape, F32), pltpu.VMEM(profile_rows.shape, BF16),
            pltpu.VMEM(profile_cols.shape, BF16), pltpu.VMEM(weight_ids.shape, jnp.int32),
            pltpu.SMEM((nb,), jnp.int32), pltpu.SMEM((nb,), jnp.int32),
            pltpu.SemaphoreType.DMA((8,)), pltpu.SemaphoreType.DMA((6,)),
        ],
        compiler_params=pltpu.CompilerParams(vmem_limit_bytes=FULL),
        name="gather",
    )(frame, row_frac, col_frac, row_shift, col_shift, coef_table, profile_rows, profile_cols, weight_ids)
    meta_up = moved(row_meta, (-1, 1, 0), (1,))
    meta_down = moved(row_meta, (-1, -1, 0), (1,))
    left = moved(to_right, (0, 0, 1), (0,))
    right = moved(to_left, (0, 0, -1), (0,))
    depth = row_start(nb, nb)
    own_mid, mid, *parts = call(
        functools.partial(center_kernel, nb), "center",
        (shape((side, inner), BF16), shape((kept, inner), BF16))
        + (shape((side, 2 * BLK), BF16),) * 2
        + (shape((side, inner), BF16),) * 2
        + (shape((depth, BLK), BF16),) * 2
        + (shape((4 * BLK, BLK), BF16),) * 2,
        [VM, ANY],
        [
            meta_shape, pltpu.VMEM((side, side), BF16), pltpu.VMEM((side, side), BF16),
            pltpu.SemaphoreType.DMA(()),
        ],
        flops=1 << 33,
    )(frame, meta)
    mid = moved(mid, (1, 0, 0), (0,))
    own_end, end, to_up, to_down = call(
        functools.partial(edge_kernel, nb, nx, ny), "edges",
        (shape((side, 2 * BLK), BF16), shape((kept + 128, side // 2), BF16))
        + (shape((BLK + 16, side), BF16),) * 2,
        [VM] * 12,
        [pltpu.VMEM((side, 3 * BLK), BF16)] * 2,
        flops=1 << 33,
    )(left, right, meta_up, meta_down, *parts)
    end = moved(end, (1, 0, 0), (0,))
    side_down = moved(to_up, (1, -1, 0), (0,))
    side_up = moved(to_down, (1, 1, 0), (0,))
    to_up, to_down = call(
        relay_kernel, "relay", (shape((BLK, side), BF16),) * 2, [VM] * 3
    )(to_up, to_down, own_end)
    got_down = moved(to_up, (0, -1, 0), (0,))
    got_up = moved(to_down, (0, 1, 0), (0,))
    kernels, band = call(
        functools.partial(matrices_kernel, nb, nu, nv, sets), "matrices",
        (shape((cells, BLK, width), BF16), shape((nu * BLK, 3 * BLK), BF16)),
        [ANY, VM],
        [pltpu.VMEM((8, width), F32), meta_shape, pltpu.SemaphoreType.DMA(())],
        flops=0,
    )(meta, own_end)
    result = call(
        functools.partial(finish_kernel, nb, nu), "finish",
        shape((side, side), F32),
        [VM] * 11,
        [pltpu.VMEM((side + 32, side + 2 * BLK), BF16), pltpu.VMEM((nu, side + 32, side), BF16)],
        flops=0,
    )(frame, own_mid, own_end, side_up, side_down, mid, end, kernels, band, got_up, got_down)
    return result[None]


def solution(mesh):
    placed = (
        P("segment", "skyx", "skyy"), P("skyx"), P("skyx"), P("skyy"), P("skyy"),
        P(), P(), P(), P("skyx", "skyy"),
    )
    return jax.shard_map(
        local, mesh=mesh, in_specs=placed, out_specs=P("segment", "skyx", "skyy"), check_vma=False
    )
```

```python
import functools
import math

import jax
import jax.numpy as jnp
from jax import lax
from jax.experimental import pallas as pl
from jax.experimental.pallas import tpu as pltpu
from jax.sharding import PartitionSpec as P

BLK = 128
KW = 31
HALF = 15
ROW0 = 48
F32 = jnp.float32
BF16 = jnp.bfloat16
HIGHEST = lax.Precision.HIGHEST
VM = pl.BlockSpec(memory_space=pltpu.VMEM)
ANY = pl.BlockSpec(memory_space=pl.ANY)
FULL = 64 << 20
SPARE = 1 << 15


def moved(block, step, sources):
    axes = ("segment", "skyx", "skyy")
    counts = [lax.axis_size(axis) for axis in axes]
    route = []
    for s in range(counts[0]):
        for i in range(counts[1]):
            for j in range(counts[2]):
                to = (s + step[0], i + step[1], j + step[2])
                if s in sources and all(0 <= to[k] < counts[k] for k in range(3)):
                    flat = [(a * counts[1] + b) * counts[2] + c for a, b, c in ((s, i, j), to)]
                    route.append(tuple(flat))
    return lax.ppermute(block, axes, route)


def sinc(values):
    angle = math.pi * values
    zero = values == 0.0
    return jnp.where(zero, 1.0, jnp.sin(angle) / jnp.where(zero, 1.0, angle))


def taps(fracs):
    count = len(fracs)
    spread = jnp.concatenate([jnp.broadcast_to(frac, (8, BLK)) for frac in fracs], axis=0)
    lag = (lax.broadcasted_iota(jnp.int32, (8 * count, BLK), 0) & 7) - 2
    values = lag.astype(F32) - spread
    weight = jnp.where(jnp.abs(values) < 3.0, sinc(values) * sinc(values / 3.0), 0.0)
    return [weight[8 * n : 8 * n + 8] for n in range(count)]


def split(values):
    high = values.astype(BF16)
    return high, (values - high.astype(F32)).astype(BF16)


def banded(weight, shift, depth, offset):
    lag = (
        lax.broadcasted_iota(jnp.int32, (depth, BLK), 0)
        - lax.broadcasted_iota(jnp.int32, (depth, BLK), 1)
        + (offset - shift)
    )
    total = jnp.zeros((depth, BLK), F32)
    for tap in range(6):
        total = jnp.where(lag == tap - 2, weight[tap : tap + 1], total)
    return total


def dot3(left, right, dims):
    lh, ll = left
    rh, rl = right
    dot = functools.partial(
        lax.dot_general, dimension_numbers=(dims, ((), ())), preferred_element_type=F32
    )
    return dot(lh, rh) + dot(lh, rl) + dot(ll, rh)


MATMUL = ((1,), (0,))
LEFT_T = ((0,), (0,))


def packed3(left, right):
    lh, ll = left
    rh, rl = right
    width = rh.shape[1]
    dot = functools.partial(jnp.dot, preferred_element_type=F32)
    both = dot(lh, jnp.concatenate([rh, rl], axis=1))
    return both[:, :width] + both[:, width:] + dot(ll, rh)


def gather_kernel(
    nb, frame, row_frac, col_frac, row_shift, col_shift, table, prof_rows, prof_cols, ids,
    meta_out, row_meta, to_right, to_left,
    meta, marks, table_v, rows_v, cols_v, ids_v, row_s, col_s, sems, done,
):
    side = nb * BLK
    warper = lax.axis_index("segment") == 0
    copies = [
        pltpu.make_async_copy(src, dst, sems.at[n])
        for n, (src, dst) in enumerate((
            (row_frac, meta.at[0:nb, :]),
            (col_frac, meta.at[2 * nb : 3 * nb, :]),
            (row_shift, row_s),
            (col_shift, col_s),
            (table, table_v),
            (prof_rows, rows_v),
            (prof_cols, cols_v),
            (ids, ids_v),
        ))
    ]
    slabs = [
        pltpu.make_async_copy(frame.at[:, side - BLK :], marks.at[0, :side, :], done.at[0]),
        pltpu.make_async_copy(frame.at[:, :BLK], marks.at[1, :side, :], done.at[1]),
    ]
    sends = [
        pltpu.make_async_copy(marks.at[0], to_right, done.at[2]),
        pltpu.make_async_copy(marks.at[1], to_left, done.at[3]),
    ]
    summary = pltpu.make_async_copy(meta, meta_out.at[: meta.shape[0], :], done.at[4])
    rows = pltpu.make_async_copy(meta.at[: 2 * nb, :], row_meta, done.at[5])

    @pl.when(warper)
    def _():
        for copy in slabs:
            copy.start()

    for copy in copies:
        copy.start()
    for copy in copies:
        copy.wait()
    for b in range(nb):
        meta[nb + b : nb + b + 1, :] = jnp.full((1, BLK), row_s[b].astype(F32))
        meta[3 * nb + b : 3 * nb + b + 1, :] = jnp.full((1, BLK), col_s[b].astype(F32))
    base = 4 * nb
    for part in (table_v, rows_v, cols_v, ids_v):
        meta[base : base + part.shape[0], : part.shape[1]] = part[...].astype(F32)
        base += part.shape[0]
    for n, b in ((0, nb - 1), (1, 0)):
        marks[n, side : side + 1, :] = meta[2 * nb + b : 2 * nb + b + 1, :]
        marks[n, side + 1 : side + 2, :] = meta[3 * nb + b : 3 * nb + b + 1, :]
    summary.start()
    rows.start()

    @pl.when(warper)
    def _():
        for copy, send in zip(slabs, sends):
            copy.wait()
            send.start()
        for send in sends:
            send.wait()

    summary.wait()
    rows.wait()


def center_kernel(
    nb, frame, meta_in,
    own, across, tip_hi, tip_lo, mid_hi, mid_lo, row_hi, row_lo, edge_hi, edge_lo,
    meta, src_hi, src_lo, sem,
):
    side = nb * BLK

    @pl.when(lax.axis_index("segment") == 0)
    def _():
        small = pltpu.make_async_copy(meta_in.at[: meta.shape[0], :], meta, sem)
        small.start()
        for b in range(nb):
            rows = slice(b * BLK, (b + 1) * BLK)
            hi, lo = split(frame[rows, :])
            for whole, tip, part in ((src_hi, tip_hi, hi), (src_lo, tip_lo, lo)):
                whole[rows, :] = part
                tip[rows, :BLK] = part[:, :BLK]
                tip[rows, BLK:] = part[:, side - BLK :]
        small.wait()
        fracs = [meta[2 * nb + b : 2 * nb + b + 1, :] for b in range(nb)]
        weights = taps(fracs + [meta[b : b + 1, :] for b in range(nb)])
        col_shift = [meta[3 * nb + b : 3 * nb + b + 1, :].astype(jnp.int32) for b in range(nb)]
        row_shift = [meta[nb + b : nb + b + 1, :].astype(jnp.int32) for b in range(nb)]
        for b in range(1, nb - 1):
            mat = split(banded(weights[b], col_shift[b], 3 * BLK, -BLK))
            cols = slice((b - 1) * BLK, (b + 2) * BLK)
            hi, lo = split(packed3((src_hi[:, cols], src_lo[:, cols]), mat))
            mid_hi[:, (b - 1) * BLK : b * BLK] = hi
            mid_lo[:, (b - 1) * BLK : b * BLK] = lo
        for b in range(nb):
            first, depth = (b, BLK) if b in (0, nb - 1) else (b - 1, 3 * BLK)
            mat = split(banded(weights[nb + b], row_shift[b], depth, (first - b) * BLK).T)
            rows, cols = slice(b * BLK, (b + 1) * BLK), slice(first * BLK, first * BLK + depth)
            row_hi[rows, cols], row_lo[rows, cols] = mat
            got = dot3(mat, (mid_hi[cols, :], mid_lo[cols, :]), MATMUL).astype(BF16)
            own[rows, :] = got
            low = max(b * BLK, ROW0)
            high = min((b + 1) * BLK, side - ROW0)
            across[low - ROW0 : high - ROW0, :] = got[low - b * BLK : high - b * BLK, :]
        for n, (b, offset) in enumerate(((0, -BLK), (nb - 1, 0))):
            hi, lo = split(banded(weights[b], col_shift[b], 2 * BLK, offset))
            edge_hi[n * 2 * BLK : (n + 1) * 2 * BLK, :] = hi
            edge_lo[n * 2 * BLK : (n + 1) * 2 * BLK, :] = lo


def matrices_kernel(nb, nu, nv, sets, meta_in, after, kernels, band, padded, meta, sem):
    @pl.when(lax.axis_index("segment") != 0)
    def _():
        small = pltpu.make_async_copy(meta_in.at[: meta.shape[0], :], meta, sem)
        small.start()
        small.wait()
        base = 4 * nb
        table = meta[base : base + sets, : nu * nv]
        base += sets
        prof_rows = meta[base : base + nv, :KW]
        base += nv
        prof_cols = meta[base : base + nu, :KW]
        base += nu
        entry = lax.broadcasted_iota(jnp.int32, (1, sets), 1)
        cells = []
        for bi in range(nb):
            for bj in range(nb):
                chosen = jnp.broadcast_to(meta[base + bi : base + bi + 1, bj : bj + 1], (1, sets))
                cells.append((chosen.astype(jnp.int32) == entry).astype(F32))
        coefs = jnp.dot(
            jnp.concatenate(cells, axis=0), table, precision=HIGHEST, preferred_element_type=F32
        )
        width = nu * 160
        padded[...] = jnp.zeros_like(padded)
        padded[0:nv, 0:KW] = prof_rows
        profile = padded[0:nv, :]
        spread = jnp.concatenate(
            [pltpu.roll(profile, p * 160 + 1, 1) for p in range(nu)], axis=0
        )
        base = jnp.dot(coefs, spread, precision=HIGHEST, preferred_element_type=F32)
        for cell in range(nb * nb):
            row = jnp.broadcast_to(base[cell : cell + 1, :], (BLK, width))
            kernels[cell] = pltpu.roll(row, 0, 1, stride=1, stride_axis=0).astype(BF16)
        padded[...] = jnp.zeros_like(padded)
        padded[0:nu, 0:KW] = prof_cols
        for p in range(nu):
            row = jnp.broadcast_to(padded[p : p + 1, : 2 * BLK], (BLK, 2 * BLK))
            band[p * BLK : (p + 1) * BLK, :] = pltpu.roll(row, 1, 1, stride=1, stride_axis=0).astype(BF16)


def edge_kernel(
    nb, nx, ny,
    left, right, meta_up, meta_down, tip_hi, tip_lo, mid_hi, mid_lo, row_hi, row_lo, edge_hi, edge_lo,
    own, across, side_up, side_down,
    end_hi, end_lo,
):
    side = nb * BLK
    kept = side - 2 * ROW0
    half = side // 2
    i = lax.axis_index("skyx")
    j = lax.axis_index("skyy")

    @pl.when(lax.axis_index("segment") == 0)
    def _():
        lanes = lax.broadcasted_iota(jnp.int32, (8, BLK), 1)
        weights = taps([left[side : side + 1, :], right[side : side + 1, :], meta_up[nb - 1 : nb, :], meta_down[0:1, :]])
        shifts = [
            part[row : row + 1, :].astype(jnp.int32)
            for part, row in ((left, side + 1), (right, side + 1), (meta_up, 2 * nb - 1), (meta_down, nb))
        ]
        parts = [split(left[:side, :]), split(right[:side, :])]
        for n in range(2):
            source = []
            for part, tip in zip(parts[n], (tip_hi, tip_lo)):
                inner = tip[:, n * BLK : (n + 1) * BLK]
                source.append(jnp.concatenate([part, inner] if n == 0 else [inner, part], axis=1))
            mat = tuple(edge[n * 2 * BLK : (n + 1) * 2 * BLK, :] for edge in (edge_hi, edge_lo))
            hi, lo = split(packed3(source, mat))
            end_hi[:, n * BLK : (n + 1) * BLK] = hi
            end_lo[:, n * BLK : (n + 1) * BLK] = lo
        low_ok = jnp.logical_and(lanes >= BLK - HALF, j > 0)
        high_ok = jnp.logical_and(lanes < HALF, j < ny - 1)
        low = split(banded(jnp.where(low_ok, weights[0], 0.0), shifts[0], BLK, BLK))
        high = split(banded(jnp.where(high_ok, weights[1], 0.0), shifts[1], BLK, -BLK))
        mat = [jnp.concatenate(pair, axis=0) for pair in zip(low, high)]
        hi, lo = split(packed3((tip_hi[...], tip_lo[...]), mat))
        end_hi[:, 2 * BLK :] = hi
        end_lo[:, 2 * BLK :] = lo
        outer = []
        for n, b in ((0, 0), (1, nb - 1)):
            there = (i > 0) if n == 0 else (i < nx - 1)
            weight = jnp.where(there, weights[2 + n], 0.0)
            mat = split(banded(weight, shifts[2 + n], BLK, BLK if n == 0 else -BLK).T)
            rows = slice(b * BLK, (b + 1) * BLK)
            source = [
                jnp.concatenate([mid[rows, :], end[rows, :]], axis=1)
                for mid, end in ((mid_hi, end_hi), (mid_lo, end_lo))
            ]
            got = dot3(mat, source, MATMUL)
            outer.append(got)
            out = side_up if n == 0 else side_down
            inner = side - 2 * BLK
            out[:BLK, BLK : side - BLK] = got[:, :inner].astype(BF16)
            out[:BLK, :BLK] = got[:, inner : inner + BLK].astype(BF16)
            out[:BLK, side - BLK :] = got[:, inner + BLK : side].astype(BF16)
            turned = got[:, side:].T
            out[BLK:, :BLK] = turned[:16].astype(BF16)
            out[BLK:, BLK : 2 * BLK] = turned[BLK - 16 :].astype(BF16)
        across[kept : kept + 16, :] = side_down[:16, :half]
        across[kept + 16 : kept + 32, :] = side_up[BLK - 16 : BLK, :half]
        across[kept + 32 : kept + 48, :] = side_down[:16, half:]
        across[kept + 48 : kept + 64, :] = side_up[BLK - 16 : BLK, half:]
        strips = []
        for b in range(nb):
            first, depth = (b, BLK) if b in (0, nb - 1) else (b - 1, 3 * BLK)
            rows, cols = slice(b * BLK, (b + 1) * BLK), slice(first * BLK, first * BLK + depth)
            mat = (row_hi[rows, cols], row_lo[rows, cols])
            got = dot3(mat, (end_hi[cols, : 2 * BLK], end_lo[cols, : 2 * BLK]), MATMUL).astype(BF16)
            own[rows, :] = got
            low = max(b * BLK, ROW0)
            high = min((b + 1) * BLK, side - ROW0)
            across[low - ROW0 : high - ROW0, :] = got[low - b * BLK : high - b * BLK, :]
            strips.append(packed3(mat, (end_hi[cols, 2 * BLK :], end_lo[cols, 2 * BLK :])))
        strip = jnp.concatenate(strips, axis=0)
        strip = jnp.concatenate(
            [
                strip[: ROW0 - 16], outer[0][BLK - 16 :, side:], strip[ROW0 : side - ROW0],
                outer[1][:16, side:], strip[side - ROW0 + 16 :],
            ],
            axis=0,
        ).T
        for n in range(2):
            base = kept + 64 + 32 * n
            cols = slice(n * half, (n + 1) * half)
            across[base : base + 16, :] = strip[:16, cols].astype(BF16)
            across[base + 16 : base + 32, :] = strip[BLK - 16 :, cols].astype(BF16)


def relay_kernel(up_in, down_in, end_in, up, down):
    @pl.when(lax.axis_index("segment") == 0)
    def _():
        up[...] = up_in[:BLK, :]
        down[...] = down_in[:BLK, :]


def finish_kernel(
    nb, nu,
    frame, own_mid, own_end, side_up, side_down, mid, end, kernels, band, got_up, got_down,
    out, result, wide, full, passed, sems,
):
    side = nb * BLK
    half = side // 2
    warper = lax.axis_index("segment") == 0
    last = side - BLK
    sends = []
    for b in range(nb):
        rows = pl.ds(b * BLK, BLK)
        sends.append(pltpu.make_async_copy(result.at[rows, :], out.at[rows, :], sems.at[b]))

    @pl.when(warper)
    def _():
        for b in range(nb):
            rows = slice(b * BLK, (b + 1) * BLK)
            pieces = ((0, own_end[rows, :BLK]), (BLK, own_mid[rows, :]), (last, own_end[rows, BLK:]))
            for lane, piece in pieces:
                cols = slice(lane, lane + piece.shape[1])
                total = piece.astype(F32)
                if b == 0:
                    total = (total + got_up[:BLK, cols].astype(F32)).astype(BF16).astype(F32)
                if b == nb - 1:
                    total = (total + got_down[:BLK, cols].astype(F32)).astype(BF16).astype(F32)
                result[rows, cols] = total
            sends[b].start()

    @pl.when(jnp.logical_not(warper))
    def _():
        kept = side - 2 * ROW0
        both = BLK - ROW0
        stop = 16 + side

        def added(one, two):
            return (one.astype(F32) + two.astype(F32)).astype(BF16)

        def fill(at, width, own, above, below):
            cols = slice(at, at + width)
            wide[16 : 16 + ROW0, cols] = above[:ROW0]
            wide[16 + ROW0 : 16 + BLK, cols] = added(own[:both], above[ROW0:])
            wide[16 + BLK : 16 + last, cols] = own[both : kept - both]
            wide[16 + last : stop - ROW0, cols] = added(own[kept - both :], below[:both])
            wide[stop - ROW0 : stop, cols] = below[both:]

        fill(BLK, side - 2 * BLK, mid[:kept, :], side_up[:BLK, BLK:last], side_down[:BLK, BLK:last])
        fill(0, BLK, end[:kept, :BLK], side_up[:BLK, :BLK], side_down[:BLK, :BLK])
        fill(last, BLK, end[:kept, BLK:], side_up[:BLK, last:], side_down[:BLK, last:])
        wide[:16, :half] = end[kept + 16 : kept + 32, :]
        wide[:16, half:side] = end[kept + 48 : kept + 64, :]
        wide[stop:, :half] = end[kept : kept + 16, :]
        wide[stop:, half:side] = end[kept + 32 : kept + 48, :]
        k = lax.broadcasted_iota(jnp.int32, (32, BLK), 0)
        lanes = lax.broadcasted_iota(jnp.int32, (32, BLK), 1)
        pick = (lanes == jnp.where(k < 16, k, k + BLK - 32)).astype(BF16)

        def turned(rows):
            return lax.dot_general(
                rows, pick, (LEFT_T, ((), ())), preferred_element_type=F32
            ).astype(BF16)

        base = kept + 64
        own = jnp.concatenate([turned(end[base : base + 32, :]), turned(end[base + 32 : base + 64, :])], axis=0)
        above, below = (
            turned(jnp.concatenate([part[BLK:, :BLK], part[BLK:, BLK : 2 * BLK]], axis=0))
            for part in (side_up, side_down)
        )
        fill(side, BLK, own[ROW0 : side - ROW0], above, below)
        wide[:16, side:] = own[ROW0 - 16 : ROW0]
        wide[stop:, side:] = own[side - ROW0 : side - ROW0 + 16]
        cut = side + BLK - 16
        full[...] = jnp.concatenate([wide[:, cut:], wide[:, :cut]], axis=1)
        for bj in range(nb):
            got = lax.dot_general(
                full[:, bj * BLK : (bj + 2) * BLK], band[...], (((1,), (1,)), ((), ())),
                preferred_element_type=F32,
            ).astype(BF16)
            for p in range(nu):
                passed[p, :, bj * BLK : (bj + 1) * BLK] = got[:, p * BLK : (p + 1) * BLK]
        for bi in range(nb):
            for bj in range(nb):
                cols = slice(bj * BLK, (bj + 1) * BLK)
                window = jnp.concatenate(
                    [passed[p, bi * BLK : bi * BLK + 160, cols] for p in range(nu)], axis=0
                )
                total = jnp.dot(kernels[bi * nb + bj], window, preferred_element_type=F32)
                rows = slice(bi * BLK, (bi + 1) * BLK)
                result[rows, cols] = frame[rows, cols] - total
            sends[bi].start()

    for send in sends:
        send.wait()


def call(kernel, name, out_shape, in_specs, scratch=(), flops=0, limit=40 << 20):
    many = isinstance(out_shape, tuple)
    return pl.pallas_call(
        kernel,
        out_shape=out_shape,
        in_specs=in_specs,
        out_specs=(VM,) * len(out_shape) if many else VM,
        scratch_shapes=list(scratch),
        compiler_params=pltpu.CompilerParams(vmem_limit_bytes=limit),
        cost_estimate=pl.CostEstimate(flops=flops, bytes_accessed=flops // 500, transcendentals=0),
        name=name,
    )


def local(
    frames, row_shift, row_frac, col_shift, col_frac,
    profile_cols, profile_rows, coef_table, weight_ids,
):
    frame = frames[0]
    side = frame.shape[0]
    nb = side // BLK
    nu, nv = profile_cols.shape[0], profile_rows.shape[0]
    nx, ny = lax.axis_size("skyx"), lax.axis_size("skyy")
    sets = coef_table.shape[0]
    row_frac = row_frac.reshape(nb, BLK)
    col_frac = col_frac.reshape(nb, BLK)

    width = nu * 160
    kept = side - 2 * ROW0
    inner = side - 2 * BLK
    cells = nb * nb
    shape = jax.ShapeDtypeStruct
    slab = shape((side + 8, BLK), F32)
    total = 4 * nb + sets + nv + nu + nb
    total += -total % 8
    meta_shape = pltpu.VMEM((total, BLK), F32)
    meta, row_meta, to_right, to_left = pl.pallas_call(
        functools.partial(gather_kernel, nb),
        out_shape=(shape((SPARE, BLK), F32), shape((2 * nb, BLK), F32), slab, slab),
        in_specs=[ANY] * 9,
        out_specs=(ANY,) * 4,
        scratch_shapes=[
            meta_shape, pltpu.VMEM((2, side + 8, BLK), F32),
            pltpu.VMEM(coef_table.shape, F32), pltpu.VMEM(profile_rows.shape, BF16),
            pltpu.VMEM(profile_cols.shape, BF16), pltpu.VMEM(weight_ids.shape, jnp.int32),
            pltpu.SMEM((nb,), jnp.int32), pltpu.SMEM((nb,), jnp.int32),
            pltpu.SemaphoreType.DMA((8,)), pltpu.SemaphoreType.DMA((6,)),
        ],
        compiler_params=pltpu.CompilerParams(vmem_limit_bytes=FULL),
        name="gather",
    )(frame, row_frac, col_frac, row_shift, col_shift, coef_table, profile_rows, profile_cols, weight_ids)
    meta_up = moved(row_meta, (-1, 1, 0), (1,))
    meta_down = moved(row_meta, (-1, -1, 0), (1,))
    left = moved(to_right, (0, 0, 1), (0,))
    right = moved(to_left, (0, 0, -1), (0,))
    own_mid, mid, *parts = call(
        functools.partial(center_kernel, nb), "center",
        (shape((side, inner), BF16), shape((kept, inner), BF16))
        + (shape((side, 2 * BLK), BF16),) * 2
        + (shape((side, inner), BF16),) * 2
        + (shape((side, side), BF16),) * 2
        + (shape((4 * BLK, BLK), BF16),) * 2,
        [VM, ANY],
        [
            meta_shape, pltpu.VMEM((side, side), BF16), pltpu.VMEM((side, side), BF16),
            pltpu.SemaphoreType.DMA(()),
        ],
        flops=1 << 33,
    )(frame, meta)
    mid = moved(mid, (1, 0, 0), (0,))
    own_end, end, to_up, to_down = call(
        functools.partial(edge_kernel, nb, nx, ny), "edges",
        (shape((side, 2 * BLK), BF16), shape((kept + 128, side // 2), BF16))
        + (shape((BLK + 16, side), BF16),) * 2,
        [VM] * 12,
        [pltpu.VMEM((side, 3 * BLK), BF16)] * 2,
        flops=1 << 33,
    )(left, right, meta_up, meta_down, *parts)
    end = moved(end, (1, 0, 0), (0,))
    side_down = moved(to_up, (1, -1, 0), (0,))
    side_up = moved(to_down, (1, 1, 0), (0,))
    to_up, to_down = call(
        relay_kernel, "relay", (shape((BLK, side), BF16),) * 2, [VM] * 3
    )(to_up, to_down, own_end)
    got_down = moved(to_up, (0, -1, 0), (0,))
    got_up = moved(to_down, (0, 1, 0), (0,))
    kernels, band = call(
        functools.partial(matrices_kernel, nb, nu, nv, sets), "matrices",
        (shape((cells, BLK, width), BF16), shape((nu * BLK, 2 * BLK), BF16)),
        [ANY, VM],
        [pltpu.VMEM((8, width), F32), meta_shape, pltpu.SemaphoreType.DMA(())],
        flops=0,
    )(meta, own_end)
    result = pl.pallas_call(
        functools.partial(finish_kernel, nb, nu),
        out_shape=shape((side, side), F32),
        in_specs=[VM] * 11,
        out_specs=ANY,
        scratch_shapes=[
            pltpu.VMEM((side, side), F32), pltpu.VMEM((side + 32, side + BLK), BF16),
            pltpu.VMEM((side + 32, side + BLK), BF16), pltpu.VMEM((nu, side + 32, side), BF16),
            pltpu.SemaphoreType.DMA((nb,)),
        ],
        compiler_params=pltpu.CompilerParams(vmem_limit_bytes=40 << 20),
        name="finish",
    )(frame, own_mid, own_end, side_up, side_down, mid, end, kernels, band, got_up, got_down)
    return result[None]


def solution(mesh):
    placed = (
        P("segment", "skyx", "skyy"), P("skyx"), P("skyx"), P("skyy"), P("skyy"),
        P(), P(), P(), P("skyx", "skyy"),
    )
    return jax.shard_map(
        local, mesh=mesh, in_specs=placed, out_specs=P("segment", "skyx", "skyy"), check_vma=False
    )
```

```python
import functools
import math

import jax
import jax.numpy as jnp
from jax import lax
from jax.experimental import pallas as pl
from jax.experimental.pallas import tpu as pltpu
from jax.sharding import PartitionSpec as P

BLK = 128
KW = 31
HALF = 15
ROW0 = 48
F32 = jnp.float32
BF16 = jnp.bfloat16
HIGHEST = lax.Precision.HIGHEST
VM = pl.BlockSpec(memory_space=pltpu.VMEM)
ANY = pl.BlockSpec(memory_space=pl.ANY)
FULL = 64 << 20
SPARE = 1 << 15


def moved(block, step, sources):
    axes = ("segment", "skyx", "skyy")
    counts = [lax.axis_size(axis) for axis in axes]
    route = []
    for s in range(counts[0]):
        for i in range(counts[1]):
            for j in range(counts[2]):
                to = (s + step[0], i + step[1], j + step[2])
                if s in sources and all(0 <= to[k] < counts[k] for k in range(3)):
                    flat = [(a * counts[1] + b) * counts[2] + c for a, b, c in ((s, i, j), to)]
                    route.append(tuple(flat))
    return lax.ppermute(block, axes, route)


def sinc(values):
    angle = math.pi * values
    zero = values == 0.0
    return jnp.where(zero, 1.0, jnp.sin(angle) / jnp.where(zero, 1.0, angle))


def taps(fracs):
    count = len(fracs)
    spread = jnp.concatenate([jnp.broadcast_to(frac, (8, BLK)) for frac in fracs], axis=0)
    lag = (lax.broadcasted_iota(jnp.int32, (8 * count, BLK), 0) & 7) - 2
    values = lag.astype(F32) - spread
    weight = jnp.where(jnp.abs(values) < 3.0, sinc(values) * sinc(values / 3.0), 0.0)
    return [weight[8 * n : 8 * n + 8] for n in range(count)]


def split(values):
    high = values.astype(BF16)
    return high, (values - high.astype(F32)).astype(BF16)


def banded(weight, shift, depth, offset):
    lag = (
        lax.broadcasted_iota(jnp.int32, (depth, BLK), 0)
        - lax.broadcasted_iota(jnp.int32, (depth, BLK), 1)
        + (offset - shift)
    )
    total = jnp.zeros((depth, BLK), F32)
    for tap in range(6):
        total = jnp.where(lag == tap - 2, weight[tap : tap + 1], total)
    return total


def dot3(left, right, dims):
    lh, ll = left
    rh, rl = right
    dot = functools.partial(
        lax.dot_general, dimension_numbers=(dims, ((), ())), preferred_element_type=F32
    )
    return dot(lh, rh) + dot(lh, rl) + dot(ll, rh)


MATMUL = ((1,), (0,))
LEFT_T = ((0,), (0,))


def packed3(left, right):
    lh, ll = left
    rh, rl = right
    width = rh.shape[1]
    dot = functools.partial(jnp.dot, preferred_element_type=F32)
    both = dot(lh, jnp.concatenate([rh, rl], axis=1))
    return both[:, :width] + both[:, width:] + dot(ll, rh)


def gather_kernel(
    nb, frame, row_frac, col_frac, row_shift, col_shift, table, prof_rows, prof_cols, ids,
    meta_out, row_meta, to_right, to_left,
    meta, marks, table_v, rows_v, cols_v, ids_v, row_s, col_s, sems, done,
):
    side = nb * BLK
    warper = lax.axis_index("segment") == 0
    copies = [
        pltpu.make_async_copy(src, dst, sems.at[n])
        for n, (src, dst) in enumerate((
            (row_frac, meta.at[0:nb, :]),
            (col_frac, meta.at[2 * nb : 3 * nb, :]),
            (row_shift, row_s),
            (col_shift, col_s),
            (table, table_v),
            (prof_rows, rows_v),
            (prof_cols, cols_v),
            (ids, ids_v),
        ))
    ]
    slabs = [
        pltpu.make_async_copy(frame.at[:, side - BLK :], marks.at[0, :side, :], done.at[0]),
        pltpu.make_async_copy(frame.at[:, :BLK], marks.at[1, :side, :], done.at[1]),
    ]
    sends = [
        pltpu.make_async_copy(marks.at[0], to_right, done.at[2]),
        pltpu.make_async_copy(marks.at[1], to_left, done.at[3]),
    ]
    summary = pltpu.make_async_copy(meta, meta_out.at[: meta.shape[0], :], done.at[4])
    rows = pltpu.make_async_copy(meta.at[: 2 * nb, :], row_meta, done.at[5])

    @pl.when(warper)
    def _():
        for copy in slabs:
            copy.start()

    for copy in copies:
        copy.start()
    for copy in copies:
        copy.wait()
    for b in range(nb):
        meta[nb + b : nb + b + 1, :] = jnp.full((1, BLK), row_s[b].astype(F32))
        meta[3 * nb + b : 3 * nb + b + 1, :] = jnp.full((1, BLK), col_s[b].astype(F32))
    base = 4 * nb
    for part in (table_v, rows_v, cols_v, ids_v):
        meta[base : base + part.shape[0], : part.shape[1]] = part[...].astype(F32)
        base += part.shape[0]
    for n, b in ((0, nb - 1), (1, 0)):
        marks[n, side : side + 1, :] = meta[2 * nb + b : 2 * nb + b + 1, :]
        marks[n, side + 1 : side + 2, :] = meta[3 * nb + b : 3 * nb + b + 1, :]
    summary.start()
    rows.start()

    @pl.when(warper)
    def _():
        for copy, send in zip(slabs, sends):
            copy.wait()
            send.start()
        for send in sends:
            send.wait()

    summary.wait()
    rows.wait()


def marker_kernel(meta_in, mark):
    mark[...] = jnp.zeros_like(mark)


def center_kernel(
    nb, frame, meta_in, mark,
    own, across, tip_hi, tip_lo, mid_hi, mid_lo, row_hi, row_lo, edge_hi, edge_lo,
    meta, src_hi, src_lo, sem,
):
    side = nb * BLK

    @pl.when(lax.axis_index("segment") == 0)
    def _():
        small = pltpu.make_async_copy(meta_in.at[: meta.shape[0], :], meta, sem)
        small.start()
        for b in range(nb):
            rows = slice(b * BLK, (b + 1) * BLK)
            hi, lo = split(frame[rows, :])
            for whole, tip, part in ((src_hi, tip_hi, hi), (src_lo, tip_lo, lo)):
                whole[rows, :] = part
                tip[rows, :BLK] = part[:, :BLK]
                tip[rows, BLK:] = part[:, side - BLK :]
        small.wait()
        fracs = [meta[2 * nb + b : 2 * nb + b + 1, :] for b in range(nb)]
        weights = taps(fracs + [meta[b : b + 1, :] for b in range(nb)])
        col_shift = [meta[3 * nb + b : 3 * nb + b + 1, :].astype(jnp.int32) for b in range(nb)]
        row_shift = [meta[nb + b : nb + b + 1, :].astype(jnp.int32) for b in range(nb)]
        for b in range(1, nb - 1):
            mat = split(banded(weights[b], col_shift[b], 3 * BLK, -BLK))
            cols = slice((b - 1) * BLK, (b + 2) * BLK)
            hi, lo = split(packed3((src_hi[:, cols], src_lo[:, cols]), mat))
            mid_hi[:, (b - 1) * BLK : b * BLK] = hi
            mid_lo[:, (b - 1) * BLK : b * BLK] = lo
        for b in range(nb):
            first, depth = (b, BLK) if b in (0, nb - 1) else (b - 1, 3 * BLK)
            mat = split(banded(weights[nb + b], row_shift[b], depth, (first - b) * BLK).T)
            rows, cols = slice(b * BLK, (b + 1) * BLK), slice(first * BLK, first * BLK + depth)
            row_hi[rows, cols], row_lo[rows, cols] = mat
            got = dot3(mat, (mid_hi[cols, :], mid_lo[cols, :]), MATMUL).astype(BF16)
            own[rows, :] = got
            low = max(b * BLK, ROW0)
            high = min((b + 1) * BLK, side - ROW0)
            across[low - ROW0 : high - ROW0, :] = got[low - b * BLK : high - b * BLK, :]
        for n, (b, offset) in enumerate(((0, -BLK), (nb - 1, 0))):
            hi, lo = split(banded(weights[b], col_shift[b], 2 * BLK, offset))
            edge_hi[n * 2 * BLK : (n + 1) * 2 * BLK, :] = hi
            edge_lo[n * 2 * BLK : (n + 1) * 2 * BLK, :] = lo


def matrices_kernel(nb, nu, nv, sets, meta_in, after, kernels, band, padded, meta, sem):
    @pl.when(lax.axis_index("segment") != 0)
    def _():
        small = pltpu.make_async_copy(meta_in.at[: meta.shape[0], :], meta, sem)
        small.start()
        small.wait()
        base = 4 * nb
        table = meta[base : base + sets, : nu * nv]
        base += sets
        prof_rows = meta[base : base + nv, :KW]
        base += nv
        prof_cols = meta[base : base + nu, :KW]
        base += nu
        entry = lax.broadcasted_iota(jnp.int32, (1, sets), 1)
        cells = []
        for bi in range(nb):
            for bj in range(nb):
                chosen = jnp.broadcast_to(meta[base + bi : base + bi + 1, bj : bj + 1], (1, sets))
                cells.append((chosen.astype(jnp.int32) == entry).astype(F32))
        coefs = jnp.dot(
            jnp.concatenate(cells, axis=0), table, precision=HIGHEST, preferred_element_type=F32
        )
        width = nu * 160
        padded[...] = jnp.zeros_like(padded)
        padded[0:nv, 0:KW] = prof_rows
        profile = padded[0:nv, :]
        spread = jnp.concatenate(
            [pltpu.roll(profile, p * 160 + 1, 1) for p in range(nu)], axis=0
        )
        base = jnp.dot(coefs, spread, precision=HIGHEST, preferred_element_type=F32)
        for cell in range(nb * nb):
            row = jnp.broadcast_to(base[cell : cell + 1, :], (BLK, width))
            kernels[cell] = pltpu.roll(row, 0, 1, stride=1, stride_axis=0).astype(BF16)
        padded[...] = jnp.zeros_like(padded)
        padded[0:nu, 0:KW] = prof_cols
        for p in range(nu):
            row = jnp.broadcast_to(padded[p : p + 1, : 2 * BLK], (BLK, 2 * BLK))
            band[p * BLK : (p + 1) * BLK, :] = pltpu.roll(row, 1, 1, stride=1, stride_axis=0).astype(BF16)


def edge_kernel(
    nb, nx, ny,
    left, right, meta_up, meta_down, tip_hi, tip_lo, mid_hi, mid_lo, row_hi, row_lo, edge_hi, edge_lo,
    own, across, side_up, side_down,
    end_hi, end_lo,
):
    side = nb * BLK
    kept = side - 2 * ROW0
    half = side // 2
    i = lax.axis_index("skyx")
    j = lax.axis_index("skyy")

    @pl.when(lax.axis_index("segment") == 0)
    def _():
        lanes = lax.broadcasted_iota(jnp.int32, (8, BLK), 1)
        weights = taps([left[side : side + 1, :], right[side : side + 1, :], meta_up[nb - 1 : nb, :], meta_down[0:1, :]])
        shifts = [
            part[row : row + 1, :].astype(jnp.int32)
            for part, row in ((left, side + 1), (right, side + 1), (meta_up, 2 * nb - 1), (meta_down, nb))
        ]
        parts = [split(left[:side, :]), split(right[:side, :])]
        for n in range(2):
            source = []
            for part, tip in zip(parts[n], (tip_hi, tip_lo)):
                inner = tip[:, n * BLK : (n + 1) * BLK]
                source.append(jnp.concatenate([part, inner] if n == 0 else [inner, part], axis=1))
            mat = tuple(edge[n * 2 * BLK : (n + 1) * 2 * BLK, :] for edge in (edge_hi, edge_lo))
            hi, lo = split(packed3(source, mat))
            end_hi[:, n * BLK : (n + 1) * BLK] = hi
            end_lo[:, n * BLK : (n + 1) * BLK] = lo
        low_ok = jnp.logical_and(lanes >= BLK - HALF, j > 0)
        high_ok = jnp.logical_and(lanes < HALF, j < ny - 1)
        low = split(banded(jnp.where(low_ok, weights[0], 0.0), shifts[0], BLK, BLK))
        high = split(banded(jnp.where(high_ok, weights[1], 0.0), shifts[1], BLK, -BLK))
        mat = [jnp.concatenate(pair, axis=0) for pair in zip(low, high)]
        hi, lo = split(packed3((tip_hi[...], tip_lo[...]), mat))
        end_hi[:, 2 * BLK :] = hi
        end_lo[:, 2 * BLK :] = lo
        outer = []
        for n, b in ((0, 0), (1, nb - 1)):
            there = (i > 0) if n == 0 else (i < nx - 1)
            weight = jnp.where(there, weights[2 + n], 0.0)
            mat = split(banded(weight, shifts[2 + n], BLK, BLK if n == 0 else -BLK).T)
            rows = slice(b * BLK, (b + 1) * BLK)
            source = [
                jnp.concatenate([mid[rows, :], end[rows, :]], axis=1)
                for mid, end in ((mid_hi, end_hi), (mid_lo, end_lo))
            ]
            got = dot3(mat, source, MATMUL)
            outer.append(got)
            out = side_up if n == 0 else side_down
            inner = side - 2 * BLK
            out[:BLK, BLK : side - BLK] = got[:, :inner].astype(BF16)
            out[:BLK, :BLK] = got[:, inner : inner + BLK].astype(BF16)
            out[:BLK, side - BLK :] = got[:, inner + BLK : side].astype(BF16)
            turned = got[:, side:].T
            out[BLK:, :BLK] = turned[:16].astype(BF16)
            out[BLK:, BLK : 2 * BLK] = turned[BLK - 16 :].astype(BF16)
        across[kept : kept + 16, :] = side_down[:16, :half]
        across[kept + 16 : kept + 32, :] = side_up[BLK - 16 : BLK, :half]
        across[kept + 32 : kept + 48, :] = side_down[:16, half:]
        across[kept + 48 : kept + 64, :] = side_up[BLK - 16 : BLK, half:]
        strips = []
        for b in range(nb):
            first, depth = (b, BLK) if b in (0, nb - 1) else (b - 1, 3 * BLK)
            rows, cols = slice(b * BLK, (b + 1) * BLK), slice(first * BLK, first * BLK + depth)
            mat = (row_hi[rows, cols], row_lo[rows, cols])
            got = dot3(mat, (end_hi[cols, : 2 * BLK], end_lo[cols, : 2 * BLK]), MATMUL).astype(BF16)
            own[rows, :] = got
            low = max(b * BLK, ROW0)
            high = min((b + 1) * BLK, side - ROW0)
            across[low - ROW0 : high - ROW0, :] = got[low - b * BLK : high - b * BLK, :]
            strips.append(packed3(mat, (end_hi[cols, 2 * BLK :], end_lo[cols, 2 * BLK :])))
        strip = jnp.concatenate(strips, axis=0)
        strip = jnp.concatenate(
            [
                strip[: ROW0 - 16], outer[0][BLK - 16 :, side:], strip[ROW0 : side - ROW0],
                outer[1][:16, side:], strip[side - ROW0 + 16 :],
            ],
            axis=0,
        ).T
        for n in range(2):
            base = kept + 64 + 32 * n
            cols = slice(n * half, (n + 1) * half)
            across[base : base + 16, :] = strip[:16, cols].astype(BF16)
            across[base + 16 : base + 32, :] = strip[BLK - 16 :, cols].astype(BF16)


def relay_kernel(up_in, down_in, end_in, up, down):
    @pl.when(lax.axis_index("segment") == 0)
    def _():
        up[...] = up_in[:BLK, :]
        down[...] = down_in[:BLK, :]


def finish_kernel(
    nb, nu,
    frame, own_mid, own_end, side_up, side_down, mid, end, kernels, band, got_up, got_down,
    out, result, wide, full, passed, sems,
):
    side = nb * BLK
    half = side // 2
    warper = lax.axis_index("segment") == 0
    last = side - BLK
    sends = []
    for b in range(nb):
        rows = pl.ds(b * BLK, BLK)
        sends.append(pltpu.make_async_copy(result.at[rows, :], out.at[rows, :], sems.at[b]))

    @pl.when(warper)
    def _():
        for b in range(nb):
            rows = slice(b * BLK, (b + 1) * BLK)
            pieces = ((0, own_end[rows, :BLK]), (BLK, own_mid[rows, :]), (last, own_end[rows, BLK:]))
            for lane, piece in pieces:
                cols = slice(lane, lane + piece.shape[1])
                total = piece.astype(F32)
                if b == 0:
                    total = (total + got_up[:BLK, cols].astype(F32)).astype(BF16).astype(F32)
                if b == nb - 1:
                    total = (total + got_down[:BLK, cols].astype(F32)).astype(BF16).astype(F32)
                result[rows, cols] = total
            sends[b].start()

    @pl.when(jnp.logical_not(warper))
    def _():
        kept = side - 2 * ROW0
        both = BLK - ROW0
        stop = 16 + side

        def added(one, two):
            return (one.astype(F32) + two.astype(F32)).astype(BF16)

        def fill(at, width, own, above, below):
            cols = slice(at, at + width)
            wide[16 : 16 + ROW0, cols] = above[:ROW0]
            wide[16 + ROW0 : 16 + BLK, cols] = added(own[:both], above[ROW0:])
            wide[16 + BLK : 16 + last, cols] = own[both : kept - both]
            wide[16 + last : stop - ROW0, cols] = added(own[kept - both :], below[:both])
            wide[stop - ROW0 : stop, cols] = below[both:]

        fill(BLK, side - 2 * BLK, mid[:kept, :], side_up[:BLK, BLK:last], side_down[:BLK, BLK:last])
        fill(0, BLK, end[:kept, :BLK], side_up[:BLK, :BLK], side_down[:BLK, :BLK])
        fill(last, BLK, end[:kept, BLK:], side_up[:BLK, last:], side_down[:BLK, last:])
        wide[:16, :half] = end[kept + 16 : kept + 32, :]
        wide[:16, half:side] = end[kept + 48 : kept + 64, :]
        wide[stop:, :half] = end[kept : kept + 16, :]
        wide[stop:, half:side] = end[kept + 32 : kept + 48, :]
        k = lax.broadcasted_iota(jnp.int32, (32, BLK), 0)
        lanes = lax.broadcasted_iota(jnp.int32, (32, BLK), 1)
        pick = (lanes == jnp.where(k < 16, k, k + BLK - 32)).astype(BF16)

        def turned(rows):
            return lax.dot_general(
                rows, pick, (LEFT_T, ((), ())), preferred_element_type=F32
            ).astype(BF16)

        base = kept + 64
        own = jnp.concatenate([turned(end[base : base + 32, :]), turned(end[base + 32 : base + 64, :])], axis=0)
        above, below = (
            turned(jnp.concatenate([part[BLK:, :BLK], part[BLK:, BLK : 2 * BLK]], axis=0))
            for part in (side_up, side_down)
        )
        fill(side, BLK, own[ROW0 : side - ROW0], above, below)
        wide[:16, side:] = own[ROW0 - 16 : ROW0]
        wide[stop:, side:] = own[side - ROW0 : side - ROW0 + 16]
        cut = side + BLK - 16
        full[...] = jnp.concatenate([wide[:, cut:], wide[:, :cut]], axis=1)
        for bj in range(nb):
            got = lax.dot_general(
                full[:, bj * BLK : (bj + 2) * BLK], band[...], (((1,), (1,)), ((), ())),
                preferred_element_type=F32,
            ).astype(BF16)
            for p in range(nu):
                passed[p, :, bj * BLK : (bj + 1) * BLK] = got[:, p * BLK : (p + 1) * BLK]
        for bi in range(nb):
            for bj in range(nb):
                cols = slice(bj * BLK, (bj + 1) * BLK)
                window = jnp.concatenate(
                    [passed[p, bi * BLK : bi * BLK + 160, cols] for p in range(nu)], axis=0
                )
                total = jnp.dot(kernels[bi * nb + bj], window, preferred_element_type=F32)
                rows = slice(bi * BLK, (bi + 1) * BLK)
                result[rows, cols] = frame[rows, cols] - total
            sends[bi].start()

    for send in sends:
        send.wait()


def call(kernel, name, out_shape, in_specs, scratch=(), flops=0, limit=40 << 20):
    many = isinstance(out_shape, tuple)
    return pl.pallas_call(
        kernel,
        out_shape=out_shape,
        in_specs=in_specs,
        out_specs=(VM,) * len(out_shape) if many else VM,
        scratch_shapes=list(scratch),
        compiler_params=pltpu.CompilerParams(vmem_limit_bytes=limit),
        cost_estimate=pl.CostEstimate(flops=flops, bytes_accessed=flops // 500, transcendentals=0),
        name=name,
    )


def local(
    frames, row_shift, row_frac, col_shift, col_frac,
    profile_cols, profile_rows, coef_table, weight_ids,
):
    frame = frames[0]
    side = frame.shape[0]
    nb = side // BLK
    nu, nv = profile_cols.shape[0], profile_rows.shape[0]
    nx, ny = lax.axis_size("skyx"), lax.axis_size("skyy")
    sets = coef_table.shape[0]
    row_frac = row_frac.reshape(nb, BLK)
    col_frac = col_frac.reshape(nb, BLK)

    width = nu * 160
    kept = side - 2 * ROW0
    inner = side - 2 * BLK
    cells = nb * nb
    shape = jax.ShapeDtypeStruct
    slab = shape((side + 8, BLK), F32)
    total = 4 * nb + sets + nv + nu + nb
    total += -total % 8
    meta_shape = pltpu.VMEM((total, BLK), F32)
    meta, row_meta, to_right, to_left = pl.pallas_call(
        functools.partial(gather_kernel, nb),
        out_shape=(shape((SPARE, BLK), F32), shape((2 * nb, BLK), F32), slab, slab),
        in_specs=[ANY] * 9,
        out_specs=(ANY,) * 4,
        scratch_shapes=[
            meta_shape, pltpu.VMEM((2, side + 8, BLK), F32),
            pltpu.VMEM(coef_table.shape, F32), pltpu.VMEM(profile_rows.shape, BF16),
            pltpu.VMEM(profile_cols.shape, BF16), pltpu.VMEM(weight_ids.shape, jnp.int32),
            pltpu.SMEM((nb,), jnp.int32), pltpu.SMEM((nb,), jnp.int32),
            pltpu.SemaphoreType.DMA((8,)), pltpu.SemaphoreType.DMA((6,)),
        ],
        compiler_params=pltpu.CompilerParams(vmem_limit_bytes=FULL),
        name="gather",
    )(frame, row_frac, col_frac, row_shift, col_shift, coef_table, profile_rows, profile_cols, weight_ids)
    meta_up = moved(row_meta, (-1, 1, 0), (1,))
    meta_down = moved(row_meta, (-1, -1, 0), (1,))
    left = moved(to_right, (0, 0, 1), (0,))
    right = moved(to_left, (0, 0, -1), (0,))
    mark = call(
        marker_kernel, "marker", shape((8, BLK), F32), [ANY], flops=1 << 31,
    )(meta)
    own_mid, mid, *parts = call(
        functools.partial(center_kernel, nb), "center",
        (shape((side, inner), BF16), shape((kept, inner), BF16))
        + (shape((side, 2 * BLK), BF16),) * 2
        + (shape((side, inner), BF16),) * 2
        + (shape((side, side), BF16),) * 2
        + (shape((4 * BLK, BLK), BF16),) * 2,
        [VM, ANY, ANY],
        [
            meta_shape, pltpu.VMEM((side, side), BF16), pltpu.VMEM((side, side), BF16),
            pltpu.SemaphoreType.DMA(()),
        ],
        flops=1 << 33,
    )(frame, meta, mark)
    mid = moved(mid, (1, 0, 0), (0,))
    own_end, end, to_up, to_down = call(
        functools.partial(edge_kernel, nb, nx, ny), "edges",
        (shape((side, 2 * BLK), BF16), shape((kept + 128, side // 2), BF16))
        + (shape((BLK + 16, side), BF16),) * 2,
        [VM] * 12,
        [pltpu.VMEM((side, 3 * BLK), BF16)] * 2,
        flops=1 << 33,
    )(left, right, meta_up, meta_down, *parts)
    end = moved(end, (1, 0, 0), (0,))
    side_down = moved(to_up, (1, -1, 0), (0,))
    side_up = moved(to_down, (1, 1, 0), (0,))
    to_up, to_down = call(
        relay_kernel, "relay", (shape((BLK, side), BF16),) * 2, [VM] * 3
    )(to_up, to_down, own_end)
    got_down = moved(to_up, (0, -1, 0), (0,))
    got_up = moved(to_down, (0, 1, 0), (0,))
    kernels, band = call(
        functools.partial(matrices_kernel, nb, nu, nv, sets), "matrices",
        (shape((cells, BLK, width), BF16), shape((nu * BLK, 2 * BLK), BF16)),
        [ANY, VM],
        [pltpu.VMEM((8, width), F32), meta_shape, pltpu.SemaphoreType.DMA(())],
        flops=0,
    )(meta, own_end)
    result = pl.pallas_call(
        functools.partial(finish_kernel, nb, nu),
        out_shape=shape((side, side), F32),
        in_specs=[VM] * 11,
        out_specs=ANY,
        scratch_shapes=[
            pltpu.VMEM((side, side), F32), pltpu.VMEM((side + 32, side + BLK), BF16),
            pltpu.VMEM((side + 32, side + BLK), BF16), pltpu.VMEM((nu, side + 32, side), BF16),
            pltpu.SemaphoreType.DMA((nb,)),
        ],
        compiler_params=pltpu.CompilerParams(vmem_limit_bytes=40 << 20),
        name="finish",
    )(frame, own_mid, own_end, side_up, side_down, mid, end, kernels, band, got_up, got_down)
    return result[None]


def solution(mesh):
    placed = (
        P("segment", "skyx", "skyy"), P("skyx"), P("skyx"), P("skyy"), P("skyy"),
        P(), P(), P(), P("skyx", "skyy"),
    )
    return jax.shard_map(
        local, mesh=mesh, in_specs=placed, out_specs=P("segment", "skyx", "skyy"), check_vma=False
    )
```

```python
import functools
import math

import jax
import jax.numpy as jnp
from jax import lax
from jax.experimental import pallas as pl
from jax.experimental.pallas import tpu as pltpu
from jax.sharding import PartitionSpec as P

BLK = 128
KW = 31
HALF = 15
ROW0 = 56
F32 = jnp.float32
BF16 = jnp.bfloat16
HIGHEST = lax.Precision.HIGHEST
VM = pl.BlockSpec(memory_space=pltpu.VMEM)
ANY = pl.BlockSpec(memory_space=pl.ANY)
FULL = 64 << 20
SPARE = 1 << 15


def moved(block, step, sources):
    axes = ("segment", "skyx", "skyy")
    counts = [lax.axis_size(axis) for axis in axes]
    route = []
    for s in range(counts[0]):
        for i in range(counts[1]):
            for j in range(counts[2]):
                to = (s + step[0], i + step[1], j + step[2])
                if s in sources and all(0 <= to[k] < counts[k] for k in range(3)):
                    flat = [(a * counts[1] + b) * counts[2] + c for a, b, c in ((s, i, j), to)]
                    route.append(tuple(flat))
    return lax.ppermute(block, axes, route)


def sinc(values):
    angle = math.pi * values
    zero = values == 0.0
    return jnp.where(zero, 1.0, jnp.sin(angle) / jnp.where(zero, 1.0, angle))


def taps(fracs):
    count = len(fracs)
    spread = jnp.concatenate([jnp.broadcast_to(frac, (8, BLK)) for frac in fracs], axis=0)
    lag = (lax.broadcasted_iota(jnp.int32, (8 * count, BLK), 0) & 7) - 2
    values = lag.astype(F32) - spread
    weight = jnp.where(jnp.abs(values) < 3.0, sinc(values) * sinc(values / 3.0), 0.0)
    return [weight[8 * n : 8 * n + 8] for n in range(count)]


def split(values):
    high = values.astype(BF16)
    return high, (values - high.astype(F32)).astype(BF16)


def banded(weight, shift, depth, offset):
    lag = (
        lax.broadcasted_iota(jnp.int32, (depth, BLK), 0)
        - lax.broadcasted_iota(jnp.int32, (depth, BLK), 1)
        + (offset - shift)
    )
    total = jnp.zeros((depth, BLK), F32)
    for tap in range(6):
        total = jnp.where(lag == tap - 2, weight[tap : tap + 1], total)
    return total


def dot3(left, right, dims):
    lh, ll = left
    rh, rl = right
    dot = functools.partial(
        lax.dot_general, dimension_numbers=(dims, ((), ())), preferred_element_type=F32
    )
    return dot(lh, rh) + dot(lh, rl) + dot(ll, rh)


MATMUL = ((1,), (0,))
LEFT_T = ((0,), (0,))


def packed3(left, right):
    lh, ll = left
    rh, rl = right
    width = rh.shape[1]
    dot = functools.partial(jnp.dot, preferred_element_type=F32)
    both = dot(lh, jnp.concatenate([rh, rl], axis=1))
    return both[:, :width] + both[:, width:] + dot(ll, rh)


def gather_kernel(
    nb, frame, row_frac, col_frac, row_shift, col_shift, table, prof_rows, prof_cols, ids,
    meta_out, row_meta, to_right, to_left,
    meta, marks, table_v, rows_v, cols_v, ids_v, row_s, col_s, sems, done,
):
    side = nb * BLK
    warper = lax.axis_index("segment") == 0
    copies = [
        pltpu.make_async_copy(src, dst, sems.at[n])
        for n, (src, dst) in enumerate((
            (row_frac, meta.at[0:nb, :]),
            (col_frac, meta.at[2 * nb : 3 * nb, :]),
            (row_shift, row_s),
            (col_shift, col_s),
            (table, table_v),
            (prof_rows, rows_v),
            (prof_cols, cols_v),
            (ids, ids_v),
        ))
    ]
    slabs = [
        pltpu.make_async_copy(frame.at[:, side - BLK :], marks.at[0, :side, :], done.at[0]),
        pltpu.make_async_copy(frame.at[:, :BLK], marks.at[1, :side, :], done.at[1]),
    ]
    sends = [
        pltpu.make_async_copy(marks.at[0], to_right, done.at[2]),
        pltpu.make_async_copy(marks.at[1], to_left, done.at[3]),
    ]
    summary = pltpu.make_async_copy(meta, meta_out.at[: meta.shape[0], :], done.at[4])
    rows = pltpu.make_async_copy(meta.at[: 2 * nb, :], row_meta, done.at[5])

    @pl.when(warper)
    def _():
        for copy in slabs:
            copy.start()

    for copy in copies:
        copy.start()
    for copy in copies:
        copy.wait()
    for b in range(nb):
        meta[nb + b : nb + b + 1, :] = jnp.full((1, BLK), row_s[b].astype(F32))
        meta[3 * nb + b : 3 * nb + b + 1, :] = jnp.full((1, BLK), col_s[b].astype(F32))
    base = 4 * nb
    for part in (table_v, rows_v, cols_v, ids_v):
        meta[base : base + part.shape[0], : part.shape[1]] = part[...].astype(F32)
        base += part.shape[0]
    for n, b in ((0, nb - 1), (1, 0)):
        marks[n, side : side + 1, :] = meta[2 * nb + b : 2 * nb + b + 1, :]
        marks[n, side + 1 : side + 2, :] = meta[3 * nb + b : 3 * nb + b + 1, :]
    summary.start()
    rows.start()

    @pl.when(warper)
    def _():
        for copy, send in zip(slabs, sends):
            copy.wait()
            send.start()
        for send in sends:
            send.wait()

    summary.wait()
    rows.wait()


def marker_kernel(meta_in, mark):
    mark[...] = jnp.zeros_like(mark)


def center_kernel(
    nb, frame, meta_in, mark,
    own, across, tip_hi, tip_lo, mid_hi, mid_lo, row_hi, row_lo, edge_hi, edge_lo,
    meta, src_hi, src_lo, sem,
):
    side = nb * BLK

    @pl.when(lax.axis_index("segment") == 0)
    def _():
        small = pltpu.make_async_copy(meta_in.at[: meta.shape[0], :], meta, sem)
        small.start()
        for b in range(nb):
            rows = slice(b * BLK, (b + 1) * BLK)
            hi, lo = split(frame[rows, :])
            for whole, tip, part in ((src_hi, tip_hi, hi), (src_lo, tip_lo, lo)):
                whole[rows, :] = part
                tip[rows, :BLK] = part[:, :BLK]
                tip[rows, BLK:] = part[:, side - BLK :]
        small.wait()
        fracs = [meta[2 * nb + b : 2 * nb + b + 1, :] for b in range(nb)]
        weights = taps(fracs + [meta[b : b + 1, :] for b in range(nb)])
        col_shift = [meta[3 * nb + b : 3 * nb + b + 1, :].astype(jnp.int32) for b in range(nb)]
        row_shift = [meta[nb + b : nb + b + 1, :].astype(jnp.int32) for b in range(nb)]
        for b in range(1, nb - 1):
            mat = split(banded(weights[b], col_shift[b], 3 * BLK, -BLK))
            cols = slice((b - 1) * BLK, (b + 2) * BLK)
            hi, lo = split(packed3((src_hi[:, cols], src_lo[:, cols]), mat))
            mid_hi[:, (b - 1) * BLK : b * BLK] = hi
            mid_lo[:, (b - 1) * BLK : b * BLK] = lo
        for b in range(nb):
            first, depth = (b, BLK) if b in (0, nb - 1) else (b - 1, 3 * BLK)
            mat = split(banded(weights[nb + b], row_shift[b], depth, (first - b) * BLK).T)
            rows, cols = slice(b * BLK, (b + 1) * BLK), slice(first * BLK, first * BLK + depth)
            row_hi[rows, cols], row_lo[rows, cols] = mat
            got = dot3(mat, (mid_hi[cols, :], mid_lo[cols, :]), MATMUL)
            own[rows, :] = got.astype(BF16)
            low = max(b * BLK, ROW0)
            high = min((b + 1) * BLK, side - ROW0)
            across[low - ROW0 : high - ROW0, :] = got[low - b * BLK : high - b * BLK, :].astype(BF16)
        for n, (b, offset) in enumerate(((0, -BLK), (nb - 1, 0))):
            hi, lo = split(banded(weights[b], col_shift[b], 2 * BLK, offset))
            edge_hi[n * 2 * BLK : (n + 1) * 2 * BLK, :] = hi
            edge_lo[n * 2 * BLK : (n + 1) * 2 * BLK, :] = lo


def matrices_kernel(nb, nu, nv, sets, meta_in, after, kernels, band, padded, meta, sem):
    @pl.when(lax.axis_index("segment") != 0)
    def _():
        small = pltpu.make_async_copy(meta_in.at[: meta.shape[0], :], meta, sem)
        small.start()
        small.wait()
        base = 4 * nb
        table = meta[base : base + sets, : nu * nv]
        base += sets
        prof_rows = meta[base : base + nv, :KW]
        base += nv
        prof_cols = meta[base : base + nu, :KW]
        base += nu
        entry = lax.broadcasted_iota(jnp.int32, (1, sets), 1)
        cells = []
        for bi in range(nb):
            for bj in range(nb):
                chosen = jnp.broadcast_to(meta[base + bi : base + bi + 1, bj : bj + 1], (1, sets))
                cells.append((chosen.astype(jnp.int32) == entry).astype(F32))
        coefs = jnp.dot(
            jnp.concatenate(cells, axis=0), table, precision=HIGHEST, preferred_element_type=F32
        )
        width = nu * 160
        padded[...] = jnp.zeros_like(padded)
        padded[0:nv, 0:KW] = prof_rows
        profile = padded[0:nv, :]
        spread = jnp.concatenate(
            [pltpu.roll(profile, p * 160 + 1, 1) for p in range(nu)], axis=0
        )
        base = jnp.dot(coefs, spread, precision=HIGHEST, preferred_element_type=F32)
        for cell in range(nb * nb):
            row = jnp.broadcast_to(base[cell : cell + 1, :], (BLK, width))
            kernels[cell] = pltpu.roll(row, 0, 1, stride=1, stride_axis=0).astype(BF16)
        padded[...] = jnp.zeros_like(padded)
        padded[0:nu, 0:KW] = prof_cols
        for p in range(nu):
            row = jnp.broadcast_to(padded[p : p + 1, : 2 * BLK], (BLK, 2 * BLK))
            turned = pltpu.roll(row, 1, 1, stride=1, stride_axis=0).T
            band[:, p * BLK : (p + 1) * BLK] = turned.astype(BF16)


def edge_kernel(
    nb, nx, ny,
    left, right, meta_up, meta_down, tip_hi, tip_lo, mid_hi, mid_lo, row_hi, row_lo, edge_hi, edge_lo,
    own, across, side_up, side_down,
    end_hi, end_lo,
):
    side = nb * BLK
    kept = side - 2 * ROW0
    half = side // 2
    i = lax.axis_index("skyx")
    j = lax.axis_index("skyy")

    @pl.when(lax.axis_index("segment") == 0)
    def _():
        lanes = lax.broadcasted_iota(jnp.int32, (8, BLK), 1)
        weights = taps([left[side : side + 1, :], right[side : side + 1, :], meta_up[nb - 1 : nb, :], meta_down[0:1, :]])
        shifts = [
            part[row : row + 1, :].astype(jnp.int32)
            for part, row in ((left, side + 1), (right, side + 1), (meta_up, 2 * nb - 1), (meta_down, nb))
        ]
        parts = [split(left[:side, :]), split(right[:side, :])]
        for n in range(2):
            source = []
            for part, tip in zip(parts[n], (tip_hi, tip_lo)):
                inner = tip[:, n * BLK : (n + 1) * BLK]
                source.append(jnp.concatenate([part, inner] if n == 0 else [inner, part], axis=1))
            mat = tuple(edge[n * 2 * BLK : (n + 1) * 2 * BLK, :] for edge in (edge_hi, edge_lo))
            hi, lo = split(packed3(source, mat))
            end_hi[:, n * BLK : (n + 1) * BLK] = hi
            end_lo[:, n * BLK : (n + 1) * BLK] = lo
        low_ok = jnp.logical_and(lanes >= BLK - HALF, j > 0)
        high_ok = jnp.logical_and(lanes < HALF, j < ny - 1)
        low = split(banded(jnp.where(low_ok, weights[0], 0.0), shifts[0], BLK, BLK))
        high = split(banded(jnp.where(high_ok, weights[1], 0.0), shifts[1], BLK, -BLK))
        mat = [jnp.concatenate(pair, axis=0) for pair in zip(low, high)]
        hi, lo = split(packed3((tip_hi[...], tip_lo[...]), mat))
        end_hi[:, 2 * BLK :] = hi
        end_lo[:, 2 * BLK :] = lo
        outer = []
        for n, b in ((0, 0), (1, nb - 1)):
            there = (i > 0) if n == 0 else (i < nx - 1)
            weight = jnp.where(there, weights[2 + n], 0.0)
            mat = split(banded(weight, shifts[2 + n], BLK, BLK if n == 0 else -BLK).T)
            rows = slice(b * BLK, (b + 1) * BLK)
            source = [
                jnp.concatenate([mid[rows, :], end[rows, :]], axis=1)
                for mid, end in ((mid_hi, end_hi), (mid_lo, end_lo))
            ]
            got = dot3(mat, source, MATMUL)
            outer.append(got)
            out = side_up if n == 0 else side_down
            inner = side - 2 * BLK
            out[:BLK, BLK : side - BLK] = got[:, :inner].astype(BF16)
            out[:BLK, :BLK] = got[:, inner : inner + BLK].astype(BF16)
            out[:BLK, side - BLK :] = got[:, inner + BLK : side].astype(BF16)
            turned = got[:, side:].T
            for k, row in enumerate((0, 8, BLK - 16, BLK - 8)):
                out[BLK:, k * BLK : (k + 1) * BLK] = turned[row : row + 8].astype(BF16)
        across[kept : kept + 16, :] = side_down[:16, :half]
        across[kept + 16 : kept + 32, :] = side_up[BLK - 16 : BLK, :half]
        across[kept + 32 : kept + 48, :] = side_down[:16, half:]
        across[kept + 48 : kept + 64, :] = side_up[BLK - 16 : BLK, half:]
        strips = []
        for b in range(nb):
            first, depth = (b, BLK) if b in (0, nb - 1) else (b - 1, 3 * BLK)
            rows, cols = slice(b * BLK, (b + 1) * BLK), slice(first * BLK, first * BLK + depth)
            mat = (row_hi[rows, cols], row_lo[rows, cols])
            got = dot3(mat, (end_hi[cols, : 2 * BLK], end_lo[cols, : 2 * BLK]), MATMUL)
            own[rows, :] = got.astype(BF16)
            low = max(b * BLK, ROW0)
            high = min((b + 1) * BLK, side - ROW0)
            across[low - ROW0 : high - ROW0, :] = got[low - b * BLK : high - b * BLK, :].astype(BF16)
            strips.append(packed3(mat, (end_hi[cols, 2 * BLK :], end_lo[cols, 2 * BLK :])))
        strip = jnp.concatenate(strips, axis=0)
        strip = jnp.concatenate(
            [
                strip[: ROW0 - 16], outer[0][BLK - 16 :, side:], strip[ROW0 : side - ROW0],
                outer[1][:16, side:], strip[side - ROW0 + 16 :],
            ],
            axis=0,
        ).T
        for n in range(2):
            base = kept + 64 + 32 * n
            cols = slice(n * half, (n + 1) * half)
            across[base : base + 16, :] = strip[:16, cols].astype(BF16)
            across[base + 16 : base + 32, :] = strip[BLK - 16 :, cols].astype(BF16)


def relay_kernel(up_in, down_in, end_in, up, down):
    @pl.when(lax.axis_index("segment") == 0)
    def _():
        up[...] = up_in[:BLK, :]
        down[...] = down_in[:BLK, :]


def finish_kernel(
    nb, nu,
    frame, own_mid, own_end, side_up, side_down, mid, end, kernels, band, got_up, got_down,
    out, result, wide, full, passed, sems,
):
    side = nb * BLK
    half = side // 2
    warper = lax.axis_index("segment") == 0
    last = side - BLK
    sends = []
    for b in range(nb):
        rows = pl.ds(b * BLK, BLK)
        sends.append(pltpu.make_async_copy(result.at[rows, :], out.at[rows, :], sems.at[b]))

    @pl.when(warper)
    def _():
        for b in range(nb):
            rows = slice(b * BLK, (b + 1) * BLK)
            pieces = ((0, own_end[rows, :BLK]), (BLK, own_mid[rows, :]), (last, own_end[rows, BLK:]))
            for lane, piece in pieces:
                cols = slice(lane, lane + piece.shape[1])
                total = piece.astype(F32)
                if b == 0:
                    total = (total + got_up[:BLK, cols].astype(F32)).astype(BF16).astype(F32)
                if b == nb - 1:
                    total = (total + got_down[:BLK, cols].astype(F32)).astype(BF16).astype(F32)
                result[rows, cols] = total
            sends[b].start()

    @pl.when(jnp.logical_not(warper))
    def _():
        kept = side - 2 * ROW0
        both = BLK - ROW0
        stop = 16 + side

        def fill(at, width, own, above, below):
            cols = slice(at, at + width)
            own = own.astype(F32)
            above, below = above.astype(F32), below.astype(F32)
            top = jnp.concatenate([above[:ROW0], own[:both] + above[ROW0:]], axis=0)
            bottom = jnp.concatenate([own[kept - both :] + below[:both], below[both:]], axis=0)
            wide[16 : 16 + BLK, cols] = top.astype(BF16)
            wide[16 + BLK : 16 + last, cols] = own[both : kept - both].astype(BF16)
            wide[16 + last : stop, cols] = bottom.astype(BF16)

        fill(BLK, side - 2 * BLK, mid[:kept, :], side_up[:BLK, BLK:last], side_down[:BLK, BLK:last])
        fill(0, BLK, end[:kept, :BLK], side_up[:BLK, :BLK], side_down[:BLK, :BLK])
        fill(last, BLK, end[:kept, BLK:], side_up[:BLK, last:], side_down[:BLK, last:])
        wide[:16, :half] = end[kept + 16 : kept + 32, :]
        wide[:16, half:side] = end[kept + 48 : kept + 64, :]
        wide[stop:, :half] = end[kept : kept + 16, :]
        wide[stop:, half:side] = end[kept + 32 : kept + 48, :]
        k = lax.broadcasted_iota(jnp.int32, (32, BLK), 0)
        lanes = lax.broadcasted_iota(jnp.int32, (32, BLK), 1)
        pick = (lanes == jnp.where(k < 16, k, k + BLK - 32)).astype(BF16)

        def turned(rows):
            return lax.dot_general(
                rows, pick, (LEFT_T, ((), ())), preferred_element_type=F32
            ).astype(BF16)

        base = kept + 64
        own = jnp.concatenate(
            [turned(end[base : base + 32, :]), turned(end[base + 32 : base + 64, :])], axis=0
        ).astype(F32)
        above, below = (
            turned(
                jnp.concatenate(
                    [part[BLK:, k * BLK : (k + 1) * BLK].astype(F32) for k in range(4)], axis=0
                ).astype(BF16)
            )
            for part in (side_up, side_down)
        )
        fill(side, BLK, own[ROW0 : side - ROW0], above, below)
        wide[:16, side:] = own[ROW0 - 16 : ROW0].astype(BF16)
        wide[stop:, side:] = own[side - ROW0 : side - ROW0 + 16].astype(BF16)
        cut = side + BLK - 16
        full[...] = jnp.concatenate([wide[:, cut:], wide[:, :cut]], axis=1)
        for bj in range(nb):
            got = jnp.dot(
                full[:, bj * BLK : (bj + 2) * BLK], band[...], preferred_element_type=F32
            ).astype(BF16)
            for p in range(nu):
                passed[p, :, bj * BLK : (bj + 1) * BLK] = got[:, p * BLK : (p + 1) * BLK]
        for bi in range(nb):
            for bj in range(nb):
                cols = slice(bj * BLK, (bj + 1) * BLK)
                window = jnp.concatenate(
                    [passed[p, bi * BLK : bi * BLK + 160, cols] for p in range(nu)], axis=0
                )
                total = jnp.dot(kernels[bi * nb + bj], window, preferred_element_type=F32)
                rows = slice(bi * BLK, (bi + 1) * BLK)
                result[rows, cols] = frame[rows, cols] - total
            sends[bi].start()

    for send in sends:
        send.wait()


def call(kernel, name, out_shape, in_specs, scratch=(), flops=0, limit=40 << 20):
    many = isinstance(out_shape, tuple)
    return pl.pallas_call(
        kernel,
        out_shape=out_shape,
        in_specs=in_specs,
        out_specs=(VM,) * len(out_shape) if many else VM,
        scratch_shapes=list(scratch),
        compiler_params=pltpu.CompilerParams(vmem_limit_bytes=limit),
        cost_estimate=pl.CostEstimate(flops=flops, bytes_accessed=flops // 500, transcendentals=0),
        name=name,
    )


def local(
    frames, row_shift, row_frac, col_shift, col_frac,
    profile_cols, profile_rows, coef_table, weight_ids,
):
    frame = frames[0]
    side = frame.shape[0]
    nb = side // BLK
    nu, nv = profile_cols.shape[0], profile_rows.shape[0]
    nx, ny = lax.axis_size("skyx"), lax.axis_size("skyy")
    sets = coef_table.shape[0]
    row_frac = row_frac.reshape(nb, BLK)
    col_frac = col_frac.reshape(nb, BLK)

    width = nu * 160
    kept = side - 2 * ROW0
    inner = side - 2 * BLK
    cells = nb * nb
    shape = jax.ShapeDtypeStruct
    slab = shape((side + 8, BLK), F32)
    total = 4 * nb + sets + nv + nu + nb
    total += -total % 8
    meta_shape = pltpu.VMEM((total, BLK), F32)
    meta, row_meta, to_right, to_left = pl.pallas_call(
        functools.partial(gather_kernel, nb),
        out_shape=(shape((SPARE, BLK), F32), shape((2 * nb, BLK), F32), slab, slab),
        in_specs=[ANY] * 9,
        out_specs=(ANY,) * 4,
        scratch_shapes=[
            meta_shape, pltpu.VMEM((2, side + 8, BLK), F32),
            pltpu.VMEM(coef_table.shape, F32), pltpu.VMEM(profile_rows.shape, BF16),
            pltpu.VMEM(profile_cols.shape, BF16), pltpu.VMEM(weight_ids.shape, jnp.int32),
            pltpu.SMEM((nb,), jnp.int32), pltpu.SMEM((nb,), jnp.int32),
            pltpu.SemaphoreType.DMA((8,)), pltpu.SemaphoreType.DMA((6,)),
        ],
        compiler_params=pltpu.CompilerParams(vmem_limit_bytes=FULL),
        name="gather",
    )(frame, row_frac, col_frac, row_shift, col_shift, coef_table, profile_rows, profile_cols, weight_ids)
    meta_up = moved(row_meta, (-1, 1, 0), (1,))
    meta_down = moved(row_meta, (-1, -1, 0), (1,))
    left = moved(to_right, (0, 0, 1), (0,))
    right = moved(to_left, (0, 0, -1), (0,))
    mark = call(
        marker_kernel, "marker", shape((8, BLK), F32), [ANY], flops=1 << 31,
    )(meta)
    own_mid, mid, *parts = call(
        functools.partial(center_kernel, nb), "center",
        (shape((side, inner), BF16), shape((kept, inner), BF16))
        + (shape((side, 2 * BLK), BF16),) * 2
        + (shape((side, inner), BF16),) * 2
        + (shape((side, side), BF16),) * 2
        + (shape((4 * BLK, BLK), BF16),) * 2,
        [VM, ANY, ANY],
        [
            meta_shape, pltpu.VMEM((side, side), BF16), pltpu.VMEM((side, side), BF16),
            pltpu.SemaphoreType.DMA(()),
        ],
        flops=1 << 33,
    )(frame, meta, mark)
    mid = moved(mid, (1, 0, 0), (0,))
    own_end, end, to_up, to_down = call(
        functools.partial(edge_kernel, nb, nx, ny), "edges",
        (shape((side, 2 * BLK), BF16), shape((kept + 128, side // 2), BF16))
        + (shape((BLK + 8, side), BF16),) * 2,
        [VM] * 12,
        [pltpu.VMEM((side, 3 * BLK), BF16)] * 2,
        flops=1 << 33,
    )(left, right, meta_up, meta_down, *parts)
    end = moved(end, (1, 0, 0), (0,))
    side_down = moved(to_up, (1, -1, 0), (0,))
    side_up = moved(to_down, (1, 1, 0), (0,))
    to_up, to_down = call(
        relay_kernel, "relay", (shape((BLK, side), BF16),) * 2, [VM] * 3
    )(to_up, to_down, own_end)
    got_down = moved(to_up, (0, -1, 0), (0,))
    got_up = moved(to_down, (0, 1, 0), (0,))
    kernels, band = call(
        functools.partial(matrices_kernel, nb, nu, nv, sets), "matrices",
        (shape((cells, BLK, width), BF16), shape((2 * BLK, nu * BLK), BF16)),
        [ANY, VM],
        [pltpu.VMEM((8, width), F32), meta_shape, pltpu.SemaphoreType.DMA(())],
        flops=0,
    )(meta, own_end)
    result = pl.pallas_call(
        functools.partial(finish_kernel, nb, nu),
        out_shape=shape((side, side), F32),
        in_specs=[VM] * 11,
        out_specs=ANY,
        scratch_shapes=[
            pltpu.VMEM((side, side), F32), pltpu.VMEM((side + 32, side + BLK), BF16),
            pltpu.VMEM((side + 32, side + BLK), BF16), pltpu.VMEM((nu, side + 32, side), BF16),
            pltpu.SemaphoreType.DMA((nb,)),
        ],
        compiler_params=pltpu.CompilerParams(vmem_limit_bytes=40 << 20),
        name="finish",
    )(frame, own_mid, own_end, side_up, side_down, mid, end, kernels, band, got_up, got_down)
    return result[None]


def solution(mesh):
    placed = (
        P("segment", "skyx", "skyy"), P("skyx"), P("skyx"), P("skyy"), P("skyy"),
        P(), P(), P(), P("skyx", "skyy"),
    )
    return jax.shard_map(
        local, mesh=mesh, in_specs=placed, out_specs=P("segment", "skyx", "skyy"), check_vma=False
    )
```

```python
import functools
import math

import jax
import jax.numpy as jnp
from jax import lax
from jax.experimental import pallas as pl
from jax.experimental.pallas import tpu as pltpu
from jax.sharding import PartitionSpec as P

BLK = 128
KW = 31
HALF = 15
ROW0 = 56
F32 = jnp.float32
BF16 = jnp.bfloat16
HIGHEST = lax.Precision.HIGHEST
VM = pl.BlockSpec(memory_space=pltpu.VMEM)
ANY = pl.BlockSpec(memory_space=pl.ANY)
FULL = 64 << 20
SPARE = 1 << 15


def moved(block, step, sources):
    axes = ("segment", "skyx", "skyy")
    counts = [lax.axis_size(axis) for axis in axes]
    route = []
    for s in range(counts[0]):
        for i in range(counts[1]):
            for j in range(counts[2]):
                to = (s + step[0], i + step[1], j + step[2])
                if s in sources and all(0 <= to[k] < counts[k] for k in range(3)):
                    flat = [(a * counts[1] + b) * counts[2] + c for a, b, c in ((s, i, j), to)]
                    route.append(tuple(flat))
    return lax.ppermute(block, axes, route)


def sinc(values):
    angle = math.pi * values
    zero = values == 0.0
    return jnp.where(zero, 1.0, jnp.sin(angle) / jnp.where(zero, 1.0, angle))


def taps(fracs):
    count = len(fracs)
    spread = jnp.concatenate([jnp.broadcast_to(frac, (8, BLK)) for frac in fracs], axis=0)
    lag = (lax.broadcasted_iota(jnp.int32, (8 * count, BLK), 0) & 7) - 2
    values = lag.astype(F32) - spread
    weight = jnp.where(jnp.abs(values) < 3.0, sinc(values) * sinc(values / 3.0), 0.0)
    return [weight[8 * n : 8 * n + 8] for n in range(count)]


def split(values):
    high = values.astype(BF16)
    return high, (values - high.astype(F32)).astype(BF16)


def banded(weight, shift, depth, offset):
    lag = (
        lax.broadcasted_iota(jnp.int32, (depth, BLK), 0)
        - lax.broadcasted_iota(jnp.int32, (depth, BLK), 1)
        + (offset - shift)
    )
    total = jnp.zeros((depth, BLK), F32)
    for tap in range(6):
        total = jnp.where(lag == tap - 2, weight[tap : tap + 1], total)
    return total


def dot3(left, right, dims):
    lh, ll = left
    rh, rl = right
    dot = functools.partial(
        lax.dot_general, dimension_numbers=(dims, ((), ())), preferred_element_type=F32
    )
    return dot(lh, rh) + dot(lh, rl) + dot(ll, rh)


MATMUL = ((1,), (0,))
LEFT_T = ((0,), (0,))


def packed3(left, right):
    lh, ll = left
    rh, rl = right
    width = rh.shape[1]
    dot = functools.partial(jnp.dot, preferred_element_type=F32)
    both = dot(lh, jnp.concatenate([rh, rl], axis=1))
    return both[:, :width] + both[:, width:] + dot(ll, rh)


def gather_kernel(
    nb, frame, row_frac, col_frac, row_shift, col_shift, table, prof_rows, prof_cols, ids,
    meta_out, token, row_meta, to_right, to_left,
    meta, marks, table_v, rows_v, cols_v, ids_v, row_s, col_s, sems, done,
):
    side = nb * BLK
    warper = lax.axis_index("segment") == 0
    copies = [
        pltpu.make_async_copy(src, dst, sems.at[n])
        for n, (src, dst) in enumerate((
            (row_frac, meta.at[0:nb, :]),
            (col_frac, meta.at[2 * nb : 3 * nb, :]),
            (row_shift, row_s),
            (col_shift, col_s),
            (table, table_v),
            (prof_rows, rows_v),
            (prof_cols, cols_v),
            (ids, ids_v),
        ))
    ]
    slabs = [
        pltpu.make_async_copy(frame.at[:, side - BLK :], marks.at[0, :side, :], done.at[0]),
        pltpu.make_async_copy(frame.at[:, :BLK], marks.at[1, :side, :], done.at[1]),
    ]
    sends = [
        pltpu.make_async_copy(marks.at[0], to_right, done.at[2]),
        pltpu.make_async_copy(marks.at[1], to_left, done.at[3]),
    ]
    summary = pltpu.make_async_copy(meta, meta_out, done.at[4])
    rows = pltpu.make_async_copy(meta.at[: 2 * nb, :], row_meta, done.at[5])

    @pl.when(warper)
    def _():
        for copy in slabs:
            copy.start()

    for copy in copies:
        copy.start()
    for copy in copies:
        copy.wait()
    for b in range(nb):
        meta[nb + b : nb + b + 1, :] = jnp.full((1, BLK), row_s[b].astype(F32))
        meta[3 * nb + b : 3 * nb + b + 1, :] = jnp.full((1, BLK), col_s[b].astype(F32))
    base = 4 * nb
    for part in (table_v, rows_v, cols_v, ids_v):
        meta[base : base + part.shape[0], : part.shape[1]] = part[...].astype(F32)
        base += part.shape[0]
    for n, b in ((0, nb - 1), (1, 0)):
        marks[n, side : side + 1, :] = meta[2 * nb + b : 2 * nb + b + 1, :]
        marks[n, side + 1 : side + 2, :] = meta[3 * nb + b : 3 * nb + b + 1, :]
    summary.start()
    rows.start()

    @pl.when(warper)
    def _():
        for copy, send in zip(slabs, sends):
            copy.wait()
            send.start()
        for send in sends:
            send.wait()

    summary.wait()
    rows.wait()


def marker_kernel(meta_in, mark):
    mark[...] = jnp.zeros_like(mark)


def center_kernel(
    nb, frame, meta, mark,
    own, across, mid_hi, mid_lo, row_hi, row_lo,
    src_hi, src_lo,
):
    side = nb * BLK

    @pl.when(lax.axis_index("segment") == 0)
    def _():
        hi, lo = split(frame[...])
        src_hi[...] = hi
        src_lo[...] = lo
        fracs = [meta[2 * nb + b : 2 * nb + b + 1, :] for b in range(nb)]
        weights = taps(fracs + [meta[b : b + 1, :] for b in range(nb)])
        col_shift = [meta[3 * nb + b : 3 * nb + b + 1, :].astype(jnp.int32) for b in range(nb)]
        row_shift = [meta[nb + b : nb + b + 1, :].astype(jnp.int32) for b in range(nb)]
        for b in range(1, nb - 1):
            mat = split(banded(weights[b], col_shift[b], 3 * BLK, -BLK))
            cols = slice((b - 1) * BLK, (b + 2) * BLK)
            hi, lo = split(packed3((src_hi[:, cols], src_lo[:, cols]), mat))
            mid_hi[:, (b - 1) * BLK : b * BLK] = hi
            mid_lo[:, (b - 1) * BLK : b * BLK] = lo
        for b in range(nb):
            first, depth = (b, BLK) if b in (0, nb - 1) else (b - 1, 3 * BLK)
            mat = split(banded(weights[nb + b], row_shift[b], depth, (first - b) * BLK).T)
            rows, cols = slice(b * BLK, (b + 1) * BLK), slice(first * BLK, first * BLK + depth)
            row_hi[rows, cols], row_lo[rows, cols] = mat
            got = dot3(mat, (mid_hi[cols, :], mid_lo[cols, :]), MATMUL)
            own[rows, :] = got.astype(BF16)
            low = max(b * BLK, ROW0)
            high = min((b + 1) * BLK, side - ROW0)
            across[low - ROW0 : high - ROW0, :] = got[low - b * BLK : high - b * BLK, :].astype(BF16)


def outer_kernel(
    nb, nx, frame, meta, meta_up, meta_down, mid_hi, mid_lo, after,
    early_up, early_down, tip_hi, tip_lo, edge_hi, edge_lo, out_hi, out_lo,
):
    side = nb * BLK
    i = lax.axis_index("skyx")

    @pl.when(lax.axis_index("segment") == 0)
    def _():
        weights = taps([
            meta_up[nb - 1 : nb, :], meta_down[0:1, :],
            meta[2 * nb : 2 * nb + 1, :], meta[3 * nb - 1 : 3 * nb, :],
        ])
        shifts = [
            row.astype(jnp.int32)
            for row in (
                meta_up[2 * nb - 1 : 2 * nb, :], meta_down[nb : nb + 1, :],
                meta[3 * nb : 3 * nb + 1, :], meta[4 * nb - 1 : 4 * nb, :],
            )
        ]
        for n, b in ((0, 0), (1, nb - 1)):
            there = (i > 0) if n == 0 else (i < nx - 1)
            weight = jnp.where(there, weights[n], 0.0)
            mat = split(banded(weight, shifts[n], BLK, BLK if n == 0 else -BLK).T)
            rows = slice(b * BLK, (b + 1) * BLK)
            early = early_up if n == 0 else early_down
            early[...] = dot3(mat, (mid_hi[rows, :], mid_lo[rows, :]), MATMUL).astype(BF16)
            out_hi[n * BLK : (n + 1) * BLK, :], out_lo[n * BLK : (n + 1) * BLK, :] = mat
            mat = split(banded(weights[2 + n], shifts[2 + n], 2 * BLK, -BLK if n == 0 else 0))
            edge_hi[n * 2 * BLK : (n + 1) * 2 * BLK, :], edge_lo[n * 2 * BLK : (n + 1) * 2 * BLK, :] = mat
            cols = slice(n * BLK, (n + 1) * BLK)
            tip_hi[:, cols], tip_lo[:, cols] = split(frame[:, b * BLK : (b + 1) * BLK])


def matrices_kernel(nb, nu, nv, sets, meta, after, kernels, band, padded):
    @pl.when(lax.axis_index("segment") != 0)
    def _():
        base = 4 * nb
        table = meta[base : base + sets, : nu * nv]
        base += sets
        prof_rows = meta[base : base + nv, :KW]
        base += nv
        prof_cols = meta[base : base + nu, :KW]
        base += nu
        entry = lax.broadcasted_iota(jnp.int32, (1, sets), 1)
        cells = []
        for bi in range(nb):
            for bj in range(nb):
                chosen = jnp.broadcast_to(meta[base + bi : base + bi + 1, bj : bj + 1], (1, sets))
                cells.append((chosen.astype(jnp.int32) == entry).astype(F32))
        coefs = jnp.dot(
            jnp.concatenate(cells, axis=0), table, precision=HIGHEST, preferred_element_type=F32
        )
        width = nu * 96
        padded[...] = jnp.zeros_like(padded)
        padded[0:nv, 0:KW] = prof_rows
        profile = padded[0:nv, :]
        spread = jnp.concatenate(
            [pltpu.roll(profile, p * 96 + 1, 1) for p in range(nu)], axis=0
        )
        base = jnp.dot(coefs, spread, precision=HIGHEST, preferred_element_type=F32)
        for cell in range(nb * nb):
            row = jnp.broadcast_to(base[cell : cell + 1, :], (BLK // 2, width))
            kernels[cell] = pltpu.roll(row, 0, 1, stride=1, stride_axis=0).astype(BF16)
        padded[...] = jnp.zeros_like(padded)
        padded[0:nu, 0:KW] = prof_cols
        for p in range(nu):
            row = jnp.broadcast_to(padded[p : p + 1, : 2 * BLK], (BLK, 2 * BLK))
            turned = pltpu.roll(row, 1, 1, stride=1, stride_axis=0).T
            band[:, p * BLK : (p + 1) * BLK] = turned.astype(BF16)


def edge_kernel(
    nb, ny,
    left, right, early_up, early_down, tip_hi, tip_lo, row_hi, row_lo, edge_hi, edge_lo, out_hi, out_lo,
    own, across, side_up, side_down,
    end_hi, end_lo,
):
    side = nb * BLK
    kept = side - 2 * ROW0
    half = side // 2
    j = lax.axis_index("skyy")

    @pl.when(lax.axis_index("segment") == 0)
    def _():
        lanes = lax.broadcasted_iota(jnp.int32, (8, BLK), 1)
        weights = taps([left[side : side + 1, :], right[side : side + 1, :]])
        shifts = [part[side + 1 : side + 2, :].astype(jnp.int32) for part in (left, right)]
        parts = [split(left[:side, :]), split(right[:side, :])]
        for n in range(2):
            source = []
            for part, tip in zip(parts[n], (tip_hi, tip_lo)):
                inner = tip[:, n * BLK : (n + 1) * BLK]
                source.append(jnp.concatenate([part, inner] if n == 0 else [inner, part], axis=1))
            mat = tuple(edge[n * 2 * BLK : (n + 1) * 2 * BLK, :] for edge in (edge_hi, edge_lo))
            hi, lo = split(packed3(source, mat))
            end_hi[:, n * BLK : (n + 1) * BLK] = hi
            end_lo[:, n * BLK : (n + 1) * BLK] = lo
        low_ok = jnp.logical_and(lanes >= BLK - HALF, j > 0)
        high_ok = jnp.logical_and(lanes < HALF, j < ny - 1)
        low = split(banded(jnp.where(low_ok, weights[0], 0.0), shifts[0], BLK, BLK))
        high = split(banded(jnp.where(high_ok, weights[1], 0.0), shifts[1], BLK, -BLK))
        mat = [jnp.concatenate(pair, axis=0) for pair in zip(low, high)]
        hi, lo = split(packed3((tip_hi[...], tip_lo[...]), mat))
        end_hi[:, 2 * BLK :] = hi
        end_lo[:, 2 * BLK :] = lo
        outer = []
        for n, b in ((0, 0), (1, nb - 1)):
            rows = slice(b * BLK, (b + 1) * BLK)
            mat = tuple(part[n * BLK : (n + 1) * BLK, :] for part in (out_hi, out_lo))
            got = dot3(mat, (end_hi[rows, :], end_lo[rows, :]), MATMUL)
            outer.append(got[:, 2 * BLK :])
            out = side_up if n == 0 else side_down
            out[:BLK, :BLK] = got[:, :BLK].astype(BF16)
            out[:BLK, BLK : side - BLK] = (early_up if n == 0 else early_down)[...]
            out[:BLK, side - BLK :] = got[:, BLK : 2 * BLK].astype(BF16)
            turned = got[:, 2 * BLK :].T
            for k, row in enumerate((0, 8, BLK - 16, BLK - 8)):
                out[BLK:, k * BLK : (k + 1) * BLK] = turned[row : row + 8].astype(BF16)
        across[kept : kept + 16, :] = side_down[:16, :half]
        across[kept + 16 : kept + 32, :] = side_up[BLK - 16 : BLK, :half]
        across[kept + 32 : kept + 48, :] = side_down[:16, half:]
        across[kept + 48 : kept + 64, :] = side_up[BLK - 16 : BLK, half:]
        strips = []
        for b in range(nb):
            first, depth = (b, BLK) if b in (0, nb - 1) else (b - 1, 3 * BLK)
            rows, cols = slice(b * BLK, (b + 1) * BLK), slice(first * BLK, first * BLK + depth)
            mat = (row_hi[rows, cols], row_lo[rows, cols])
            got = dot3(mat, (end_hi[cols, : 2 * BLK], end_lo[cols, : 2 * BLK]), MATMUL)
            own[rows, :] = got.astype(BF16)
            low = max(b * BLK, ROW0)
            high = min((b + 1) * BLK, side - ROW0)
            across[low - ROW0 : high - ROW0, :] = got[low - b * BLK : high - b * BLK, :].astype(BF16)
            strips.append(packed3(mat, (end_hi[cols, 2 * BLK :], end_lo[cols, 2 * BLK :])))
        strip = jnp.concatenate(strips, axis=0)
        strip = jnp.concatenate(
            [
                strip[: ROW0 - 16], outer[0][BLK - 16 :], strip[ROW0 : side - ROW0],
                outer[1][:16], strip[side - ROW0 + 16 :],
            ],
            axis=0,
        ).T
        for n in range(2):
            base = kept + 64 + 32 * n
            cols = slice(n * half, (n + 1) * half)
            across[base : base + 16, :] = strip[:16, cols].astype(BF16)
            across[base + 16 : base + 32, :] = strip[BLK - 16 :, cols].astype(BF16)


def relay_kernel(up_in, down_in, end_in, up, down):
    @pl.when(lax.axis_index("segment") == 0)
    def _():
        up[...] = up_in[:BLK, :]
        down[...] = down_in[:BLK, :]


def finish_kernel(
    nb, nu,
    frame, own_mid, own_end, side_up, side_down, mid, end, kernels, band, got_up, got_down,
    out, result, wide, full, passed, sems,
):
    side = nb * BLK
    half = side // 2
    warper = lax.axis_index("segment") == 0
    last = side - BLK
    sends = []
    for b in range(nb):
        rows = pl.ds(b * BLK, BLK)
        sends.append(pltpu.make_async_copy(result.at[rows, :], out.at[rows, :], sems.at[b]))

    @pl.when(warper)
    def _():
        for b in range(nb):
            rows = slice(b * BLK, (b + 1) * BLK)
            pieces = ((0, own_end[rows, :BLK]), (BLK, own_mid[rows, :]), (last, own_end[rows, BLK:]))
            for lane, piece in pieces:
                cols = slice(lane, lane + piece.shape[1])
                total = piece.astype(F32)
                if b == 0:
                    total = (total + got_up[:BLK, cols].astype(F32)).astype(BF16).astype(F32)
                if b == nb - 1:
                    total = (total + got_down[:BLK, cols].astype(F32)).astype(BF16).astype(F32)
                result[rows, cols] = total
            sends[b].start()

    @pl.when(jnp.logical_not(warper))
    def _():
        kept = side - 2 * ROW0
        both = BLK - ROW0
        stop = 16 + side

        def fill(at, width, own, above, below):
            cols = slice(at, at + width)
            own = own.astype(F32)
            above, below = above.astype(F32), below.astype(F32)
            top = jnp.concatenate([above[:ROW0], own[:both] + above[ROW0:]], axis=0)
            bottom = jnp.concatenate([own[kept - both :] + below[:both], below[both:]], axis=0)
            wide[16 : 16 + BLK, cols] = top.astype(BF16)
            wide[16 + BLK : 16 + last, cols] = own[both : kept - both].astype(BF16)
            wide[16 + last : stop, cols] = bottom.astype(BF16)

        fill(BLK, side - 2 * BLK, mid[:kept, :], side_up[:BLK, BLK:last], side_down[:BLK, BLK:last])
        fill(0, BLK, end[:kept, :BLK], side_up[:BLK, :BLK], side_down[:BLK, :BLK])
        fill(last, BLK, end[:kept, BLK:], side_up[:BLK, last:], side_down[:BLK, last:])
        wide[:16, :half] = end[kept + 16 : kept + 32, :]
        wide[:16, half:side] = end[kept + 48 : kept + 64, :]
        wide[stop:, :half] = end[kept : kept + 16, :]
        wide[stop:, half:side] = end[kept + 32 : kept + 48, :]
        k = lax.broadcasted_iota(jnp.int32, (32, BLK), 0)
        lanes = lax.broadcasted_iota(jnp.int32, (32, BLK), 1)
        pick = (lanes == jnp.where(k < 16, k, k + BLK - 32)).astype(BF16)

        def turned(rows):
            return lax.dot_general(
                rows, pick, (LEFT_T, ((), ())), preferred_element_type=F32
            ).astype(BF16)

        base = kept + 64
        own = jnp.concatenate(
            [turned(end[base : base + 32, :]), turned(end[base + 32 : base + 64, :])], axis=0
        ).astype(F32)
        above, below = (
            turned(
                jnp.concatenate(
                    [part[BLK:, k * BLK : (k + 1) * BLK].astype(F32) for k in range(4)], axis=0
                ).astype(BF16)
            )
            for part in (side_up, side_down)
        )
        fill(side, BLK, own[ROW0 : side - ROW0], above, below)
        wide[:16, side:] = own[ROW0 - 16 : ROW0].astype(BF16)
        wide[stop:, side:] = own[side - ROW0 : side - ROW0 + 16].astype(BF16)
        cut = side + BLK - 16
        full[...] = jnp.concatenate([wide[:, cut:], wide[:, :cut]], axis=1)
        for bj in range(nb):
            got = jnp.dot(
                full[:, bj * BLK : (bj + 2) * BLK], band[...], preferred_element_type=F32
            ).astype(BF16)
            for p in range(nu):
                passed[p, :, bj * BLK : (bj + 1) * BLK] = got[:, p * BLK : (p + 1) * BLK]
        for bi in range(nb):
            for bj in range(nb):
                cols = slice(bj * BLK, (bj + 1) * BLK)
                window = jnp.concatenate(
                    [
                        jnp.concatenate(
                            [passed[p, row : row + 96, cols] for row in (bi * BLK, bi * BLK + BLK // 2)],
                            axis=1,
                        )
                        for p in range(nu)
                    ],
                    axis=0,
                )
                total = jnp.dot(kernels[bi * nb + bj], window, preferred_element_type=F32)
                for n in range(2):
                    rows = slice(bi * BLK + n * BLK // 2, bi * BLK + (n + 1) * BLK // 2)
                    result[rows, cols] = frame[rows, cols] - total[:, n * BLK : (n + 1) * BLK]
            sends[bi].start()

    for send in sends:
        send.wait()


def call(kernel, name, out_shape, in_specs, scratch=(), flops=0, limit=40 << 20):
    many = isinstance(out_shape, tuple)
    return pl.pallas_call(
        kernel,
        out_shape=out_shape,
        in_specs=in_specs,
        out_specs=(VM,) * len(out_shape) if many else VM,
        scratch_shapes=list(scratch),
        compiler_params=pltpu.CompilerParams(vmem_limit_bytes=limit),
        cost_estimate=pl.CostEstimate(flops=flops, bytes_accessed=flops // 500, transcendentals=0),
        name=name,
    )


def local(
    frames, row_shift, row_frac, col_shift, col_frac,
    profile_cols, profile_rows, coef_table, weight_ids,
):
    frame = frames[0]
    side = frame.shape[0]
    nb = side // BLK
    nu, nv = profile_cols.shape[0], profile_rows.shape[0]
    nx, ny = lax.axis_size("skyx"), lax.axis_size("skyy")
    sets = coef_table.shape[0]
    row_frac = row_frac.reshape(nb, BLK)
    col_frac = col_frac.reshape(nb, BLK)

    width = nu * 96
    kept = side - 2 * ROW0
    inner = side - 2 * BLK
    cells = nb * nb
    shape = jax.ShapeDtypeStruct
    slab = shape((side + 8, BLK), F32)
    total = 4 * nb + sets + nv + nu + nb
    total += -total % 8
    meta_shape = pltpu.VMEM((total, BLK), F32)
    meta, token, row_meta, to_right, to_left = pl.pallas_call(
        functools.partial(gather_kernel, nb),
        out_shape=(
            shape((total, BLK), F32), shape((SPARE, BLK), F32), shape((2 * nb, BLK), F32), slab, slab,
        ),
        in_specs=[ANY] * 9,
        out_specs=(ANY,) * 5,
        scratch_shapes=[
            meta_shape, pltpu.VMEM((2, side + 8, BLK), F32),
            pltpu.VMEM(coef_table.shape, F32), pltpu.VMEM(profile_rows.shape, BF16),
            pltpu.VMEM(profile_cols.shape, BF16), pltpu.VMEM(weight_ids.shape, jnp.int32),
            pltpu.SMEM((nb,), jnp.int32), pltpu.SMEM((nb,), jnp.int32),
            pltpu.SemaphoreType.DMA((8,)), pltpu.SemaphoreType.DMA((6,)),
        ],
        compiler_params=pltpu.CompilerParams(vmem_limit_bytes=FULL),
        name="gather",
    )(frame, row_frac, col_frac, row_shift, col_shift, coef_table, profile_rows, profile_cols, weight_ids)
    meta_up = moved(row_meta, (-1, 1, 0), (1,))
    meta_down = moved(row_meta, (-1, -1, 0), (1,))
    left = moved(to_right, (0, 0, 1), (0,))
    right = moved(to_left, (0, 0, -1), (0,))
    mark = call(
        marker_kernel, "marker", shape((8, BLK), F32), [ANY], flops=1 << 31,
    )(token)
    own_mid, mid, mid_hi, mid_lo, row_hi, row_lo = call(
        functools.partial(center_kernel, nb), "center",
        (shape((side, inner), BF16), shape((kept, inner), BF16))
        + (shape((side, inner), BF16),) * 2
        + (shape((side, side), BF16),) * 2,
        [VM, VM, ANY],
        [pltpu.VMEM((side, side), BF16), pltpu.VMEM((side, side), BF16)],
        flops=1 << 33,
    )(frame, meta, mark)
    early_up, early_down, *parts = call(
        functools.partial(outer_kernel, nb, nx), "outer",
        (shape((BLK, inner), BF16),) * 2
        + (shape((side, 2 * BLK), BF16),) * 2
        + (shape((4 * BLK, BLK), BF16),) * 2
        + (shape((2 * BLK, BLK), BF16),) * 2,
        [VM] * 6 + [ANY],
        flops=1 << 33,
    )(frame, meta, meta_up, meta_down, mid_hi, mid_lo, own_mid)
    mid = moved(mid, (1, 0, 0), (0,))
    tip_hi, tip_lo, edge_hi, edge_lo, out_hi, out_lo = parts
    own_end, end, to_up, to_down = call(
        functools.partial(edge_kernel, nb, ny), "edges",
        (shape((side, 2 * BLK), BF16), shape((kept + 128, side // 2), BF16))
        + (shape((BLK + 8, side), BF16),) * 2,
        [VM] * 12,
        [pltpu.VMEM((side, 3 * BLK), BF16)] * 2,
        flops=1 << 33,
    )(
        left, right, early_up, early_down, tip_hi, tip_lo, row_hi, row_lo, edge_hi, edge_lo,
        out_hi, out_lo,
    )
    end = moved(end, (1, 0, 0), (0,))
    side_down = moved(to_up, (1, -1, 0), (0,))
    side_up = moved(to_down, (1, 1, 0), (0,))
    to_up, to_down = call(
        relay_kernel, "relay", (shape((BLK, side), BF16),) * 2, [VM] * 3
    )(to_up, to_down, own_end)
    got_down = moved(to_up, (0, -1, 0), (0,))
    got_up = moved(to_down, (0, 1, 0), (0,))
    kernels, band = call(
        functools.partial(matrices_kernel, nb, nu, nv, sets), "matrices",
        (shape((cells, BLK // 2, width), BF16), shape((2 * BLK, nu * BLK), BF16)),
        [VM, ANY],
        [pltpu.VMEM((8, width), F32)],
        flops=0,
    )(meta, own_end)
    result = pl.pallas_call(
        functools.partial(finish_kernel, nb, nu),
        out_shape=shape((side, side), F32),
        in_specs=[VM] * 11,
        out_specs=ANY,
        scratch_shapes=[
            pltpu.VMEM((side, side), F32), pltpu.VMEM((side + 32, side + BLK), BF16),
            pltpu.VMEM((side + 32, side + BLK), BF16), pltpu.VMEM((nu, side + 32, side), BF16),
            pltpu.SemaphoreType.DMA((nb,)),
        ],
        compiler_params=pltpu.CompilerParams(vmem_limit_bytes=40 << 20),
        name="finish",
    )(frame, own_mid, own_end, side_up, side_down, mid, end, kernels, band, got_up, got_down)
    return result[None]


def solution(mesh):
    placed = (
        P("segment", "skyx", "skyy"), P("skyx"), P("skyx"), P("skyy"), P("skyy"),
        P(), P(), P(), P("skyx", "skyy"),
    )
    return jax.shard_map(
        local, mesh=mesh, in_specs=placed, out_specs=P("segment", "skyx", "skyy"), check_vma=False
    )
```

```python
import functools
import math

import jax
import jax.numpy as jnp
from jax import lax
from jax.experimental import pallas as pl
from jax.experimental.pallas import tpu as pltpu
from jax.sharding import PartitionSpec as P

BLK = 128
KW = 31
HALF = 15
ROW0 = 56
F32 = jnp.float32
BF16 = jnp.bfloat16
HIGHEST = lax.Precision.HIGHEST
VM = pl.BlockSpec(memory_space=pltpu.VMEM)
ANY = pl.BlockSpec(memory_space=pl.ANY)
FULL = 64 << 20
SPARE = 1 << 15


def moved(block, step, sources):
    axes = ("segment", "skyx", "skyy")
    counts = [lax.axis_size(axis) for axis in axes]
    route = []
    for s in range(counts[0]):
        for i in range(counts[1]):
            for j in range(counts[2]):
                to = (s + step[0], i + step[1], j + step[2])
                if s in sources and all(0 <= to[k] < counts[k] for k in range(3)):
                    flat = [(a * counts[1] + b) * counts[2] + c for a, b, c in ((s, i, j), to)]
                    route.append(tuple(flat))
    return lax.ppermute(block, axes, route)


def sinc(values):
    angle = math.pi * values
    zero = values == 0.0
    return jnp.where(zero, 1.0, jnp.sin(angle) / jnp.where(zero, 1.0, angle))


def taps(fracs):
    count = len(fracs)
    spread = jnp.concatenate([jnp.broadcast_to(frac, (8, BLK)) for frac in fracs], axis=0)
    lag = (lax.broadcasted_iota(jnp.int32, (8 * count, BLK), 0) & 7) - 2
    values = lag.astype(F32) - spread
    weight = jnp.where(jnp.abs(values) < 3.0, sinc(values) * sinc(values / 3.0), 0.0)
    return [weight[8 * n : 8 * n + 8] for n in range(count)]


def split(values):
    high = values.astype(BF16)
    return high, (values - high.astype(F32)).astype(BF16)


def banded(weight, shift, depth, offset):
    lag = (
        lax.broadcasted_iota(jnp.int32, (depth, BLK), 0)
        - lax.broadcasted_iota(jnp.int32, (depth, BLK), 1)
        + (offset - shift)
    )
    total = jnp.zeros((depth, BLK), F32)
    for tap in range(6):
        total = jnp.where(lag == tap - 2, weight[tap : tap + 1], total)
    return total


def dot3(left, right, dims):
    lh, ll = left
    rh, rl = right
    dot = functools.partial(
        lax.dot_general, dimension_numbers=(dims, ((), ())), preferred_element_type=F32
    )
    return dot(lh, rh) + dot(lh, rl) + dot(ll, rh)


MATMUL = ((1,), (0,))
LEFT_T = ((0,), (0,))


def packed3(left, right):
    lh, ll = left
    rh, rl = right
    width = rh.shape[1]
    dot = functools.partial(jnp.dot, preferred_element_type=F32)
    both = dot(lh, jnp.concatenate([rh, rl], axis=1))
    return both[:, :width] + both[:, width:] + dot(ll, rh)


def gather_kernel(
    nb, frame, row_frac, col_frac, row_shift, col_shift, table, prof_rows, prof_cols, ids,
    meta_out, token, row_meta, to_right, to_left,
    meta, marks, table_v, rows_v, cols_v, ids_v, row_s, col_s, sems, done,
):
    side = nb * BLK
    warper = lax.axis_index("segment") == 0
    copies = [
        pltpu.make_async_copy(src, dst, sems.at[n])
        for n, (src, dst) in enumerate((
            (row_frac, meta.at[0:nb, :]),
            (col_frac, meta.at[2 * nb : 3 * nb, :]),
            (row_shift, row_s),
            (col_shift, col_s),
            (table, table_v),
            (prof_rows, rows_v),
            (prof_cols, cols_v),
            (ids, ids_v),
        ))
    ]
    slabs = [
        pltpu.make_async_copy(frame.at[:, side - BLK :], marks.at[0, :side, :], done.at[0]),
        pltpu.make_async_copy(frame.at[:, :BLK], marks.at[1, :side, :], done.at[1]),
    ]
    sends = [
        pltpu.make_async_copy(marks.at[0], to_right, done.at[2]),
        pltpu.make_async_copy(marks.at[1], to_left, done.at[3]),
    ]
    summary = pltpu.make_async_copy(meta, meta_out, done.at[4])
    rows = pltpu.make_async_copy(meta.at[: 2 * nb, :], row_meta, done.at[5])

    @pl.when(warper)
    def _():
        for copy in slabs:
            copy.start()

    for copy in copies:
        copy.start()
    for copy in copies:
        copy.wait()
    for b in range(nb):
        meta[nb + b : nb + b + 1, :] = jnp.full((1, BLK), row_s[b].astype(F32))
        meta[3 * nb + b : 3 * nb + b + 1, :] = jnp.full((1, BLK), col_s[b].astype(F32))
    base = 4 * nb
    for part in (table_v, rows_v, cols_v, ids_v):
        meta[base : base + part.shape[0], : part.shape[1]] = part[...].astype(F32)
        base += part.shape[0]
    for n, b in ((0, nb - 1), (1, 0)):
        marks[n, side : side + 1, :] = meta[2 * nb + b : 2 * nb + b + 1, :]
        marks[n, side + 1 : side + 2, :] = meta[3 * nb + b : 3 * nb + b + 1, :]
    summary.start()
    rows.start()

    @pl.when(warper)
    def _():
        for copy, send in zip(slabs, sends):
            copy.wait()
            send.start()
        for send in sends:
            send.wait()

    summary.wait()
    rows.wait()


def marker_kernel(meta_in, mark):
    mark[...] = jnp.zeros_like(mark)


def center_kernel(
    nb, frame, meta, mark,
    own, across, mid_hi, mid_lo, row_hi, row_lo,
    src_hi, src_lo,
):
    side = nb * BLK

    @pl.when(lax.axis_index("segment") == 0)
    def _():
        hi, lo = split(frame[...])
        src_hi[...] = hi
        src_lo[...] = lo
        fracs = [meta[2 * nb + b : 2 * nb + b + 1, :] for b in range(nb)]
        weights = taps(fracs + [meta[b : b + 1, :] for b in range(nb)])
        col_shift = [meta[3 * nb + b : 3 * nb + b + 1, :].astype(jnp.int32) for b in range(nb)]
        row_shift = [meta[nb + b : nb + b + 1, :].astype(jnp.int32) for b in range(nb)]
        for b in range(1, nb - 1):
            mat = split(banded(weights[b], col_shift[b], 3 * BLK, -BLK))
            cols = slice((b - 1) * BLK, (b + 2) * BLK)
            hi, lo = split(packed3((src_hi[:, cols], src_lo[:, cols]), mat))
            mid_hi[:, (b - 1) * BLK : b * BLK] = hi
            mid_lo[:, (b - 1) * BLK : b * BLK] = lo
        for b in range(nb):
            first, depth = (b, BLK) if b in (0, nb - 1) else (b - 1, 3 * BLK)
            mat = split(banded(weights[nb + b], row_shift[b], depth, (first - b) * BLK).T)
            rows, cols = slice(b * BLK, (b + 1) * BLK), slice(first * BLK, first * BLK + depth)
            row_hi[rows, cols], row_lo[rows, cols] = mat
            got = dot3(mat, (mid_hi[cols, :], mid_lo[cols, :]), MATMUL)
            own[rows, :] = got.astype(BF16)
            low = max(b * BLK, ROW0)
            high = min((b + 1) * BLK, side - ROW0)
            across[low - ROW0 : high - ROW0, :] = got[low - b * BLK : high - b * BLK, :].astype(BF16)


def outer_kernel(
    nb, nx, frame, meta, meta_up, meta_down, mid_hi, mid_lo, after,
    early_up, early_down, tip_hi, tip_lo, edge_hi, edge_lo, out_hi, out_lo,
):
    side = nb * BLK
    i = lax.axis_index("skyx")

    @pl.when(lax.axis_index("segment") == 0)
    def _():
        weights = taps([
            meta_up[nb - 1 : nb, :], meta_down[0:1, :],
            meta[2 * nb : 2 * nb + 1, :], meta[3 * nb - 1 : 3 * nb, :],
        ])
        shifts = [
            row.astype(jnp.int32)
            for row in (
                meta_up[2 * nb - 1 : 2 * nb, :], meta_down[nb : nb + 1, :],
                meta[3 * nb : 3 * nb + 1, :], meta[4 * nb - 1 : 4 * nb, :],
            )
        ]
        for n, b in ((0, 0), (1, nb - 1)):
            there = (i > 0) if n == 0 else (i < nx - 1)
            weight = jnp.where(there, weights[n], 0.0)
            mat = split(banded(weight, shifts[n], BLK, BLK if n == 0 else -BLK).T)
            rows = slice(b * BLK, (b + 1) * BLK)
            early = early_up if n == 0 else early_down
            early[...] = dot3(mat, (mid_hi[rows, :], mid_lo[rows, :]), MATMUL).astype(BF16)
            out_hi[n * BLK : (n + 1) * BLK, :], out_lo[n * BLK : (n + 1) * BLK, :] = mat
            mat = split(banded(weights[2 + n], shifts[2 + n], 2 * BLK, -BLK if n == 0 else 0))
            edge_hi[n * 2 * BLK : (n + 1) * 2 * BLK, :], edge_lo[n * 2 * BLK : (n + 1) * 2 * BLK, :] = mat
            cols = slice(n * BLK, (n + 1) * BLK)
            tip_hi[:, cols], tip_lo[:, cols] = split(frame[:, b * BLK : (b + 1) * BLK])


def matrices_kernel(nb, nu, nv, sets, meta, after, kernels, band, padded):
    @pl.when(lax.axis_index("segment") != 0)
    def _():
        base = 4 * nb
        table = meta[base : base + sets, : nu * nv]
        base += sets
        prof_rows = meta[base : base + nv, :KW]
        base += nv
        prof_cols = meta[base : base + nu, :KW]
        base += nu
        entry = lax.broadcasted_iota(jnp.int32, (1, sets), 1)
        cells = []
        for bi in range(nb):
            for bj in range(nb):
                chosen = jnp.broadcast_to(meta[base + bi : base + bi + 1, bj : bj + 1], (1, sets))
                cells.append((chosen.astype(jnp.int32) == entry).astype(F32))
        coefs = jnp.dot(
            jnp.concatenate(cells, axis=0), table, precision=HIGHEST, preferred_element_type=F32
        )
        width = nu * 96
        padded[...] = jnp.zeros_like(padded)
        padded[0:nv, 0:KW] = prof_rows
        profile = padded[0:nv, :]
        spread = jnp.concatenate(
            [pltpu.roll(profile, p * 96 + 1, 1) for p in range(nu)], axis=0
        )
        base = jnp.dot(coefs, spread, precision=HIGHEST, preferred_element_type=F32)
        for cell in range(nb * nb):
            row = jnp.broadcast_to(base[cell : cell + 1, :], (BLK // 2, width))
            kernels[cell] = pltpu.roll(row, 0, 1, stride=1, stride_axis=0).astype(BF16)
        padded[...] = jnp.zeros_like(padded)
        padded[0:nu, 0:KW] = prof_cols
        for p in range(nu):
            row = jnp.broadcast_to(padded[p : p + 1, : 2 * BLK], (BLK, 2 * BLK))
            turned = pltpu.roll(row, 1, 1, stride=1, stride_axis=0).T
            band[:, p * BLK : (p + 1) * BLK] = turned.astype(BF16)


def row_blocks(nb):
    for b in range(nb):
        first, depth = (b, BLK) if b in (0, nb - 1) else (b - 1, 3 * BLK)
        yield b, slice(b * BLK, (b + 1) * BLK), slice(first * BLK, first * BLK + depth)


def left_kernel(nb, left, tip_hi, tip_lo, row_hi, row_lo, edge_hi, edge_lo, own, across, end_hi, end_lo):
    side = nb * BLK

    @pl.when(lax.axis_index("segment") == 0)
    def _():
        source = [
            jnp.concatenate([part, tip[:, :BLK]], axis=1)
            for part, tip in zip(split(left[:side, :]), (tip_hi, tip_lo))
        ]
        mat = (edge_hi[: 2 * BLK, :], edge_lo[: 2 * BLK, :])
        end_hi[...], end_lo[...] = split(packed3(source, mat))
        for b, rows, cols in row_blocks(nb):
            mat = (row_hi[rows, cols], row_lo[rows, cols])
            got = packed3(mat, (end_hi[cols, :], end_lo[cols, :]))
            own[rows, :] = got.astype(BF16)
            low, high = max(b * BLK, ROW0), min((b + 1) * BLK, side - ROW0)
            across[low - ROW0 : high - ROW0, :] = got[low - b * BLK : high - b * BLK, :].astype(BF16)


def edge_kernel(
    nb, ny,
    left, right, early_up, early_down, tip_hi, tip_lo, row_hi, row_lo, edge_hi, edge_lo, out_hi, out_lo,
    own_low, low, low_hi, low_lo,
    own, across, side_up, side_down,
    end_hi, end_lo,
):
    side = nb * BLK
    kept = side - 2 * ROW0
    half = side // 2
    j = lax.axis_index("skyy")

    @pl.when(lax.axis_index("segment") == 0)
    def _():
        lanes = lax.broadcasted_iota(jnp.int32, (8, BLK), 1)
        weights = taps([left[side : side + 1, :], right[side : side + 1, :]])
        shifts = [part[side + 1 : side + 2, :].astype(jnp.int32) for part in (left, right)]
        source = [
            jnp.concatenate([tip[:, BLK:], part], axis=1)
            for part, tip in zip(split(right[:side, :]), (tip_hi, tip_lo))
        ]
        mat = (edge_hi[2 * BLK :, :], edge_lo[2 * BLK :, :])
        hi, lo = split(packed3(source, mat))
        for end, done, part in ((end_hi, low_hi, hi), (end_lo, low_lo, lo)):
            end[:, :BLK] = done[...]
            end[:, BLK : 2 * BLK] = part
        own[:, :BLK] = own_low[...]
        across[:kept, :BLK] = low[...]
        low_ok = jnp.logical_and(lanes >= BLK - HALF, j > 0)
        high_ok = jnp.logical_and(lanes < HALF, j < ny - 1)
        lower = split(banded(jnp.where(low_ok, weights[0], 0.0), shifts[0], BLK, BLK))
        high = split(banded(jnp.where(high_ok, weights[1], 0.0), shifts[1], BLK, -BLK))
        mat = [jnp.concatenate(pair, axis=0) for pair in zip(lower, high)]
        hi, lo = split(packed3((tip_hi[...], tip_lo[...]), mat))
        end_hi[:, 2 * BLK :] = hi
        end_lo[:, 2 * BLK :] = lo
        outer = []
        for n, b in ((0, 0), (1, nb - 1)):
            rows = slice(b * BLK, (b + 1) * BLK)
            mat = tuple(part[n * BLK : (n + 1) * BLK, :] for part in (out_hi, out_lo))
            got = dot3(mat, (end_hi[rows, :], end_lo[rows, :]), MATMUL)
            outer.append(got[:, 2 * BLK :])
            out = side_up if n == 0 else side_down
            out[:BLK, :BLK] = got[:, :BLK].astype(BF16)
            out[:BLK, BLK : side - BLK] = (early_up if n == 0 else early_down)[...]
            out[:BLK, side - BLK :] = got[:, BLK : 2 * BLK].astype(BF16)
            turned = got[:, 2 * BLK :].T
            for k, row in enumerate((0, 8, BLK - 16, BLK - 8)):
                out[BLK:, k * BLK : (k + 1) * BLK] = turned[row : row + 8].astype(BF16)
        across[kept : kept + 16, :] = side_down[:16, :half]
        across[kept + 16 : kept + 32, :] = side_up[BLK - 16 : BLK, :half]
        across[kept + 32 : kept + 48, :] = side_down[:16, half:]
        across[kept + 48 : kept + 64, :] = side_up[BLK - 16 : BLK, half:]
        strips = []
        for b, rows, cols in row_blocks(nb):
            mat = (row_hi[rows, cols], row_lo[rows, cols])
            got = dot3(mat, (end_hi[cols, BLK:], end_lo[cols, BLK:]), MATMUL)
            own[rows, BLK:] = got[:, :BLK].astype(BF16)
            start, stop = max(b * BLK, ROW0), min((b + 1) * BLK, side - ROW0)
            across[start - ROW0 : stop - ROW0, BLK:] = (
                got[start - b * BLK : stop - b * BLK, :BLK].astype(BF16)
            )
            strips.append(got[:, BLK:])
        strip = jnp.concatenate(strips, axis=0)
        strip = jnp.concatenate(
            [
                strip[: ROW0 - 16], outer[0][BLK - 16 :], strip[ROW0 : side - ROW0],
                outer[1][:16], strip[side - ROW0 + 16 :],
            ],
            axis=0,
        ).T
        for n in range(2):
            base = kept + 64 + 32 * n
            cols = slice(n * half, (n + 1) * half)
            across[base : base + 16, :] = strip[:16, cols].astype(BF16)
            across[base + 16 : base + 32, :] = strip[BLK - 16 :, cols].astype(BF16)


def relay_kernel(up_in, down_in, end_in, up, down):
    @pl.when(lax.axis_index("segment") == 0)
    def _():
        up[...] = up_in[:BLK, :]
        down[...] = down_in[:BLK, :]


def finish_kernel(
    nb, nu,
    frame, own_mid, own_end, side_up, side_down, mid, end, kernels, band, got_up, got_down,
    out, result, wide, full, passed, sems,
):
    side = nb * BLK
    half = side // 2
    warper = lax.axis_index("segment") == 0
    last = side - BLK
    sends = []
    for b in range(nb):
        rows = pl.ds(b * BLK, BLK)
        sends.append(pltpu.make_async_copy(result.at[rows, :], out.at[rows, :], sems.at[b]))

    @pl.when(warper)
    def _():
        for b in range(nb):
            rows = slice(b * BLK, (b + 1) * BLK)
            pieces = ((0, own_end[rows, :BLK]), (BLK, own_mid[rows, :]), (last, own_end[rows, BLK:]))
            for lane, piece in pieces:
                cols = slice(lane, lane + piece.shape[1])
                total = piece.astype(F32)
                if b == 0:
                    total = (total + got_up[:BLK, cols].astype(F32)).astype(BF16).astype(F32)
                if b == nb - 1:
                    total = (total + got_down[:BLK, cols].astype(F32)).astype(BF16).astype(F32)
                result[rows, cols] = total
            sends[b].start()

    @pl.when(jnp.logical_not(warper))
    def _():
        kept = side - 2 * ROW0
        both = BLK - ROW0
        stop = 16 + side

        def fill(at, width, own, above, below):
            cols = slice(at, at + width)
            own = own.astype(F32)
            above, below = above.astype(F32), below.astype(F32)
            top = jnp.concatenate([above[:ROW0], own[:both] + above[ROW0:]], axis=0)
            bottom = jnp.concatenate([own[kept - both :] + below[:both], below[both:]], axis=0)
            wide[16 : 16 + BLK, cols] = top.astype(BF16)
            wide[16 + BLK : 16 + last, cols] = own[both : kept - both].astype(BF16)
            wide[16 + last : stop, cols] = bottom.astype(BF16)

        fill(BLK, side - 2 * BLK, mid[:kept, :], side_up[:BLK, BLK:last], side_down[:BLK, BLK:last])
        fill(0, BLK, end[:kept, :BLK], side_up[:BLK, :BLK], side_down[:BLK, :BLK])
        fill(last, BLK, end[:kept, BLK:], side_up[:BLK, last:], side_down[:BLK, last:])
        wide[:16, :half] = end[kept + 16 : kept + 32, :]
        wide[:16, half:side] = end[kept + 48 : kept + 64, :]
        wide[stop:, :half] = end[kept : kept + 16, :]
        wide[stop:, half:side] = end[kept + 32 : kept + 48, :]
        k = lax.broadcasted_iota(jnp.int32, (32, BLK), 0)
        lanes = lax.broadcasted_iota(jnp.int32, (32, BLK), 1)
        pick = (lanes == jnp.where(k < 16, k, k + BLK - 32)).astype(BF16)

        def turned(rows):
            return lax.dot_general(
                rows, pick, (LEFT_T, ((), ())), preferred_element_type=F32
            ).astype(BF16)

        base = kept + 64
        own = jnp.concatenate(
            [turned(end[base : base + 32, :]), turned(end[base + 32 : base + 64, :])], axis=0
        ).astype(F32)
        above, below = (
            turned(
                jnp.concatenate(
                    [part[BLK:, k * BLK : (k + 1) * BLK].astype(F32) for k in range(4)], axis=0
                ).astype(BF16)
            )
            for part in (side_up, side_down)
        )
        fill(side, BLK, own[ROW0 : side - ROW0], above, below)
        wide[:16, side:] = own[ROW0 - 16 : ROW0].astype(BF16)
        wide[stop:, side:] = own[side - ROW0 : side - ROW0 + 16].astype(BF16)
        cut = side + BLK - 16
        full[...] = jnp.concatenate([wide[:, cut:], wide[:, :cut]], axis=1)
        for bj in range(nb):
            got = jnp.dot(
                full[:, bj * BLK : (bj + 2) * BLK], band[...], preferred_element_type=F32
            ).astype(BF16)
            for p in range(nu):
                passed[p, :, bj * BLK : (bj + 1) * BLK] = got[:, p * BLK : (p + 1) * BLK]
        for bi in range(nb):
            for bj in range(nb):
                cols = slice(bj * BLK, (bj + 1) * BLK)
                window = jnp.concatenate(
                    [
                        jnp.concatenate(
                            [passed[p, row : row + 96, cols] for row in (bi * BLK, bi * BLK + BLK // 2)],
                            axis=1,
                        )
                        for p in range(nu)
                    ],
                    axis=0,
                )
                total = jnp.dot(kernels[bi * nb + bj], window, preferred_element_type=F32)
                for n in range(2):
                    rows = slice(bi * BLK + n * BLK // 2, bi * BLK + (n + 1) * BLK // 2)
                    result[rows, cols] = frame[rows, cols] - total[:, n * BLK : (n + 1) * BLK]
            sends[bi].start()

    for send in sends:
        send.wait()


def call(kernel, name, out_shape, in_specs, scratch=(), flops=0, limit=40 << 20):
    many = isinstance(out_shape, tuple)
    return pl.pallas_call(
        kernel,
        out_shape=out_shape,
        in_specs=in_specs,
        out_specs=(VM,) * len(out_shape) if many else VM,
        scratch_shapes=list(scratch),
        compiler_params=pltpu.CompilerParams(vmem_limit_bytes=limit),
        cost_estimate=pl.CostEstimate(flops=flops, bytes_accessed=flops // 500, transcendentals=0),
        name=name,
    )


def local(
    frames, row_shift, row_frac, col_shift, col_frac,
    profile_cols, profile_rows, coef_table, weight_ids,
):
    frame = frames[0]
    side = frame.shape[0]
    nb = side // BLK
    nu, nv = profile_cols.shape[0], profile_rows.shape[0]
    nx, ny = lax.axis_size("skyx"), lax.axis_size("skyy")
    sets = coef_table.shape[0]
    row_frac = row_frac.reshape(nb, BLK)
    col_frac = col_frac.reshape(nb, BLK)

    width = nu * 96
    kept = side - 2 * ROW0
    inner = side - 2 * BLK
    cells = nb * nb
    shape = jax.ShapeDtypeStruct
    slab = shape((side + 8, BLK), F32)
    total = 4 * nb + sets + nv + nu + nb
    total += -total % 8
    meta_shape = pltpu.VMEM((total, BLK), F32)
    meta, token, row_meta, to_right, to_left = pl.pallas_call(
        functools.partial(gather_kernel, nb),
        out_shape=(
            shape((total, BLK), F32), shape((SPARE, BLK), F32), shape((2 * nb, BLK), F32), slab, slab,
        ),
        in_specs=[ANY] * 9,
        out_specs=(ANY,) * 5,
        scratch_shapes=[
            meta_shape, pltpu.VMEM((2, side + 8, BLK), F32),
            pltpu.VMEM(coef_table.shape, F32), pltpu.VMEM(profile_rows.shape, BF16),
            pltpu.VMEM(profile_cols.shape, BF16), pltpu.VMEM(weight_ids.shape, jnp.int32),
            pltpu.SMEM((nb,), jnp.int32), pltpu.SMEM((nb,), jnp.int32),
            pltpu.SemaphoreType.DMA((8,)), pltpu.SemaphoreType.DMA((6,)),
        ],
        compiler_params=pltpu.CompilerParams(vmem_limit_bytes=FULL),
        name="gather",
    )(frame, row_frac, col_frac, row_shift, col_shift, coef_table, profile_rows, profile_cols, weight_ids)
    meta_up = moved(row_meta, (-1, 1, 0), (1,))
    meta_down = moved(row_meta, (-1, -1, 0), (1,))
    left = moved(to_right, (0, 0, 1), (0,))
    right = moved(to_left, (0, 0, -1), (0,))
    mark = call(
        marker_kernel, "marker", shape((8, BLK), F32), [ANY], flops=1 << 31,
    )(token)
    own_mid, mid, mid_hi, mid_lo, row_hi, row_lo = call(
        functools.partial(center_kernel, nb), "center",
        (shape((side, inner), BF16), shape((kept, inner), BF16))
        + (shape((side, inner), BF16),) * 2
        + (shape((side, side), BF16),) * 2,
        [VM, VM, ANY],
        [pltpu.VMEM((side, side), BF16), pltpu.VMEM((side, side), BF16)],
        flops=1 << 33,
    )(frame, meta, mark)
    early_up, early_down, *parts = call(
        functools.partial(outer_kernel, nb, nx), "outer",
        (shape((BLK, inner), BF16),) * 2
        + (shape((side, 2 * BLK), BF16),) * 2
        + (shape((4 * BLK, BLK), BF16),) * 2
        + (shape((2 * BLK, BLK), BF16),) * 2,
        [VM] * 6 + [ANY],
        flops=1 << 33,
    )(frame, meta, meta_up, meta_down, mid_hi, mid_lo, own_mid)
    mid = moved(mid, (1, 0, 0), (0,))
    tip_hi, tip_lo, edge_hi, edge_lo, out_hi, out_lo = parts
    tip_row = (tip_hi, tip_lo, row_hi, row_lo, edge_hi, edge_lo)
    lows = call(
        functools.partial(left_kernel, nb), "left",
        (shape((side, BLK), BF16), shape((kept, BLK), BF16)) + (shape((side, BLK), BF16),) * 2,
        [VM] * 7,
        flops=1 << 33,
    )(left, *tip_row)
    own_end, end, to_up, to_down = call(
        functools.partial(edge_kernel, nb, ny), "edges",
        (shape((side, 2 * BLK), BF16), shape((kept + 128, side // 2), BF16))
        + (shape((BLK + 8, side), BF16),) * 2,
        [VM] * 16,
        [pltpu.VMEM((side, 3 * BLK), BF16)] * 2,
        flops=1 << 33,
    )(left, right, early_up, early_down, *tip_row, out_hi, out_lo, *lows)
    end = moved(end, (1, 0, 0), (0,))
    side_down = moved(to_up, (1, -1, 0), (0,))
    side_up = moved(to_down, (1, 1, 0), (0,))
    to_up, to_down = call(
        relay_kernel, "relay", (shape((BLK, side), BF16),) * 2, [VM] * 3
    )(to_up, to_down, own_end)
    got_down = moved(to_up, (0, -1, 0), (0,))
    got_up = moved(to_down, (0, 1, 0), (0,))
    kernels, band = call(
        functools.partial(matrices_kernel, nb, nu, nv, sets), "matrices",
        (shape((cells, BLK // 2, width), BF16), shape((2 * BLK, nu * BLK), BF16)),
        [VM, ANY],
        [pltpu.VMEM((8, width), F32)],
        flops=0,
    )(meta, own_end)
    result = pl.pallas_call(
        functools.partial(finish_kernel, nb, nu),
        out_shape=shape((side, side), F32),
        in_specs=[VM] * 11,
        out_specs=ANY,
        scratch_shapes=[
            pltpu.VMEM((side, side), F32), pltpu.VMEM((side + 32, side + BLK), BF16),
            pltpu.VMEM((side + 32, side + BLK), BF16), pltpu.VMEM((nu, side + 32, side), BF16),
            pltpu.SemaphoreType.DMA((nb,)),
        ],
        compiler_params=pltpu.CompilerParams(vmem_limit_bytes=40 << 20),
        name="finish",
    )(frame, own_mid, own_end, side_up, side_down, mid, end, kernels, band, got_up, got_down)
    return result[None]


def solution(mesh):
    placed = (
        P("segment", "skyx", "skyy"), P("skyx"), P("skyx"), P("skyy"), P("skyy"),
        P(), P(), P(), P("skyx", "skyy"),
    )
    return jax.shard_map(
        local, mesh=mesh, in_specs=placed, out_specs=P("segment", "skyx", "skyy"), check_vma=False
    )
```

```python
import functools
import math

import jax
import jax.numpy as jnp
from jax import lax
from jax.experimental import pallas as pl
from jax.experimental.pallas import tpu as pltpu
from jax.sharding import PartitionSpec as P

BLK = 128
KW = 31
HALF = 15
ROW0 = 56
F32 = jnp.float32
BF16 = jnp.bfloat16
HIGHEST = lax.Precision.HIGHEST
VM = pl.BlockSpec(memory_space=pltpu.VMEM)
ANY = pl.BlockSpec(memory_space=pl.ANY)
FULL = 64 << 20
SPARE = 1 << 15


def moved(block, step, sources):
    axes = ("segment", "skyx", "skyy")
    counts = [lax.axis_size(axis) for axis in axes]
    route = []
    for s in range(counts[0]):
        for i in range(counts[1]):
            for j in range(counts[2]):
                to = (s + step[0], i + step[1], j + step[2])
                if s in sources and all(0 <= to[k] < counts[k] for k in range(3)):
                    flat = [(a * counts[1] + b) * counts[2] + c for a, b, c in ((s, i, j), to)]
                    route.append(tuple(flat))
    return lax.ppermute(block, axes, route)


def sinc(values):
    angle = math.pi * values
    zero = values == 0.0
    return jnp.where(zero, 1.0, jnp.sin(angle) / jnp.where(zero, 1.0, angle))


def taps(fracs):
    count = len(fracs)
    spread = jnp.concatenate([jnp.broadcast_to(frac, (8, BLK)) for frac in fracs], axis=0)
    lag = (lax.broadcasted_iota(jnp.int32, (8 * count, BLK), 0) & 7) - 2
    values = lag.astype(F32) - spread
    weight = jnp.where(jnp.abs(values) < 3.0, sinc(values) * sinc(values / 3.0), 0.0)
    return [weight[8 * n : 8 * n + 8] for n in range(count)]


def split(values):
    high = values.astype(BF16)
    return high, (values - high.astype(F32)).astype(BF16)


def banded(weight, shift, depth, offset):
    lag = (
        lax.broadcasted_iota(jnp.int32, (depth, BLK), 0)
        - lax.broadcasted_iota(jnp.int32, (depth, BLK), 1)
        + (offset - shift)
    )
    total = jnp.zeros((depth, BLK), F32)
    for tap in range(6):
        total = jnp.where(lag == tap - 2, weight[tap : tap + 1], total)
    return total


def dot3(left, right, dims):
    lh, ll = left
    rh, rl = right
    dot = functools.partial(
        lax.dot_general, dimension_numbers=(dims, ((), ())), preferred_element_type=F32
    )
    return dot(lh, rh) + dot(lh, rl) + dot(ll, rh)


MATMUL = ((1,), (0,))
LEFT_T = ((0,), (0,))


def packed3(left, right):
    lh, ll = left
    rh, rl = right
    width = rh.shape[1]
    dot = functools.partial(jnp.dot, preferred_element_type=F32)
    both = dot(lh, jnp.concatenate([rh, rl], axis=1))
    return both[:, :width] + both[:, width:] + dot(ll, rh)


def gather_kernel(
    nb, frame, row_frac, col_frac, row_shift, col_shift, table, prof_rows, prof_cols, ids,
    meta_out, token, row_meta, to_right, to_left,
    meta, marks, table_v, rows_v, cols_v, ids_v, row_s, col_s, sems, done,
):
    side = nb * BLK
    warper = lax.axis_index("segment") == 0
    copies = [
        pltpu.make_async_copy(src, dst, sems.at[n])
        for n, (src, dst) in enumerate((
            (row_frac, meta.at[0:nb, :]),
            (col_frac, meta.at[2 * nb : 3 * nb, :]),
            (row_shift, row_s),
            (col_shift, col_s),
            (table, table_v),
            (prof_rows, rows_v),
            (prof_cols, cols_v),
            (ids, ids_v),
        ))
    ]
    slabs = [
        pltpu.make_async_copy(frame.at[:, side - BLK :], marks.at[0, :side, :], done.at[0]),
        pltpu.make_async_copy(frame.at[:, :BLK], marks.at[1, :side, :], done.at[1]),
    ]
    sends = [
        pltpu.make_async_copy(marks.at[0], to_right, done.at[2]),
        pltpu.make_async_copy(marks.at[1], to_left, done.at[3]),
    ]
    summary = pltpu.make_async_copy(meta, meta_out, done.at[4])
    rows = pltpu.make_async_copy(meta.at[: 2 * nb, :], row_meta, done.at[5])

    @pl.when(warper)
    def _():
        for copy in slabs:
            copy.start()

    for copy in copies:
        copy.start()
    for copy in copies:
        copy.wait()
    for b in range(nb):
        meta[nb + b : nb + b + 1, :] = jnp.full((1, BLK), row_s[b].astype(F32))
        meta[3 * nb + b : 3 * nb + b + 1, :] = jnp.full((1, BLK), col_s[b].astype(F32))
    base = 4 * nb
    for part in (table_v, rows_v, cols_v, ids_v):
        meta[base : base + part.shape[0], : part.shape[1]] = part[...].astype(F32)
        base += part.shape[0]
    for n, b in ((0, nb - 1), (1, 0)):
        marks[n, side : side + 1, :] = meta[2 * nb + b : 2 * nb + b + 1, :]
        marks[n, side + 1 : side + 2, :] = meta[3 * nb + b : 3 * nb + b + 1, :]
    summary.start()
    rows.start()

    @pl.when(warper)
    def _():
        for copy, send in zip(slabs, sends):
            copy.wait()
            send.start()
        for send in sends:
            send.wait()

    summary.wait()
    rows.wait()


def marker_kernel(meta_in, mark):
    mark[...] = jnp.zeros_like(mark)


def center_kernel(
    nb, frame, meta, mark,
    own, across, mid_hi, mid_lo, row_hi, row_lo,
    src_hi, src_lo,
):
    side = nb * BLK

    @pl.when(lax.axis_index("segment") == 0)
    def _():
        hi, lo = split(frame[...])
        src_hi[...] = hi
        src_lo[...] = lo
        fracs = [meta[2 * nb + b : 2 * nb + b + 1, :] for b in range(nb)]
        weights = taps(fracs + [meta[b : b + 1, :] for b in range(nb)])
        col_shift = [meta[3 * nb + b : 3 * nb + b + 1, :].astype(jnp.int32) for b in range(nb)]
        row_shift = [meta[nb + b : nb + b + 1, :].astype(jnp.int32) for b in range(nb)]
        for b in range(1, nb - 1):
            mat = split(banded(weights[b], col_shift[b], 3 * BLK, -BLK))
            cols = slice((b - 1) * BLK, (b + 2) * BLK)
            hi, lo = split(packed3((src_hi[:, cols], src_lo[:, cols]), mat))
            mid_hi[:, (b - 1) * BLK : b * BLK] = hi
            mid_lo[:, (b - 1) * BLK : b * BLK] = lo
        for b in range(nb):
            first, depth = (b, BLK) if b in (0, nb - 1) else (b - 1, 3 * BLK)
            mat = split(banded(weights[nb + b], row_shift[b], depth, (first - b) * BLK).T)
            rows, cols = slice(b * BLK, (b + 1) * BLK), slice(first * BLK, first * BLK + depth)
            row_hi[rows, cols], row_lo[rows, cols] = mat
            got = dot3(mat, (mid_hi[cols, :], mid_lo[cols, :]), MATMUL)
            own[rows, :] = got.astype(BF16)
            low = max(b * BLK, ROW0)
            high = min((b + 1) * BLK, side - ROW0)
            across[low - ROW0 : high - ROW0, :] = got[low - b * BLK : high - b * BLK, :].astype(BF16)


def outer_kernel(
    nb, nx, frame, meta, meta_up, meta_down, mid_hi, mid_lo, after,
    early_up, early_down, tip_hi, tip_lo, edge_hi, edge_lo, out_hi, out_lo,
):
    side = nb * BLK
    i = lax.axis_index("skyx")

    @pl.when(lax.axis_index("segment") == 0)
    def _():
        weights = taps([
            meta_up[nb - 1 : nb, :], meta_down[0:1, :],
            meta[2 * nb : 2 * nb + 1, :], meta[3 * nb - 1 : 3 * nb, :],
        ])
        shifts = [
            row.astype(jnp.int32)
            for row in (
                meta_up[2 * nb - 1 : 2 * nb, :], meta_down[nb : nb + 1, :],
                meta[3 * nb : 3 * nb + 1, :], meta[4 * nb - 1 : 4 * nb, :],
            )
        ]
        for n, b in ((0, 0), (1, nb - 1)):
            there = (i > 0) if n == 0 else (i < nx - 1)
            weight = jnp.where(there, weights[n], 0.0)
            mat = split(banded(weight, shifts[n], BLK, BLK if n == 0 else -BLK).T)
            rows = slice(b * BLK, (b + 1) * BLK)
            early = early_up if n == 0 else early_down
            early[...] = dot3(mat, (mid_hi[rows, :], mid_lo[rows, :]), MATMUL).astype(BF16)
            out_hi[n * BLK : (n + 1) * BLK, :], out_lo[n * BLK : (n + 1) * BLK, :] = mat
            mat = split(banded(weights[2 + n], shifts[2 + n], 2 * BLK, -BLK if n == 0 else 0))
            edge_hi[n * 2 * BLK : (n + 1) * 2 * BLK, :], edge_lo[n * 2 * BLK : (n + 1) * 2 * BLK, :] = mat
            cols = slice(n * BLK, (n + 1) * BLK)
            tip_hi[:, cols], tip_lo[:, cols] = split(frame[:, b * BLK : (b + 1) * BLK])


def matrices_kernel(nb, nu, nv, sets, meta, after, kernels, band, padded):
    @pl.when(lax.axis_index("segment") != 0)
    def _():
        base = 4 * nb
        table = meta[base : base + sets, : nu * nv]
        base += sets
        prof_rows = meta[base : base + nv, :KW]
        base += nv
        prof_cols = meta[base : base + nu, :KW]
        base += nu
        entry = lax.broadcasted_iota(jnp.int32, (1, sets), 1)
        cells = []
        for bi in range(nb):
            for bj in range(nb):
                chosen = jnp.broadcast_to(meta[base + bi : base + bi + 1, bj : bj + 1], (1, sets))
                cells.append((chosen.astype(jnp.int32) == entry).astype(F32))
        coefs = jnp.dot(
            jnp.concatenate(cells, axis=0), table, precision=HIGHEST, preferred_element_type=F32
        )
        width = nu * 96
        padded[...] = jnp.zeros_like(padded)
        padded[0:nv, 0:KW] = prof_rows
        profile = padded[0:nv, :]
        spread = jnp.concatenate(
            [pltpu.roll(profile, p * 96 + 1, 1) for p in range(nu)], axis=0
        )
        base = jnp.dot(coefs, spread, precision=HIGHEST, preferred_element_type=F32)
        for cell in range(nb * nb):
            row = jnp.broadcast_to(base[cell : cell + 1, :], (BLK // 2, width))
            kernels[cell] = pltpu.roll(row, 0, 1, stride=1, stride_axis=0).astype(BF16)
        padded[...] = jnp.zeros_like(padded)
        padded[0:nu, 0:KW] = prof_cols
        for p in range(nu):
            row = jnp.broadcast_to(padded[p : p + 1, : 2 * BLK], (BLK, 2 * BLK))
            turned = pltpu.roll(row, 1, 1, stride=1, stride_axis=0).T
            band[:, p * BLK : (p + 1) * BLK] = turned.astype(BF16)


def row_blocks(nb):
    for b in range(nb):
        first, depth = (b, BLK) if b in (0, nb - 1) else (b - 1, 3 * BLK)
        yield b, slice(b * BLK, (b + 1) * BLK), slice(first * BLK, first * BLK + depth)


def left_kernel(
    nb, left, tip_hi, tip_lo, row_hi, row_lo, edge_hi, edge_lo, own, across, end_hi, end_lo, halo
):
    side = nb * BLK
    j = lax.axis_index("skyy")

    @pl.when(lax.axis_index("segment") == 0)
    def _():
        lanes = lax.broadcasted_iota(jnp.int32, (8, BLK), 1)
        kept = jnp.logical_and(lanes >= BLK - HALF, j > 0)
        weight = jnp.where(kept, taps([left[side : side + 1, :]])[0], 0.0)
        mat = split(banded(weight, left[side + 1 : side + 2, :].astype(jnp.int32), BLK, BLK))
        halo[...] = packed3((tip_hi[:, :BLK], tip_lo[:, :BLK]), mat)
        source = [
            jnp.concatenate([part, tip[:, :BLK]], axis=1)
            for part, tip in zip(split(left[:side, :]), (tip_hi, tip_lo))
        ]
        mat = (edge_hi[: 2 * BLK, :], edge_lo[: 2 * BLK, :])
        end_hi[...], end_lo[...] = split(packed3(source, mat))
        for b, rows, cols in row_blocks(nb):
            mat = (row_hi[rows, cols], row_lo[rows, cols])
            got = packed3(mat, (end_hi[cols, :], end_lo[cols, :]))
            own[rows, :] = got.astype(BF16)
            low, high = max(b * BLK, ROW0), min((b + 1) * BLK, side - ROW0)
            across[low - ROW0 : high - ROW0, :] = got[low - b * BLK : high - b * BLK, :].astype(BF16)


def edge_kernel(
    nb, ny,
    left, right, early_up, early_down, tip_hi, tip_lo, row_hi, row_lo, edge_hi, edge_lo, out_hi, out_lo,
    own_low, low, low_hi, low_lo, halo,
    own, across, side_up, side_down,
    end_hi, end_lo,
):
    side = nb * BLK
    kept = side - 2 * ROW0
    half = side // 2
    j = lax.axis_index("skyy")

    @pl.when(lax.axis_index("segment") == 0)
    def _():
        lanes = lax.broadcasted_iota(jnp.int32, (8, BLK), 1)
        weight = taps([right[side : side + 1, :]])[0]
        shift = right[side + 1 : side + 2, :].astype(jnp.int32)
        source = [
            jnp.concatenate([tip[:, BLK:], part], axis=1)
            for part, tip in zip(split(right[:side, :]), (tip_hi, tip_lo))
        ]
        mat = (edge_hi[2 * BLK :, :], edge_lo[2 * BLK :, :])
        hi, lo = split(packed3(source, mat))
        for end, done, part in ((end_hi, low_hi, hi), (end_lo, low_lo, lo)):
            end[:, :BLK] = done[...]
            end[:, BLK : 2 * BLK] = part
        own[:, :BLK] = own_low[...]
        across[:kept, :BLK] = low[...]
        high_ok = jnp.logical_and(lanes < HALF, j < ny - 1)
        mat = split(banded(jnp.where(high_ok, weight, 0.0), shift, BLK, -BLK))
        hi, lo = split(packed3((tip_hi[:, BLK:], tip_lo[:, BLK:]), mat) + halo[...])
        end_hi[:, 2 * BLK :] = hi
        end_lo[:, 2 * BLK :] = lo
        outer = []
        for n, b in ((0, 0), (1, nb - 1)):
            rows = slice(b * BLK, (b + 1) * BLK)
            mat = tuple(part[n * BLK : (n + 1) * BLK, :] for part in (out_hi, out_lo))
            got = dot3(mat, (end_hi[rows, :], end_lo[rows, :]), MATMUL)
            outer.append(got[:, 2 * BLK :])
            out = side_up if n == 0 else side_down
            out[:BLK, :BLK] = got[:, :BLK].astype(BF16)
            out[:BLK, BLK : side - BLK] = (early_up if n == 0 else early_down)[...]
            out[:BLK, side - BLK :] = got[:, BLK : 2 * BLK].astype(BF16)
            turned = got[:, 2 * BLK :].T
            for k, row in enumerate((0, 8, BLK - 16, BLK - 8)):
                out[BLK:, k * BLK : (k + 1) * BLK] = turned[row : row + 8].astype(BF16)
        across[kept : kept + 16, :] = side_down[:16, :half]
        across[kept + 16 : kept + 32, :] = side_up[BLK - 16 : BLK, :half]
        across[kept + 32 : kept + 48, :] = side_down[:16, half:]
        across[kept + 48 : kept + 64, :] = side_up[BLK - 16 : BLK, half:]
        strips = []
        for b, rows, cols in row_blocks(nb):
            mat = (row_hi[rows, cols], row_lo[rows, cols])
            got = dot3(mat, (end_hi[cols, BLK:], end_lo[cols, BLK:]), MATMUL)
            own[rows, BLK:] = got[:, :BLK].astype(BF16)
            start, stop = max(b * BLK, ROW0), min((b + 1) * BLK, side - ROW0)
            across[start - ROW0 : stop - ROW0, BLK:] = (
                got[start - b * BLK : stop - b * BLK, :BLK].astype(BF16)
            )
            strips.append(got[:, BLK:])
        strip = jnp.concatenate(strips, axis=0)
        strip = jnp.concatenate(
            [
                strip[: ROW0 - 16], outer[0][BLK - 16 :], strip[ROW0 : side - ROW0],
                outer[1][:16], strip[side - ROW0 + 16 :],
            ],
            axis=0,
        ).T
        for n in range(2):
            base = kept + 64 + 32 * n
            cols = slice(n * half, (n + 1) * half)
            across[base : base + 16, :] = strip[:16, cols].astype(BF16)
            across[base + 16 : base + 32, :] = strip[BLK - 16 :, cols].astype(BF16)


def relay_kernel(up_in, down_in, end_in, up, down):
    @pl.when(lax.axis_index("segment") == 0)
    def _():
        up[...] = up_in[:BLK, :]
        down[...] = down_in[:BLK, :]


def finish_kernel(
    nb, nu,
    frame, own_mid, own_end, side_up, side_down, mid, end, kernels, band, got_up, got_down,
    out, result, wide, full, passed, sems,
):
    side = nb * BLK
    half = side // 2
    warper = lax.axis_index("segment") == 0
    last = side - BLK
    sends = []
    for b in range(nb):
        rows = pl.ds(b * BLK, BLK)
        sends.append(pltpu.make_async_copy(result.at[rows, :], out.at[rows, :], sems.at[b]))

    @pl.when(warper)
    def _():
        for b in range(nb):
            rows = slice(b * BLK, (b + 1) * BLK)
            pieces = ((0, own_end[rows, :BLK]), (BLK, own_mid[rows, :]), (last, own_end[rows, BLK:]))
            for lane, piece in pieces:
                cols = slice(lane, lane + piece.shape[1])
                total = piece.astype(F32)
                if b == 0:
                    total = (total + got_up[:BLK, cols].astype(F32)).astype(BF16).astype(F32)
                if b == nb - 1:
                    total = (total + got_down[:BLK, cols].astype(F32)).astype(BF16).astype(F32)
                result[rows, cols] = total
            sends[b].start()

    @pl.when(jnp.logical_not(warper))
    def _():
        kept = side - 2 * ROW0
        both = BLK - ROW0
        stop = 16 + side

        def fill(at, width, own, above, below):
            cols = slice(at, at + width)
            own = own.astype(F32)
            above, below = above.astype(F32), below.astype(F32)
            top = jnp.concatenate([above[:ROW0], own[:both] + above[ROW0:]], axis=0)
            bottom = jnp.concatenate([own[kept - both :] + below[:both], below[both:]], axis=0)
            wide[16 : 16 + BLK, cols] = top.astype(BF16)
            wide[16 + BLK : 16 + last, cols] = own[both : kept - both].astype(BF16)
            wide[16 + last : stop, cols] = bottom.astype(BF16)

        fill(BLK, side - 2 * BLK, mid[:kept, :], side_up[:BLK, BLK:last], side_down[:BLK, BLK:last])
        fill(0, BLK, end[:kept, :BLK], side_up[:BLK, :BLK], side_down[:BLK, :BLK])
        fill(last, BLK, end[:kept, BLK:], side_up[:BLK, last:], side_down[:BLK, last:])
        wide[:16, :half] = end[kept + 16 : kept + 32, :]
        wide[:16, half:side] = end[kept + 48 : kept + 64, :]
        wide[stop:, :half] = end[kept : kept + 16, :]
        wide[stop:, half:side] = end[kept + 32 : kept + 48, :]
        k = lax.broadcasted_iota(jnp.int32, (32, BLK), 0)
        lanes = lax.broadcasted_iota(jnp.int32, (32, BLK), 1)
        pick = (lanes == jnp.where(k < 16, k, k + BLK - 32)).astype(BF16)

        def turned(rows):
            return lax.dot_general(
                rows, pick, (LEFT_T, ((), ())), preferred_element_type=F32
            ).astype(BF16)

        base = kept + 64
        own = jnp.concatenate(
            [turned(end[base : base + 32, :]), turned(end[base + 32 : base + 64, :])], axis=0
        ).astype(F32)
        above, below = (
            turned(
                jnp.concatenate(
                    [part[BLK:, k * BLK : (k + 1) * BLK].astype(F32) for k in range(4)], axis=0
                ).astype(BF16)
            )
            for part in (side_up, side_down)
        )
        fill(side, BLK, own[ROW0 : side - ROW0], above, below)
        wide[:16, side:] = own[ROW0 - 16 : ROW0].astype(BF16)
        wide[stop:, side:] = own[side - ROW0 : side - ROW0 + 16].astype(BF16)
        cut = side + BLK - 16
        full[...] = jnp.concatenate([wide[:, cut:], wide[:, :cut]], axis=1)
        for bj in range(nb):
            got = jnp.dot(
                full[:, bj * BLK : (bj + 2) * BLK], band[...], preferred_element_type=F32
            ).astype(BF16)
            for p in range(nu):
                passed[p, :, bj * BLK : (bj + 1) * BLK] = got[:, p * BLK : (p + 1) * BLK]
        for bi in range(nb):
            for bj in range(nb):
                cols = slice(bj * BLK, (bj + 1) * BLK)
                window = jnp.concatenate(
                    [
                        jnp.concatenate(
                            [passed[p, row : row + 96, cols] for row in (bi * BLK, bi * BLK + BLK // 2)],
                            axis=1,
                        )
                        for p in range(nu)
                    ],
                    axis=0,
                )
                total = jnp.dot(kernels[bi * nb + bj], window, preferred_element_type=F32)
                for n in range(2):
                    rows = slice(bi * BLK + n * BLK // 2, bi * BLK + (n + 1) * BLK // 2)
                    result[rows, cols] = frame[rows, cols] - total[:, n * BLK : (n + 1) * BLK]
            sends[bi].start()

    for send in sends:
        send.wait()


def call(kernel, name, out_shape, in_specs, scratch=(), flops=0, limit=40 << 20):
    many = isinstance(out_shape, tuple)
    return pl.pallas_call(
        kernel,
        out_shape=out_shape,
        in_specs=in_specs,
        out_specs=(VM,) * len(out_shape) if many else VM,
        scratch_shapes=list(scratch),
        compiler_params=pltpu.CompilerParams(vmem_limit_bytes=limit),
        cost_estimate=pl.CostEstimate(flops=flops, bytes_accessed=flops // 500, transcendentals=0),
        name=name,
    )


def local(
    frames, row_shift, row_frac, col_shift, col_frac,
    profile_cols, profile_rows, coef_table, weight_ids,
):
    frame = frames[0]
    side = frame.shape[0]
    nb = side // BLK
    nu, nv = profile_cols.shape[0], profile_rows.shape[0]
    nx, ny = lax.axis_size("skyx"), lax.axis_size("skyy")
    sets = coef_table.shape[0]
    row_frac = row_frac.reshape(nb, BLK)
    col_frac = col_frac.reshape(nb, BLK)

    width = nu * 96
    kept = side - 2 * ROW0
    inner = side - 2 * BLK
    cells = nb * nb
    shape = jax.ShapeDtypeStruct
    slab = shape((side + 8, BLK), F32)
    total = 4 * nb + sets + nv + nu + nb
    total += -total % 8
    meta_shape = pltpu.VMEM((total, BLK), F32)
    meta, token, row_meta, to_right, to_left = pl.pallas_call(
        functools.partial(gather_kernel, nb),
        out_shape=(
            shape((total, BLK), F32), shape((SPARE, BLK), F32), shape((2 * nb, BLK), F32), slab, slab,
        ),
        in_specs=[ANY] * 9,
        out_specs=(ANY,) * 5,
        scratch_shapes=[
            meta_shape, pltpu.VMEM((2, side + 8, BLK), F32),
            pltpu.VMEM(coef_table.shape, F32), pltpu.VMEM(profile_rows.shape, BF16),
            pltpu.VMEM(profile_cols.shape, BF16), pltpu.VMEM(weight_ids.shape, jnp.int32),
            pltpu.SMEM((nb,), jnp.int32), pltpu.SMEM((nb,), jnp.int32),
            pltpu.SemaphoreType.DMA((8,)), pltpu.SemaphoreType.DMA((6,)),
        ],
        compiler_params=pltpu.CompilerParams(vmem_limit_bytes=FULL),
        name="gather",
    )(frame, row_frac, col_frac, row_shift, col_shift, coef_table, profile_rows, profile_cols, weight_ids)
    meta_up = moved(row_meta, (-1, 1, 0), (1,))
    meta_down = moved(row_meta, (-1, -1, 0), (1,))
    left = moved(to_right, (0, 0, 1), (0,))
    right = moved(to_left, (0, 0, -1), (0,))
    mark = call(
        marker_kernel, "marker", shape((8, BLK), F32), [ANY], flops=1 << 31,
    )(token)
    own_mid, mid, mid_hi, mid_lo, row_hi, row_lo = call(
        functools.partial(center_kernel, nb), "center",
        (shape((side, inner), BF16), shape((kept, inner), BF16))
        + (shape((side, inner), BF16),) * 2
        + (shape((side, side), BF16),) * 2,
        [VM, VM, ANY],
        [pltpu.VMEM((side, side), BF16), pltpu.VMEM((side, side), BF16)],
        flops=1 << 33,
    )(frame, meta, mark)
    early_up, early_down, *parts = call(
        functools.partial(outer_kernel, nb, nx), "outer",
        (shape((BLK, inner), BF16),) * 2
        + (shape((side, 2 * BLK), BF16),) * 2
        + (shape((4 * BLK, BLK), BF16),) * 2
        + (shape((2 * BLK, BLK), BF16),) * 2,
        [VM] * 6 + [ANY],
        flops=1 << 33,
    )(frame, meta, meta_up, meta_down, mid_hi, mid_lo, own_mid)
    mid = moved(mid, (1, 0, 0), (0,))
    tip_hi, tip_lo, edge_hi, edge_lo, out_hi, out_lo = parts
    tip_row = (tip_hi, tip_lo, row_hi, row_lo, edge_hi, edge_lo)
    lows = call(
        functools.partial(left_kernel, nb), "left",
        (shape((side, BLK), BF16), shape((kept, BLK), BF16)) + (shape((side, BLK), BF16),) * 2
        + (shape((side, BLK), F32),),
        [VM] * 7,
        flops=1 << 33,
    )(left, *tip_row)
    own_end, end, to_up, to_down = call(
        functools.partial(edge_kernel, nb, ny), "edges",
        (shape((side, 2 * BLK), BF16), shape((kept + 128, side // 2), BF16))
        + (shape((BLK + 8, side), BF16),) * 2,
        [ANY] + [VM] * 16,
        [pltpu.VMEM((side, 3 * BLK), BF16)] * 2,
        flops=1 << 33,
    )(left, right, early_up, early_down, *tip_row, out_hi, out_lo, *lows)
    end = moved(end, (1, 0, 0), (0,))
    side_down = moved(to_up, (1, -1, 0), (0,))
    side_up = moved(to_down, (1, 1, 0), (0,))
    to_up, to_down = call(
        relay_kernel, "relay", (shape((BLK, side), BF16),) * 2, [VM] * 3
    )(to_up, to_down, own_end)
    got_down = moved(to_up, (0, -1, 0), (0,))
    got_up = moved(to_down, (0, 1, 0), (0,))
    kernels, band = call(
        functools.partial(matrices_kernel, nb, nu, nv, sets), "matrices",
        (shape((cells, BLK // 2, width), BF16), shape((2 * BLK, nu * BLK), BF16)),
        [VM, ANY],
        [pltpu.VMEM((8, width), F32)],
        flops=0,
    )(meta, own_end)
    result = pl.pallas_call(
        functools.partial(finish_kernel, nb, nu),
        out_shape=shape((side, side), F32),
        in_specs=[VM] * 11,
        out_specs=ANY,
        scratch_shapes=[
            pltpu.VMEM((side, side), F32), pltpu.VMEM((side + 32, side + BLK), BF16),
            pltpu.VMEM((side + 32, side + BLK), BF16), pltpu.VMEM((nu, side + 32, side), BF16),
            pltpu.SemaphoreType.DMA((nb,)),
        ],
        compiler_params=pltpu.CompilerParams(vmem_limit_bytes=40 << 20),
        name="finish",
    )(frame, own_mid, own_end, side_up, side_down, mid, end, kernels, band, got_up, got_down)
    return result[None]


def solution(mesh):
    placed = (
        P("segment", "skyx", "skyy"), P("skyx"), P("skyx"), P("skyy"), P("skyy"),
        P(), P(), P(), P("skyx", "skyy"),
    )
    return jax.shard_map(
        local, mesh=mesh, in_specs=placed, out_specs=P("segment", "skyx", "skyy"), check_vma=False
    )
```
